32 devices in a mesh: seq: 8 (over y, x, core), dp: 4 (over z).
Axes of the slice: x: 2, y: 2, z: 4, core: 2. Of those that a mesh axis runs over, the one named last changes fastest.
Arguments:
- projected: bfloat16 [3, 4096, 4096], P(None, 'seq', 'dp'), may hold values from -6 to 6
- featurizer: bfloat16 [7, 3, 4096], P(None, None, 'dp'), may hold values from -25 to 25
- long_filter: bfloat16 [256, 128], P('dp'), may hold values from -0.5 to 0.5
- skip_gain: bfloat16 [4096], P('dp'), may hold values from -4 to 4
- out_cotangent: bfloat16 [4096, 4096], P('seq', 'dp'), may hold values from -6 to 6
Outputs:
- grad_featurizer: float32 [7, 3, 4096], P(None, None, 'dp')
- grad_filter: float32 [256, 128], P('dp')
- grad_skip: float32 [4096], P('dp')
The draws below stay inside these ranges and needn't reach their ends.
All inputs are finite; a program needn't handle non-finite values.
Results may differ from the reference program's by a relative error of at most 0.0071.
Values may be sent and summed in bfloat16 or wider, within the bound.
No kernel may reach another device: no remote copies, remote signals or barrier semaphores. Data moves between devices by JAX's collectives and lax.ppermute only.
A program may use at most 64 MiB of HBM per device.

```python
import math
import jax
import jax.numpy as jnp
from jax import lax

D = 4096
GS = 16
L = 128
FEAT = 7
G = 256
TOKENS = 4096


def draw_featurizer(key, part):
    noise_key = jax.random.fold_in(key, 11)
    position = jnp.arange(D, dtype=jnp.float32) / (D - 1)
    base = jnp.clip(jax.random.normal(noise_key, (FEAT, 3, D), jnp.float32), -4.0, 4.0)
    rising = 10.0 ** position
    scales = jnp.stack([rising, jnp.ones_like(rising), jnp.ones_like(rising)])
    return (base * scales[None] / math.sqrt(FEAT)).astype(jnp.bfloat16)


def levels(stream_key, dims, pieces, smallest, high):
    def one(dim, blocks):
        draws = jax.random.uniform(jax.random.fold_in(jax.random.fold_in(stream_key, 6), dim), (blocks,), jnp.float32, smallest / len(pieces), high / len(pieces))
        return jnp.repeat(jnp.exp(draws), dims[dim] // blocks).reshape((-1,) + (1,) * (len(dims) - dim - 1))

    gain = one(*pieces[0])
    for cut in pieces[1:]:
        gain = gain * one(*cut)
    return gain


def bell_draw(key, shape, width, limit, pieces=(), kind=jnp.bfloat16):
    entries = jax.random.normal(key, shape, jnp.float32) * width
    if len(pieces) > 0:
        entries = levels(key, shape, pieces, -0.22, 0.18) * entries
    return jnp.clip(entries, min=-limit, max=limit).astype(kind)


def setup_inputs(seed: int = 0) -> dict:
    streams_of = jax.random.split(jax.random.key(seed), 6)
    return {
        "projected": bell_draw(streams_of[0], (3, TOKENS, D), 1.0, 6.0, ((1, 8), (2, 4))),
        "featurizer": draw_featurizer(jax.random.fold_in(streams_of[5], 71), 0),
        "long_filter": bell_draw(streams_of[2], (G, L), L ** -0.5, 0.5, ((0, 4),)),
        "skip_gain": bell_draw(streams_of[3], (D,), 1.0, 4.0, ((0, 4),)),
        "out_cotangent": bell_draw(streams_of[4], (TOKENS, D), 1.0, 6.0, ((0, 8), (1, 4))),
    }


def settle(values):
    return lax.optimization_barrier(values.astype(jnp.bfloat16)).astype(jnp.float32)

def causal(signal, kernel, fft_size, keep_rows):
    spectrum = jnp.fft.rfft(signal, n=fft_size, axis=0) * jnp.fft.rfft(kernel, n=fft_size, axis=0)
    return jnp.fft.irfft(spectrum, n=fft_size, axis=0)[:keep_rows]

def reference(projected, featurizer, long_filter, skip_gain, out_cotangent):
    token_scale = 1.0 / math.sqrt(TOKENS)
    fft_size = 2 ** (TOKENS + L - 1).bit_length()
    width_block = math.gcd(D, 256)
    group_block = width_block // GS
    block_count = D // width_block
    starts = jnp.arange(block_count, dtype=jnp.int32) * width_block

    def forward(start):
        source = lax.dynamic_slice_in_dim(projected, start, width_block, 2).astype(jnp.float32)
        taps = lax.dynamic_slice_in_dim(featurizer, start, width_block, 2).astype(jnp.float32)
        filters = lax.dynamic_slice_in_dim(long_filter, start // GS, group_block, 0).astype(jnp.float32)
        skip = lax.dynamic_slice_in_dim(skip_gain, start, width_block, 0).astype(jnp.float32)
        padded = jnp.pad(source, ((0, 0), (FEAT - 1, 0), (0, 0)))
        featured = jnp.zeros_like(source)
        for tap_index in range(FEAT):
            begin = FEAT - 1 - tap_index
            featured = featured + taps[tap_index][:, None, :] * padded[:, begin:begin + TOKENS]
        rounded = settle(featured)
        queries = rounded[0]
        key_part = rounded[1]
        value_part = rounded[2]
        product = settle(key_part * value_part)
        kernel = jnp.repeat(filters.T, GS, axis=1)
        filtered = causal(product, kernel, fft_size, TOKENS)
        inner_sum = filtered + skip * product
        output = queries * inner_sum
        return (padded, queries, key_part, value_part, product, kernel, skip, inner_sum, output)

    def stats(carry, start):
        output = forward(start)[8]
        cot = lax.dynamic_slice_in_dim(out_cotangent, start, width_block, 1).astype(jnp.float32)
        return ((carry[0] + lax.optimization_barrier(jnp.sum(output * output, axis=1)), carry[1] + lax.optimization_barrier(jnp.sum(cot * output, axis=1))), None)
    initial = (jnp.zeros((TOKENS,), jnp.float32), jnp.zeros((TOKENS,), jnp.float32))
    sums, unused = lax.scan(stats, initial, starts)
    rms = jnp.sqrt(sums[0] / D + 1e-05)
    cross_mean = sums[1] / D

    def grads(start):
        padded, queries, key_part, value_part, product, kernel, skip, inner_sum, output = forward(start)
        cot = lax.dynamic_slice_in_dim(out_cotangent, start, width_block, 1).astype(jnp.float32)
        out_grad = (cot / rms[:, None] - output * (cross_mean / rms ** 3)[:, None]) * token_scale
        conv_grad = out_grad * queries
        cotangent = settle(conv_grad)
        query_grad = out_grad * inner_sum
        backward = jnp.flip(causal(jnp.flip(cotangent, 0), kernel, fft_size, TOKENS), 0)
        product_grad = backward + skip * conv_grad
        all_grad = jnp.stack([query_grad, product_grad * value_part, product_grad * key_part])
        feat_grad = jnp.stack([lax.optimization_barrier(jnp.sum(all_grad * padded[:, FEAT - 1 - tap_index:FEAT - 1 - tap_index + TOKENS], axis=1)) for tap_index in range(FEAT)])
        skip_grad = lax.optimization_barrier(jnp.sum(conv_grad * product, axis=0))
        spectra = jnp.fft.rfft(cotangent, n=fft_size, axis=0) * jnp.conj(jnp.fft.rfft(product, n=fft_size, axis=0))
        lagged = jnp.fft.irfft(spectra, n=fft_size, axis=0)[:L]
        filter_grad = lagged.reshape(L, group_block, GS).sum(axis=2).T
        return (feat_grad, filter_grad, skip_grad)
    feat_all, filter_all, skip_all = lax.map(grads, starts)
    grad_featurizer = jnp.moveaxis(feat_all, 0, 2).reshape(FEAT, 3, D)
    grad_filter = filter_all.reshape(G, L)
    grad_skip = skip_all.reshape(D)
    return (grad_featurizer, grad_filter, grad_skip)
```

```python
import functools
import math

import jax
import jax.numpy as jnp
from jax import lax
from jax.experimental import pallas as pl
from jax.experimental.pallas import tpu as pltpu
from jax.sharding import PartitionSpec as P

F32 = jnp.float32
BF16 = jnp.bfloat16
LANES = 128
HALO = 8
EDGE = 16


def matmul(a, b, contract):
    return lax.dot_general(
        a, b, ((contract[0], contract[1]), ((), ())), preferred_element_type=F32
    )


def featurize(buf, part, start, rows, taps_ref):
    taps = taps_ref.shape[1]
    total = None
    for tap in range(taps):
        weight = taps_ref[part, tap : tap + 1, :].astype(F32)
        term = weight * buf[part, start - tap : start - tap + rows, :]
        total = term if total is None else total + term
    return total.astype(BF16)


def lag_masks(block):
    row = lax.broadcasted_iota(jnp.int32, (block, block), 0)
    col = lax.broadcasted_iota(jnp.int32, (block, block), 1)
    return row, col


def front_kernel(
    x_ref, taps_ref, filt_ref, cot_ref,
    kv_ref, q0_ref, pt_ref, qt_ref, ct_ref, w_ref,
    buf,
):
    parts, rows, lanes = x_ref.shape
    groups, block = filt_ref.shape
    members = lanes // groups
    blocks = rows // block
    buf[:, :HALO, :] = jnp.zeros((parts, HALO, lanes), F32)
    for part in range(parts):
        buf[part, HALO:, :] = x_ref[part].astype(F32)
    for number in range(blocks):
        span = slice(number * block, (number + 1) * block)
        start = HALO + number * block
        q, k, v = (featurize(buf, part, start, block, taps_ref) for part in range(3))
        kv_ref[0, span, :] = k
        kv_ref[1, span, :] = v
        if number == 0:
            q0_ref[...] = q
        else:
            place = slice((number - 1) * members, number * members)
            product = (k.astype(F32) * v.astype(F32)).astype(BF16)
            pt_ref[:, place, :] = product.T.reshape(groups, members, block)
            qt_ref[:, place, :] = q.T.reshape(groups, members, block)
        place = slice(number * members, (number + 1) * members)
        ct_ref[:, place, :] = cot_ref[span, :].T.reshape(groups, members, block)
    row, col = lag_masks(block)
    for group in range(groups):
        taps = jnp.broadcast_to(filt_ref[group : group + 1, :].astype(F32), (block, block))
        circ = pltpu.roll(taps, 0, 1, stride=1, stride_axis=0)
        w_ref[group, :block, :] = jnp.where(col >= row, circ, 0.0).astype(BF16)
        w_ref[group, block:, :] = jnp.where(col < row, circ, 0.0).astype(BF16)


def skip_columns(skip_ref, block):
    lanes = skip_ref.shape[1]
    return jnp.broadcast_to(skip_ref[...].astype(F32), (block, lanes)).T


def middle_kernel(
    rim_ref, x0_ref, taps_ref, skip_ref, kv_ref, q0_ref, pt_ref, qt_ref, ct_ref, w_ref,
    kvr_ref, pta_ref, qta_ref, inner_ref, stats_ref,
    buf, acc,
):
    block = q0_ref.shape[0]
    groups, width, lanes = w_ref.shape[0], ct_ref.shape[1], q0_ref.shape[1]
    members = lanes // groups
    blocks = width // members
    tail = block + HALO
    step = pl.program_id(0)

    @pl.when(step == 0)
    def _():
        acc[...] = jnp.zeros_like(acc)

    for part in range(2):
        buf[1 + part, :tail, :] = rim_ref[part * tail : (part + 1) * tail, :].astype(F32)
        buf[1 + part, tail : tail + EDGE, :] = x0_ref[1 + part].astype(F32)
    buf[0, :HALO, :] = rim_ref[2 * tail : 2 * tail + HALO, :].astype(F32)
    buf[0, HALO : HALO + EDGE, :] = x0_ref[0].astype(F32)
    q_edge = featurize(buf, 0, HALO, EDGE, taps_ref)
    k_rim = featurize(buf, 1, HALO, block, taps_ref)
    v_rim = featurize(buf, 2, HALO, block, taps_ref)
    k_edge = featurize(buf, 1, tail, EDGE, taps_ref)
    v_edge = featurize(buf, 2, tail, EDGE, taps_ref)
    kvr_ref[0, :block, :] = k_rim
    kvr_ref[1, :block, :] = v_rim
    kvr_ref[0, block:, :] = k_edge
    kvr_ref[1, block:, :] = v_edge
    k0 = jnp.concatenate([k_edge, kv_ref[0, EDGE:, :]], axis=0)
    v0 = jnp.concatenate([v_edge, kv_ref[1, EDGE:, :]], axis=0)
    q0 = jnp.concatenate([q_edge, q0_ref[EDGE:, :]], axis=0)
    p_rim = (k_rim.astype(F32) * v_rim.astype(F32)).astype(BF16)
    p0 = (k0.astype(F32) * v0.astype(F32)).astype(BF16)
    pta_ref[:, :members, :] = p_rim.T.reshape(groups, members, block)
    pta_ref[:, members:, :] = p0.T.reshape(groups, members, block)
    qta_ref[...] = q0.T.reshape(groups, members, block)
    skip = skip_columns(skip_ref, block)
    for group in range(groups):
        every = jnp.concatenate([pta_ref[group], pt_ref[group]], axis=0)
        now = every[members:]
        filtered = matmul(
            jnp.concatenate([now, every[:width]], axis=1), w_ref[group], ((1,), (0,))
        )
        own = skip[group * members : (group + 1) * members]
        own = jnp.concatenate([own] * blocks, axis=0)
        inner = filtered + own * now.astype(F32)
        inner_ref[group] = inner
        q = jnp.concatenate([qta_ref[group], qt_ref[group]], axis=0).astype(F32)
        output = q * inner
        square = output * output
        cross = ct_ref[group].astype(F32) * output
        for number in range(blocks):
            for half in range(0, members, 8):
                at = number * members + half
                place = slice(number * 8, number * 8 + 8)
                acc[0, place, :] += square[at : at + 8]
                acc[1, place, :] += cross[at : at + 8]

    @pl.when(step == pl.num_programs(0) - 1)
    def _():
        for which in range(2):
            for number in range(blocks):
                at = which * blocks + number
                stats_ref[at : at + 1, :] = jnp.sum(
                    acc[which, number * 8 : number * 8 + 8, :], axis=0, keepdims=True
                )


def back_kernel(
    channels_all, token_scale, n_stats, *refs
):
    stats_refs = refs[:n_stats]
    (rim_ref, x_ref, skip_ref, kv_ref, kvr_ref, pt_ref, pta_ref, qt_ref, qta_ref, ct_ref,
     inner_ref, w_ref, out_ref, buf, coef, skip_acc, filt_acc, pg, qg, gn) = refs[n_stats:]
    parts, rows, lanes = x_ref.shape
    groups, width, block = ct_ref.shape
    members = lanes // groups
    blocks = rows // block
    tail = block + HALO
    taps = 7
    step = pl.program_id(0)

    @pl.when(step == 0)
    def _():
        if n_stats == 4:
            total = (stats_refs[0][...] + stats_refs[1][...]) + (stats_refs[2][...] + stats_refs[3][...])
        else:
            total = stats_refs[0][...]
        square = total[:blocks]
        cross = total[blocks : 2 * blocks] / channels_all
        rms = jnp.sqrt(square / channels_all + 1e-05)
        inv = token_scale / rms
        fall = token_scale * cross / (rms * rms * rms)
        for number in range(blocks):
            place = slice(number * members, (number + 1) * members)
            coef[0, place, :] = jnp.broadcast_to(inv[number : number + 1], (members, block))
            coef[1, place, :] = jnp.broadcast_to(fall[number : number + 1], (members, block))

    buf[0, tail - HALO : tail, :] = rim_ref[2 * tail : 2 * tail + HALO, :].astype(F32)
    for part in range(parts):
        if part:
            buf[part, :tail, :] = rim_ref[(part - 1) * tail : part * tail, :].astype(F32)
        buf[part, tail:, :] = x_ref[part].astype(F32)
    skip = skip_columns(skip_ref, block)
    row, col = lag_masks(block)
    near_side = col <= row
    for group in range(groups):
        members_at = slice(group * members, (group + 1) * members)
        every = jnp.concatenate([pta_ref[group], pt_ref[group]], axis=0)
        now = every[members:]
        q = jnp.concatenate([qta_ref[group], qt_ref[group]], axis=0).astype(F32)
        inner = inner_ref[group]
        output = q * inner
        out_grad = coef[0] * ct_ref[group].astype(F32) - coef[1] * output
        conv_grad = out_grad * q
        cot = conv_grad.astype(BF16)
        query_grad = out_grad * inner
        weighted = conv_grad * now.astype(F32)
        part_sum = weighted[:members]
        for number in range(1, blocks):
            part_sum = part_sum + weighted[number * members : (number + 1) * members]
        skip_acc[members_at, :] = part_sum
        gap = jnp.zeros((members, block), BF16)
        here = jnp.concatenate([gap, cot], axis=0)
        later = jnp.concatenate([cot, gap], axis=0)
        grad = matmul(here, w_ref[group, :block, :], ((1,), (1,))) + matmul(
            later, w_ref[group, block:, :], ((1,), (1,))
        )
        own = skip[members_at]
        pg[0, members_at, :] = grad[:members]
        for number in range(blocks):
            span = slice(number * members, (number + 1) * members)
            pg[1 + number, members_at, :] = (
                grad[(number + 1) * members : (number + 2) * members] + own * conv_grad[span]
            )
            qg[number, members_at, :] = query_grad[span]
        both = matmul(cot, jnp.concatenate([now, every[:width]], axis=1), ((0,), (0,)))
        lagged = jnp.where(near_side, both[:, :block], both[:, block:])
        skewed = lagged[:8]
        for at in range(8, block, 8):
            skewed = skewed + pltpu.roll(lagged[at : at + 8], block - at, 1)
        filt_acc[group * 8 : group * 8 + 8, :] = skewed
    flip = jnp.where(((row + col) % block) == 0, 1.0, 0.0).astype(F32)
    lags = filt_acc[pl.ds(0, groups, stride=8), :]
    for at in range(1, 8):
        lags = lags + pltpu.roll(filt_acc[pl.ds(at, groups, stride=8), :], block - at, 1)
    out_ref[3 * 8 :, :] = lax.dot_general(
        lags, flip, (((1,), (0,)), ((), ())),
        preferred_element_type=F32, precision=lax.Precision.HIGHEST,
    )
    skip_row = jnp.sum(skip_acc[...].T, axis=0, keepdims=True)
    for number in range(blocks + 1):
        span = slice(number * block, (number + 1) * block)
        back = pg[number].T
        if number == 0:
            k, v = kvr_ref[0, :block, :], kvr_ref[1, :block, :]
        elif number == 1:
            k = jnp.concatenate([kvr_ref[0, block:, :], kv_ref[0, EDGE:block, :]], axis=0)
            v = jnp.concatenate([kvr_ref[1, block:, :], kv_ref[1, EDGE:block, :]], axis=0)
        else:
            local = slice((number - 1) * block, number * block)
            k, v = kv_ref[0, local, :], kv_ref[1, local, :]
        gn[1, span, :] = back * v.astype(F32)
        gn[2, span, :] = back * k.astype(F32)
        if number:
            gn[0, span, :] = qg[number - 1].T
    chunk = 64
    for part in range(parts):
        first = 0 if part else block
        sums = [None] * taps
        for at in range(first, rows + block, chunk):
            grads = gn[part, at : at + chunk, :]
            for tap in range(taps):
                start = HALO + at - tap
                term = grads * buf[part, start : start + chunk, :]
                term = term.reshape(chunk // 8, 8, lanes).sum(axis=0)
                sums[tap] = term if sums[tap] is None else sums[tap] + term
        for tap in range(taps):
            at = part * 8 + tap
            out_ref[at : at + 1, :] = jnp.sum(sums[tap], axis=0, keepdims=True)
        out_ref[part * 8 + taps : part * 8 + 8, :] = skip_row


def finish_kernel(n_in, *refs):
    ins = refs[:n_in]
    feat_ref, filt_ref, skip_ref = refs[n_in:]
    if n_in == 4:
        total = (ins[0][...].astype(F32) + ins[1][...].astype(F32)) + (
            ins[2][...].astype(F32) + ins[3][...].astype(F32)
        )
    else:
        total = ins[0][...].astype(F32)
    taps = feat_ref.shape[1]
    for part in range(feat_ref.shape[0]):
        feat_ref[part] = total[part * 8 : part * 8 + taps]
    skip_ref[...] = total[taps : taps + 1]
    filt_ref[...] = total[24:]


def shifted(array, axis, by):
    length = lax.axis_size(axis)
    pairs = [(i, i + by) for i in range(length) if 0 <= i + by < length]
    return lax.ppermute(array, axis, pairs)


def crossed(array, axis, bit):
    length = lax.axis_size(axis)
    return lax.ppermute(array, axis, [(i, i ^ bit) for i in range(length)])


def quartet(array, axis, bit):
    return [array] + [crossed(array, axis, bit * k) for k in (1, 2, 3)]


def merged(parts):
    if len(parts) == 1:
        return parts[0]
    return (parts[0] + parts[1]) + (parts[2] + parts[3])


def body(projected, featurizer, long_filter, skip_gain, out_cotangent):
    parts, rows, channels = projected.shape
    groups, block = long_filter.shape
    taps = featurizer.shape[0]
    members = channels // groups
    chunk_groups = LANES // members
    chunks = channels // LANES
    blocks = rows // block
    width = blocks * members
    tail = block + HALO
    taps_major = jnp.transpose(featurizer, (1, 0, 2))
    skip_row = skip_gain.reshape(1, channels)
    params = pltpu.CompilerParams(vmem_limit_bytes=56 * 1024 * 1024)

    packed = jnp.concatenate(
        [projected[1, rows - tail :], projected[2, rows - tail :], projected[0, rows - HALO :]], axis=0
    )
    rim = shifted(packed, "seq", 1)

    whole = lambda *shape: pl.BlockSpec(shape, lambda i: (0,) * (len(shape) - 1) + (i,))
    grouped = lambda *shape: pl.BlockSpec((chunk_groups,) + shape, lambda i: (i,) + (0,) * len(shape))
    sds = jax.ShapeDtypeStruct

    kv, q0, pt, qt, ct, w = pl.pallas_call(
        front_kernel,
        name="front",
        grid=(chunks,),
        in_specs=[
            whole(parts, rows, LANES),
            whole(parts, taps, LANES),
            pl.BlockSpec((chunk_groups, block), lambda i: (i, 0)),
            whole(rows, LANES),
        ],
        out_specs=[
            whole(2, rows, LANES),
            whole(block, LANES),
            grouped(width - members, block),
            grouped(width - members, block),
            grouped(width, block),
            grouped(2 * block, block),
        ],
        out_shape=[
            sds((2, rows, channels), BF16),
            sds((block, channels), BF16),
            sds((groups, width - members, block), BF16),
            sds((groups, width - members, block), BF16),
            sds((groups, width, block), BF16),
            sds((groups, 2 * block, block), BF16),
        ],
        scratch_shapes=[pltpu.VMEM((parts, HALO + rows, LANES), F32)],
        compiler_params=params,
    )(projected, taps_major, long_filter, out_cotangent)

    kvr, pta, qta, inner, stats = pl.pallas_call(
        middle_kernel,
        name="middle",
        grid=(chunks,),
        in_specs=[
            whole(2 * tail + HALO, LANES),
            whole(parts, EDGE, LANES),
            whole(parts, taps, LANES),
            whole(1, LANES),
            whole(2, block, LANES),
            whole(block, LANES),
            grouped(width - members, block),
            grouped(width - members, block),
            grouped(width, block),
            grouped(2 * block, block),
        ],
        out_specs=[
            whole(2, block + EDGE, LANES),
            grouped(2 * members, block),
            grouped(members, block),
            grouped(width, block),
            pl.BlockSpec((2 * blocks, block), lambda i: (0, 0)),
        ],
        out_shape=[
            sds((2, block + EDGE, channels), BF16),
            sds((groups, 2 * members, block), BF16),
            sds((groups, members, block), BF16),
            sds((groups, width, block), F32),
            sds((2 * blocks, block), F32),
        ],
        scratch_shapes=[
            pltpu.VMEM((parts, tail + EDGE, LANES), F32),
            pltpu.VMEM((2, 8 * blocks, block), F32),
        ],
        compiler_params=params,
    )(rim, projected, taps_major, skip_row, kv, q0, pt, qt, ct, w)

    dp_size = lax.axis_size("dp")
    stat_parts = [stats]
    bit = 1
    while bit < dp_size:
        current = merged(stat_parts)
        if bit * 4 <= dp_size:
            stat_parts = quartet(current, "dp", bit)
            bit *= 4
        else:
            stat_parts = [current + crossed(current, "dp", bit)]
            bit *= 2
    token_scale = 1.0 / math.sqrt(rows * lax.axis_size("seq"))
    small = pl.BlockSpec((2 * blocks, block), lambda i: (0, 0))
    out = pl.pallas_call(
        functools.partial(back_kernel, channels * dp_size, token_scale, len(stat_parts)),
        name="back",
        grid=(chunks,),
        in_specs=[small] * len(stat_parts)
        + [
            whole(2 * tail + HALO, LANES),
            whole(parts, rows, LANES),
            whole(1, LANES),
            whole(2, rows, LANES),
            whole(2, block + EDGE, LANES),
            grouped(width - members, block),
            grouped(2 * members, block),
            grouped(width - members, block),
            grouped(members, block),
            grouped(width, block),
            grouped(width, block),
            grouped(2 * block, block),
        ],
        out_specs=whole(24 + chunk_groups, LANES),
        out_shape=sds((24 + chunk_groups, channels), F32),
        scratch_shapes=[
            pltpu.VMEM((parts, tail + rows, LANES), F32),
            pltpu.VMEM((2, width, block), F32),
            pltpu.VMEM((LANES, block), F32),
            pltpu.VMEM((chunk_groups * 8, block), F32),
            pltpu.VMEM((blocks + 1, LANES, block), F32),
            pltpu.VMEM((blocks, LANES, block), F32),
            pltpu.VMEM((parts, block + rows, LANES), F32),
        ],
        compiler_params=params,
    )(*stat_parts, rim, projected, skip_row, kv, kvr, pt, pta, qt, qta, ct, inner, w)

    seq_size = lax.axis_size("seq")
    out_parts = [out + crossed(out, "seq", 1)]
    bit = 2
    while bit < seq_size:
        current = merged(out_parts) if len(out_parts) == 1 else merged([o.astype(F32) for o in out_parts])
        current = current.astype(BF16)
        if bit * 4 <= seq_size:
            out_parts = quartet(current, "seq", bit)
            bit *= 4
        else:
            out_parts = [current.astype(F32) + crossed(current, "seq", bit).astype(F32)]
            bit *= 2

    feat, filt, skip = pl.pallas_call(
        functools.partial(finish_kernel, len(out_parts)),
        name="finish",
        grid=(chunks,),
        in_specs=[whole(24 + chunk_groups, LANES)] * len(out_parts),
        out_specs=[
            whole(parts, taps, LANES),
            pl.BlockSpec((chunk_groups, block), lambda i: (i, 0)),
            whole(1, LANES),
        ],
        out_shape=[
            sds((parts, taps, channels), F32),
            sds((groups, block), F32),
            sds((1, channels), F32),
        ],
        compiler_params=params,
    )(*out_parts)
    return (jnp.transpose(feat, (1, 0, 2)), filt, skip.reshape(channels))


def solution(mesh):
    return jax.shard_map(
        body,
        mesh=mesh,
        in_specs=(
            P(None, "seq", "dp"),
            P(None, None, "dp"),
            P("dp", None),
            P("dp"),
            P("seq", "dp"),
        ),
        out_specs=(P(None, None, "dp"), P("dp", None), P("dp")),
        check_vma=False,
    )
```

```python
import functools
import math

import jax
import jax.numpy as jnp
from jax import lax
from jax.experimental import pallas as pl
from jax.experimental.pallas import tpu as pltpu
from jax.sharding import PartitionSpec as P

F32 = jnp.float32
BF16 = jnp.bfloat16
LANES = 128
HALO = 8
EDGE = 16


def matmul(a, b, contract):
    return lax.dot_general(
        a, b, ((contract[0], contract[1]), ((), ())), preferred_element_type=F32
    )


def featurize(buf, part, start, rows, taps_ref):
    taps = taps_ref.shape[1]
    total = None
    for tap in range(taps):
        weight = taps_ref[part, tap : tap + 1, :].astype(F32)
        term = weight * buf[part, start - tap : start - tap + rows, :]
        total = term if total is None else total + term
    return total.astype(BF16)


def lag_masks(block):
    row = lax.broadcasted_iota(jnp.int32, (block, block), 0)
    col = lax.broadcasted_iota(jnp.int32, (block, block), 1)
    return row, col


def front_kernel(
    x_ref, taps_ref, filt_ref, cot_ref,
    kv_ref, q0_ref, pt_ref, qt_ref, ct_ref, w_ref,
    buf,
):
    parts, rows, channels = x_ref.shape
    block = filt_ref.shape[1]
    members = channels // filt_ref.shape[0]
    groups = LANES // members
    blocks = rows // block
    buf[:, :HALO, :] = jnp.zeros((parts, HALO, LANES), F32)

    @pl.loop(0, channels // LANES)
    def _(chunk):
        lane = pl.ds(pl.multiple_of(chunk * LANES, LANES), LANES)
        group_at = pl.ds(pl.multiple_of(chunk * groups, groups), groups)
        front_chunk(
            x_ref.at[:, :, lane], taps_ref.at[:, :, lane], filt_ref.at[group_at], cot_ref.at[:, lane],
            kv_ref.at[:, :, lane], q0_ref.at[:, lane], pt_ref.at[group_at], qt_ref.at[group_at],
            ct_ref.at[group_at], w_ref.at[group_at], buf,
        )


def front_chunk(
    x_ref, taps_ref, filt_ref, cot_ref,
    kv_ref, q0_ref, pt_ref, qt_ref, ct_ref, w_ref,
    buf,
):
    parts, rows, lanes = x_ref.shape
    groups, block = filt_ref.shape
    members = lanes // groups
    blocks = rows // block
    for part in range(parts):
        buf[part, HALO:, :] = x_ref[part].astype(F32)
    for number in range(blocks):
        span = slice(number * block, (number + 1) * block)
        start = HALO + number * block
        q, k, v = (featurize(buf, part, start, block, taps_ref) for part in range(3))
        kv_ref[0, span, :] = k
        kv_ref[1, span, :] = v
        if number == 0:
            q0_ref[...] = q
        else:
            place = slice((number - 1) * members, number * members)
            product = (k.astype(F32) * v.astype(F32)).astype(BF16)
            pt_ref[:, place, :] = product.T.reshape(groups, members, block)
            qt_ref[:, place, :] = q.T.reshape(groups, members, block)
        place = slice(number * members, (number + 1) * members)
        ct_ref[:, place, :] = cot_ref[span, :].T.reshape(groups, members, block)
    row, col = lag_masks(block)
    for group in range(groups):
        taps = jnp.broadcast_to(filt_ref[group : group + 1, :].astype(F32), (block, block))
        circ = pltpu.roll(taps, 0, 1, stride=1, stride_axis=0)
        w_ref[group, :block, :] = jnp.where(col >= row, circ, 0.0).astype(BF16)
        w_ref[group, block:, :] = jnp.where(col < row, circ, 0.0).astype(BF16)


def skip_columns(skip_ref, block):
    lanes = skip_ref.shape[1]
    return jnp.broadcast_to(skip_ref[...].astype(F32), (block, lanes)).T


def middle_kernel(
    rim_ref, x_ref, taps_ref, skip_ref, kv_ref, q0_ref, pt_ref, qt_ref, ct_ref, w_ref,
    kvr_ref, pta_ref, qta_ref, inner_ref, stats_ref,
    buf, acc,
):
    channels = rim_ref.shape[1]
    block = q0_ref.shape[0]
    members = channels // w_ref.shape[0]
    groups = LANES // members
    blocks = ct_ref.shape[1] // members
    acc[...] = jnp.zeros_like(acc)

    @pl.loop(0, channels // LANES)
    def _(chunk):
        lane = pl.ds(pl.multiple_of(chunk * LANES, LANES), LANES)
        group_at = pl.ds(pl.multiple_of(chunk * groups, groups), groups)
        middle_chunk(
            rim_ref.at[:, lane], x_ref.at[:, :EDGE, lane], taps_ref.at[:, :, lane], skip_ref.at[:, lane],
            kv_ref.at[:, :block, lane], q0_ref.at[:, lane], pt_ref.at[group_at], qt_ref.at[group_at],
            ct_ref.at[group_at], w_ref.at[group_at], kvr_ref.at[:, :, lane], pta_ref.at[group_at],
            qta_ref.at[group_at], inner_ref.at[group_at], buf, acc,
        )

    for which in range(2):
        for number in range(blocks):
            at = which * blocks + number
            stats_ref[at : at + 1, :] = jnp.sum(
                acc[which, number * 8 : number * 8 + 8, :], axis=0, keepdims=True
            )


def middle_chunk(
    rim_ref, x0_ref, taps_ref, skip_ref, kv_ref, q0_ref, pt_ref, qt_ref, ct_ref, w_ref,
    kvr_ref, pta_ref, qta_ref, inner_ref,
    buf, acc,
):
    block = q0_ref.shape[0]
    groups, width, lanes = w_ref.shape[0], ct_ref.shape[1], q0_ref.shape[1]
    members = lanes // groups
    blocks = width // members
    tail = block + HALO
    for part in range(2):
        buf[1 + part, :tail, :] = rim_ref[part * tail : (part + 1) * tail, :].astype(F32)
        buf[1 + part, tail : tail + EDGE, :] = x0_ref[1 + part].astype(F32)
    buf[0, :HALO, :] = rim_ref[2 * tail : 2 * tail + HALO, :].astype(F32)
    buf[0, HALO : HALO + EDGE, :] = x0_ref[0].astype(F32)
    q_edge = featurize(buf, 0, HALO, EDGE, taps_ref)
    k_rim = featurize(buf, 1, HALO, block, taps_ref)
    v_rim = featurize(buf, 2, HALO, block, taps_ref)
    k_edge = featurize(buf, 1, tail, EDGE, taps_ref)
    v_edge = featurize(buf, 2, tail, EDGE, taps_ref)
    kvr_ref[0, :block, :] = k_rim
    kvr_ref[1, :block, :] = v_rim
    kvr_ref[0, block:, :] = k_edge
    kvr_ref[1, block:, :] = v_edge
    k0 = jnp.concatenate([k_edge, kv_ref[0, EDGE:, :]], axis=0)
    v0 = jnp.concatenate([v_edge, kv_ref[1, EDGE:, :]], axis=0)
    q0 = jnp.concatenate([q_edge, q0_ref[EDGE:, :]], axis=0)
    p_rim = (k_rim.astype(F32) * v_rim.astype(F32)).astype(BF16)
    p0 = (k0.astype(F32) * v0.astype(F32)).astype(BF16)
    pta_ref[:, :members, :] = p_rim.T.reshape(groups, members, block)
    pta_ref[:, members:, :] = p0.T.reshape(groups, members, block)
    qta_ref[...] = q0.T.reshape(groups, members, block)
    skip = skip_columns(skip_ref, block)
    for group in range(groups):
        every = jnp.concatenate([pta_ref[group], pt_ref[group]], axis=0)
        now = every[members:]
        filtered = matmul(
            jnp.concatenate([now, every[:width]], axis=1), w_ref[group], ((1,), (0,))
        )
        own = skip[group * members : (group + 1) * members]
        own = jnp.concatenate([own] * blocks, axis=0)
        inner = filtered + own * now.astype(F32)
        inner_ref[group] = inner
        q = jnp.concatenate([qta_ref[group], qt_ref[group]], axis=0).astype(F32)
        output = q * inner
        square = output * output
        cross = ct_ref[group].astype(F32) * output
        for number in range(blocks):
            for half in range(0, members, 8):
                at = number * members + half
                place = slice(number * 8, number * 8 + 8)
                acc[0, place, :] += square[at : at + 8]
                acc[1, place, :] += cross[at : at + 8]


def back_kernel(channels_all, token_scale, taps, n_stats, *refs):
    stats_refs = refs[:n_stats]
    (rim_ref, x_ref, skip_ref, kv_ref, kvr_ref, pt_ref, pta_ref, qt_ref, qta_ref, ct_ref,
     inner_ref, w_ref, out_ref, buf, coef, skip_acc, filt_acc, pg, qg, gn) = refs[n_stats:]
    parts, rows, channels = x_ref.shape
    block = ct_ref.shape[2]
    members = channels // ct_ref.shape[0]
    groups = LANES // members
    blocks = rows // block
    total = merged([ref[...] for ref in stats_refs])
    square = total[:blocks]
    cross = total[blocks : 2 * blocks] / channels_all
    rms = jnp.sqrt(square / channels_all + 1e-05)
    inv = token_scale / rms
    fall = token_scale * cross / (rms * rms * rms)
    for number in range(blocks):
        place = slice(number * members, (number + 1) * members)
        coef[0, place, :] = jnp.broadcast_to(inv[number : number + 1], (members, block))
        coef[1, place, :] = jnp.broadcast_to(fall[number : number + 1], (members, block))

    @pl.loop(0, channels // LANES)
    def _(chunk):
        lane = pl.ds(pl.multiple_of(chunk * LANES, LANES), LANES)
        group_at = pl.ds(pl.multiple_of(chunk * groups, groups), groups)
        back_chunk(
            taps, rim_ref.at[:, lane], x_ref.at[:, :, lane], skip_ref.at[:, lane], kv_ref.at[:, :, lane],
            kvr_ref.at[:, :, lane], pt_ref.at[group_at], pta_ref.at[group_at], qt_ref.at[group_at],
            qta_ref.at[group_at], ct_ref.at[group_at], inner_ref.at[group_at], w_ref.at[group_at],
            out_ref.at[:, lane], buf, coef, skip_acc, filt_acc, pg, qg, gn,
        )


def back_chunk(
    taps, rim_ref, x_ref, skip_ref, kv_ref, kvr_ref, pt_ref, pta_ref, qt_ref, qta_ref, ct_ref,
    inner_ref, w_ref, out_ref, buf, coef, skip_acc, filt_acc, pg, qg, gn,
):
    parts, rows, lanes = x_ref.shape
    groups, width, block = ct_ref.shape
    members = lanes // groups
    blocks = rows // block
    tail = block + HALO
    buf[0, tail - HALO : tail, :] = rim_ref[2 * tail : 2 * tail + HALO, :].astype(F32)
    for part in range(parts):
        if part:
            buf[part, :tail, :] = rim_ref[(part - 1) * tail : part * tail, :].astype(F32)
        buf[part, tail:, :] = x_ref[part].astype(F32)
    skip = skip_columns(skip_ref, block)
    row, col = lag_masks(block)
    near_side = col <= row
    for group in range(groups):
        members_at = slice(group * members, (group + 1) * members)
        every = jnp.concatenate([pta_ref[group], pt_ref[group]], axis=0)
        now = every[members:]
        q = jnp.concatenate([qta_ref[group], qt_ref[group]], axis=0).astype(F32)
        inner = inner_ref[group]
        output = q * inner
        out_grad = coef[0] * ct_ref[group].astype(F32) - coef[1] * output
        conv_grad = out_grad * q
        cot = conv_grad.astype(BF16)
        query_grad = out_grad * inner
        weighted = conv_grad * now.astype(F32)
        part_sum = weighted[:members]
        for number in range(1, blocks):
            part_sum = part_sum + weighted[number * members : (number + 1) * members]
        skip_acc[members_at, :] = part_sum
        gap = jnp.zeros((members, block), BF16)
        here = jnp.concatenate([gap, cot], axis=0)
        later = jnp.concatenate([cot, gap], axis=0)
        grad = matmul(here, w_ref[group, :block, :], ((1,), (1,))) + matmul(
            later, w_ref[group, block:, :], ((1,), (1,))
        )
        own = skip[members_at]
        pg[0, members_at, :] = grad[:members]
        for number in range(blocks):
            span = slice(number * members, (number + 1) * members)
            pg[1 + number, members_at, :] = (
                grad[(number + 1) * members : (number + 2) * members] + own * conv_grad[span]
            )
            qg[number, members_at, :] = query_grad[span]
        both = matmul(cot, jnp.concatenate([now, every[:width]], axis=1), ((0,), (0,)))
        lagged = jnp.where(near_side, both[:, :block], both[:, block:])
        skewed = lagged[:8]
        for at in range(8, block, 8):
            skewed = skewed + pltpu.roll(lagged[at : at + 8], block - at, 1)
        filt_acc[group * 8 : group * 8 + 8, :] = skewed
    flip = jnp.where(((row + col) % block) == 0, 1.0, 0.0).astype(F32)
    lags = filt_acc[pl.ds(0, groups, stride=8), :]
    for at in range(1, 8):
        lags = lags + pltpu.roll(filt_acc[pl.ds(at, groups, stride=8), :], block - at, 1)
    out_ref[3 * 8 :, :] = lax.dot_general(
        lags, flip, (((1,), (0,)), ((), ())),
        preferred_element_type=F32, precision=lax.Precision.HIGHEST,
    )
    skip_row = jnp.sum(skip_acc[...].T, axis=0, keepdims=True)
    for number in range(blocks + 1):
        span = slice(number * block, (number + 1) * block)
        back = pg[number].T
        if number == 0:
            k, v = kvr_ref[0, :block, :], kvr_ref[1, :block, :]
        elif number == 1:
            k = jnp.concatenate([kvr_ref[0, block:, :], kv_ref[0, EDGE:block, :]], axis=0)
            v = jnp.concatenate([kvr_ref[1, block:, :], kv_ref[1, EDGE:block, :]], axis=0)
        else:
            local = slice((number - 1) * block, number * block)
            k, v = kv_ref[0, local, :], kv_ref[1, local, :]
        gn[1, span, :] = back * v.astype(F32)
        gn[2, span, :] = back * k.astype(F32)
        if number:
            gn[0, span, :] = qg[number - 1].T
    chunk = 64
    for part in range(parts):
        first = 0 if part else block
        sums = [None] * taps
        for at in range(first, rows + block, chunk):
            grads = gn[part, at : at + chunk, :]
            for tap in range(taps):
                start = HALO + at - tap
                term = grads * buf[part, start : start + chunk, :]
                term = term.reshape(chunk // 8, 8, lanes).sum(axis=0)
                sums[tap] = term if sums[tap] is None else sums[tap] + term
        for tap in range(taps):
            at = part * 8 + tap
            out_ref[at : at + 1, :] = jnp.sum(sums[tap], axis=0, keepdims=True)
        out_ref[part * 8 + taps : part * 8 + 8, :] = skip_row


def finish_kernel(n_in, *refs):
    ins = refs[:n_in]
    feat_ref, filt_ref, skip_ref = refs[n_in:]
    total = merged([ref[...].astype(F32) for ref in ins])
    taps = feat_ref.shape[1]
    for part in range(feat_ref.shape[0]):
        feat_ref[part] = total[part * 8 : part * 8 + taps]
    skip_ref[...] = total[taps : taps + 1]
    groups = total.shape[0] - 24
    for chunk in range(total.shape[1] // LANES):
        filt_ref[chunk * groups : (chunk + 1) * groups, :] = total[24:, chunk * LANES : (chunk + 1) * LANES]


def shifted(array, axis, by):
    length = lax.axis_size(axis)
    pairs = [(i, i + by) for i in range(length) if 0 <= i + by < length]
    return lax.ppermute(array, axis, pairs)


def crossed(array, axis, bit):
    length = lax.axis_size(axis)
    return lax.ppermute(array, axis, [(i, i ^ bit) for i in range(length)])


def quartet(array, axis, bit):
    return [array] + [crossed(array, axis, bit * k) for k in (1, 2, 3)]


def merged(parts):
    if len(parts) == 1:
        return parts[0]
    return (parts[0] + parts[1]) + (parts[2] + parts[3])


def on_chip(name, kernel, out_shape, scratch, args, final=False):
    place = pl.BlockSpec(memory_space=pltpu.VMEM)
    if not final:
        out_shape = [pltpu.VMEM(out.shape, out.dtype) for out in out_shape]
    args = [pltpu.with_memory_space_constraint(arg, pltpu.VMEM) for arg in args]
    return pl.pallas_call(
        kernel,
        name=name,
        in_specs=[place] * len(args),
        out_specs=[place] * len(out_shape),
        out_shape=out_shape,
        scratch_shapes=scratch,
        compiler_params=pltpu.CompilerParams(vmem_limit_bytes=16 * 1024 * 1024),
    )(*args)


def body(projected, featurizer, long_filter, skip_gain, out_cotangent):
    parts, rows, channels = projected.shape
    groups, block = long_filter.shape
    taps = featurizer.shape[0]
    members = channels // groups
    chunk_groups = LANES // members
    blocks = rows // block
    width = blocks * members
    tail = block + HALO
    taps_major = jnp.transpose(featurizer, (1, 0, 2))
    skip_row = skip_gain.reshape(1, channels)

    packed = jnp.concatenate(
        [projected[1, rows - tail :], projected[2, rows - tail :], projected[0, rows - HALO :]], axis=0
    )
    rim = shifted(packed, "seq", 1)

    sds = jax.ShapeDtypeStruct

    kv, q0, pt, qt, ct, w = on_chip(
        "front",
        front_kernel,
        [
            sds((2, rows, channels), BF16),
            sds((block, channels), BF16),
            sds((groups, width - members, block), BF16),
            sds((groups, width - members, block), BF16),
            sds((groups, width, block), BF16),
            sds((groups, 2 * block, block), BF16),
        ],
        [pltpu.VMEM((parts, HALO + rows, LANES), F32)],
        (projected, taps_major, long_filter, out_cotangent),
    )
    kvr, pta, qta, inner, stats = on_chip(
        "middle",
        middle_kernel,
        [
            sds((2, block + EDGE, channels), BF16),
            sds((groups, 2 * members, block), BF16),
            sds((groups, members, block), BF16),
            sds((groups, width, block), F32),
            sds((2 * blocks, block), F32),
        ],
        [
            pltpu.VMEM((parts, tail + EDGE, LANES), F32),
            pltpu.VMEM((2, 8 * blocks, block), F32),
        ],
        (rim, projected, taps_major, skip_row, kv, q0, pt, qt, ct, w),
    )

    dp_size = lax.axis_size("dp")
    stat_parts = [stats]
    bit = 1
    while bit < dp_size:
        current = merged(stat_parts)
        if bit * 4 <= dp_size:
            stat_parts = quartet(current, "dp", bit)
            bit *= 4
        else:
            stat_parts = [current + crossed(current, "dp", bit)]
            bit *= 2
    token_scale = 1.0 / math.sqrt(rows * lax.axis_size("seq"))
    (out,) = on_chip(
        "back",
        functools.partial(back_kernel, channels * dp_size, token_scale, taps, len(stat_parts)),
        [sds((24 + chunk_groups, channels), F32)],
        [
            pltpu.VMEM((parts, tail + rows, LANES), F32),
            pltpu.VMEM((2, width, block), F32),
            pltpu.VMEM((LANES, block), F32),
            pltpu.VMEM((chunk_groups * 8, block), F32),
            pltpu.VMEM((blocks + 1, LANES, block), F32),
            pltpu.VMEM((blocks, LANES, block), F32),
            pltpu.VMEM((parts, block + rows, LANES), F32),
        ],
        (*stat_parts, rim, projected, skip_row, kv, kvr, pt, pta, qt, qta, ct, inner, w),
    )

    seq_size = lax.axis_size("seq")
    out_parts = [out + crossed(out, "seq", 1)]
    bit = 2
    while bit < seq_size:
        current = merged([part.astype(F32) for part in out_parts]).astype(BF16)
        if bit * 4 <= seq_size:
            out_parts = quartet(current, "seq", bit)
            bit *= 4
        else:
            out_parts = [current.astype(F32) + crossed(current, "seq", bit).astype(F32)]
            bit *= 2

    feat, filt, skip = on_chip(
        "finish",
        functools.partial(finish_kernel, len(out_parts)),
        [
            sds((parts, taps, channels), F32),
            sds((groups, block), F32),
            sds((1, channels), F32),
        ],
        [],
        out_parts,
        final=True,
    )
    return (jnp.transpose(feat, (1, 0, 2)), filt, skip.reshape(channels))


def solution(mesh):
    return jax.shard_map(
        body,
        mesh=mesh,
        in_specs=(
            P(None, "seq", "dp"),
            P(None, None, "dp"),
            P("dp", None),
            P("dp"),
            P("seq", "dp"),
        ),
        out_specs=(P(None, None, "dp"), P("dp", None), P("dp")),
        check_vma=False,
    )
```

```python
import functools
import math

import jax
import jax.numpy as jnp
from jax import lax
from jax.experimental import pallas as pl
from jax.experimental.pallas import tpu as pltpu
from jax.sharding import PartitionSpec as P


F32 = jnp.float32
BF16 = jnp.bfloat16
LANES = 128
HALO = 8
EDGE = 16


def matmul(a, b, contract):
    return lax.dot_general(
        a, b, ((contract[0], contract[1]), ((), ())), preferred_element_type=F32
    )


def featurize(buf, part, start, rows, taps_ref):
    taps = taps_ref.shape[1]
    total = None
    for tap in range(taps):
        weight = taps_ref[part, tap : tap + 1, :].astype(F32)
        term = weight * buf[part, start - tap : start - tap + rows, :]
        total = term if total is None else total + term
    return total.astype(BF16)


def lag_masks(block):
    row = lax.broadcasted_iota(jnp.int32, (block, block), 0)
    col = lax.broadcasted_iota(jnp.int32, (block, block), 1)
    return row, col


def edge_kernel(x_ref, taps_hbm, near_ref, taps_ref, far_ref, buf, sems):
    _, rows, channels = x_ref.shape
    tail = far_ref.shape[1]
    block = tail - HALO
    copies = [
        pltpu.make_async_copy(
            x_ref.at[1 + part, pl.ds(rows - tail, tail), :], far_ref.at[part], sems.at[part]
        )
        for part in range(2)
    ]
    copies.append(
        pltpu.make_async_copy(
            x_ref.at[0, pl.ds(rows - HALO, HALO), :], near_ref.at[pl.ds(block, HALO), :], sems.at[2]
        )
    )
    copies.append(pltpu.make_async_copy(taps_hbm, taps_ref, sems.at[3]))
    for copy in copies:
        copy.start()
    for copy in copies:
        copy.wait()

    @pl.loop(0, channels // LANES)
    def _(chunk):
        lane = pl.ds(pl.multiple_of(chunk * LANES, LANES), LANES)
        for part in range(2):
            buf[1 + part] = far_ref[part, :, lane].astype(F32)
            at = block + (1 + part) * HALO
            near_ref[at : at + HALO, lane] = far_ref[part, tail - HALO :, lane]
        k = featurize(buf, 1, HALO, block, taps_ref.at[:, :, lane])
        v = featurize(buf, 2, HALO, block, taps_ref.at[:, :, lane])
        near_ref[:block, lane] = (k.astype(F32) * v.astype(F32)).astype(BF16)


def front_kernel(
    x_ref, taps_ref, filt_ref, cot_ref,
    far_ref, x_all, kv_ref, q0_ref, pt_ref, qt_ref, ct_ref, w_ref,
    buf, mask, cot_all, x_sems, cot_sems,
):
    parts, rows, channels = x_ref.shape
    block = filt_ref.shape[1]
    members = channels // filt_ref.shape[0]
    groups = LANES // members

    def copies(chunk):
        lane = pl.ds(pl.multiple_of(chunk * LANES, LANES), LANES)
        return (
            pltpu.make_async_copy(x_ref.at[:, :, lane], x_all.at[chunk], x_sems.at[chunk]),
            pltpu.make_async_copy(cot_ref.at[:, lane], cot_all.at[chunk], cot_sems.at[chunk]),
        )

    @pl.loop(0, channels // LANES)
    def _(chunk):
        for copy in copies(chunk):
            copy.start()

    buf[:, :HALO, :] = jnp.zeros((parts, HALO, LANES), F32)
    row, col = lag_masks(block)
    mask[...] = jnp.where(col >= row, 1.0, 0.0).astype(BF16)

    @pl.loop(0, channels // LANES)
    def _(chunk):
        rows_here = filt_ref[pl.ds(pl.multiple_of(chunk * groups, groups), groups), :].astype(F32)
        for number in range(groups):
            group = chunk * groups + number
            taps = jnp.broadcast_to(rows_here[number : number + 1], (block, block))
            circ = pltpu.roll(taps, 0, 1, stride=1, stride_axis=0).astype(BF16)
            near = circ * mask[...]
            w_ref[group, :block, :] = near
            w_ref[group, block:, :] = circ - near

    @pl.loop(0, channels // LANES)
    def _(chunk):
        lane = pl.ds(pl.multiple_of(chunk * LANES, LANES), LANES)
        group_at = pl.ds(pl.multiple_of(chunk * groups, groups), groups)
        for copy in copies(chunk):
            copy.wait()
        front_chunk(
            x_all.at[chunk], taps_ref.at[:, :, lane], cot_all.at[chunk],
            kv_ref.at[chunk], q0_ref.at[:, lane], pt_ref.at[group_at], qt_ref.at[group_at],
            ct_ref.at[group_at], buf,
        )
        tail = far_ref.shape[0] // 2
        for part in range(2):
            far_ref[part * tail : (part + 1) * tail, lane] = x_all[chunk, 1 + part, rows - tail :, :]


def front_chunk(x_ref, taps_ref, cot_ref, kv_ref, q0_ref, pt_ref, qt_ref, ct_ref, buf):
    parts, rows, lanes = x_ref.shape
    groups, _, block = ct_ref.shape
    members = lanes // groups
    blocks = rows // block
    for part in range(parts):
        buf[part, HALO:, :] = x_ref[part].astype(F32)
    for number in range(blocks):
        span = slice(number * block, (number + 1) * block)
        start = HALO + number * block
        q, k, v = (featurize(buf, part, start, block, taps_ref) for part in range(3))
        kv_ref[0, span, :] = k
        kv_ref[1, span, :] = v
        if number == 0:
            q0_ref[...] = q
        else:
            place = slice((number - 1) * members, number * members)
            product = (k.astype(F32) * v.astype(F32)).astype(BF16)
            pt_ref[:, place, :] = product.T.reshape(groups, members, block)
            qt_ref[:, place, :] = q.T.reshape(groups, members, block)
        place = slice(number * members, (number + 1) * members)
        ct_ref[:, place, :] = cot_ref[span, :].T.reshape(groups, members, block)


def skip_columns(skip_ref, block):
    lanes = skip_ref.shape[1]
    return jnp.broadcast_to(skip_ref[...].astype(F32), (block, lanes)).T


def middle_kernel(
    near_ref, x_ref, taps_ref, skip_ref, kv_ref, q0_ref, pt_ref, qt_ref, ct_ref, w_ref,
    kve_ref, pta_ref, qta_ref, inner_ref, stats_ref,
    buf, acc,
):
    channels = near_ref.shape[1]
    block = q0_ref.shape[0]
    members = channels // w_ref.shape[0]
    groups = LANES // members
    blocks = ct_ref.shape[1] // members
    acc[...] = jnp.zeros_like(acc)

    @pl.loop(0, channels // LANES)
    def _(chunk):
        lane = pl.ds(pl.multiple_of(chunk * LANES, LANES), LANES)
        group_at = pl.ds(pl.multiple_of(chunk * groups, groups), groups)
        middle_chunk(
            near_ref.at[:, lane], x_ref.at[chunk, :, :EDGE], taps_ref.at[:, :, lane], skip_ref.at[:, lane],
            kv_ref.at[chunk, :, :block], q0_ref.at[:, lane], pt_ref.at[group_at], qt_ref.at[group_at],
            ct_ref.at[group_at], w_ref.at[group_at], kve_ref.at[chunk], pta_ref.at[group_at],
            qta_ref.at[group_at], inner_ref.at[group_at], buf, acc,
        )

    for which in range(2):
        for number in range(blocks):
            at = which * blocks + number
            stats_ref[at : at + 1, :] = jnp.sum(
                acc[which, number * 8 : number * 8 + 8, :], axis=0, keepdims=True
            )


def middle_chunk(
    near_ref, x0_ref, taps_ref, skip_ref, kv_ref, q0_ref, pt_ref, qt_ref, ct_ref, w_ref,
    kve_ref, pta_ref, qta_ref, inner_ref,
    buf, acc,
):
    block = q0_ref.shape[0]
    groups, width, lanes = w_ref.shape[0], ct_ref.shape[1], q0_ref.shape[1]
    members = lanes // groups
    blocks = width // members
    for part in range(3):
        at = block + part * HALO
        buf[part, :HALO, :] = near_ref[at : at + HALO, :].astype(F32)
        buf[part, HALO:, :] = x0_ref[part].astype(F32)
    q_edge, k_edge, v_edge = (featurize(buf, part, HALO, EDGE, taps_ref) for part in range(3))
    kve_ref[0] = k_edge
    kve_ref[1] = v_edge
    k0 = jnp.concatenate([k_edge, kv_ref[0, EDGE:, :]], axis=0)
    v0 = jnp.concatenate([v_edge, kv_ref[1, EDGE:, :]], axis=0)
    q0 = jnp.concatenate([q_edge, q0_ref[EDGE:, :]], axis=0)
    p_rim = near_ref[:block, :]
    p0 = (k0.astype(F32) * v0.astype(F32)).astype(BF16)
    pta_ref[:, :members, :] = p_rim.T.reshape(groups, members, block)
    pta_ref[:, members:, :] = p0.T.reshape(groups, members, block)
    qta_ref[...] = q0.T.reshape(groups, members, block)
    skip = skip_columns(skip_ref, block)
    for group in range(groups):
        every = jnp.concatenate([pta_ref[group], pt_ref[group]], axis=0)
        now = every[members:]
        filtered = matmul(
            jnp.concatenate([now, every[:width]], axis=1), w_ref[group], ((1,), (0,))
        )
        own = skip[group * members : (group + 1) * members]
        own = jnp.concatenate([own] * blocks, axis=0)
        inner = filtered + own * now.astype(F32)
        inner_ref[group] = inner
        q = jnp.concatenate([qta_ref[group], qt_ref[group]], axis=0).astype(F32)
        output = q * inner
        square = output * output
        cross = ct_ref[group].astype(F32) * output
        for number in range(blocks):
            for half in range(0, members, 8):
                at = number * members + half
                place = slice(number * 8, number * 8 + 8)
                acc[0, place, :] += square[at : at + 8]
                acc[1, place, :] += cross[at : at + 8]


def prep_kernel(near_ref, x_ref, kv_ref, kve_ref, xf_ref, kvf_ref):
    parts, _, _ = x_ref.shape[1:]
    block = near_ref.shape[0] - parts * HALO

    @pl.loop(0, x_ref.shape[0])
    def _(chunk):
        lane = pl.ds(pl.multiple_of(chunk * LANES, LANES), LANES)
        for part in range(parts):
            at = block + part * HALO
            xf_ref[chunk, part, :HALO, :] = near_ref[at : at + HALO, lane].astype(F32)
            xf_ref[chunk, part, HALO:, :] = x_ref[chunk, part].astype(F32)
        for part in range(2):
            kvf_ref[chunk, part, :EDGE, :] = kve_ref[chunk, part].astype(F32)
            kvf_ref[chunk, part, EDGE:, :] = kv_ref[chunk, part, EDGE:, :].astype(F32)


def rim_kernel(far_ref, taps_ref, pgr_ref, out_ref, sum_ref, buf):
    chunks, block = pgr_ref.shape[:2]
    taps = taps_ref.shape[1]
    tail = block + HALO
    sum_ref[:8, :] = out_ref[:8, :]
    sum_ref[24:, :] = out_ref[24:, :]

    @pl.loop(0, chunks)
    def _(chunk):
        lane = pl.ds(pl.multiple_of(chunk * LANES, LANES), LANES)
        for part in range(2):
            buf[1 + part] = far_ref[part * tail : (part + 1) * tail, lane].astype(F32)
        back = pgr_ref[chunk].T
        for part in (1, 2):
            other = featurize(buf, 3 - part, HALO, block, taps_ref.at[:, :, lane]).astype(F32)
            grads = back * other
            for tap in range(taps):
                at = part * 8 + tap
                term = grads * buf[part, HALO - tap : HALO - tap + block, :]
                sum_ref[at : at + 1, lane] = out_ref[at : at + 1, lane] + jnp.sum(term, axis=0, keepdims=True)
            sum_ref[part * 8 + taps : part * 8 + 8, lane] = out_ref[part * 8 + taps : part * 8 + 8, lane]


def back_kernel(channels_all, token_scale, taps, n_stats, *refs):
    stats_refs = refs[:n_stats]
    (skip_ref, xf_ref, kvf_ref, pt_ref, pta_ref, qt_ref, qta_ref, ct_ref,
     inner_ref, w_ref, out_ref, pgr_ref, coef, *slots) = refs[n_stats:]
    chunks = xf_ref.shape[0]
    block = ct_ref.shape[2]
    members = chunks * LANES // ct_ref.shape[0]
    groups = LANES // members
    blocks = ct_ref.shape[1] // members
    slots = (slots[: len(slots) // 2], slots[len(slots) // 2 :])
    total = merged([ref[...] for ref in stats_refs])
    square = total[:blocks]
    cross = total[blocks : 2 * blocks] / channels_all
    rms = jnp.sqrt(square / channels_all + 1e-05)
    inv = token_scale / rms
    fall = token_scale * cross / (rms * rms * rms)
    for number in range(blocks):
        place = slice(number * members, (number + 1) * members)
        coef[0, place, :] = jnp.broadcast_to(inv[number : number + 1], (members, block))
        coef[1, place, :] = jnp.broadcast_to(fall[number : number + 1], (members, block))

    def at(chunk):
        lane = pl.ds(pl.multiple_of(chunk * LANES, LANES), LANES)
        group_at = pl.ds(pl.multiple_of(chunk * groups, groups), groups)
        return lane, group_at

    def first(chunk, slot):
        lane, group_at = at(chunk)
        return group_steps(
            skip_ref.at[:, lane], pt_ref.at[group_at], pta_ref.at[group_at], qt_ref.at[group_at],
            qta_ref.at[group_at], ct_ref.at[group_at], inner_ref.at[group_at], w_ref.at[group_at],
            coef, pgr_ref.at[chunk], *slots[slot][:4],
        )

    def second(chunk, slot):
        lane, _ = at(chunk)
        return tap_steps(
            taps, groups, xf_ref.at[chunk], kvf_ref.at[chunk], out_ref.at[:, lane], *slots[slot],
        )

    braid(first(0, 0), [])
    pairs = (chunks - 1) // 2

    @pl.loop(0, pairs)
    def _(pair):
        braid(first(2 * pair + 1, 1), second(2 * pair, 0))
        braid(first(2 * pair + 2, 0), second(2 * pair + 1, 1))

    if chunks % 2 == 0:
        braid(first(chunks - 1, 1), second(chunks - 2, 0))
        braid([], second(chunks - 1, 1))
    else:
        braid([], second(chunks - 1, 0))


def braid(one, two):
    done = 0
    for number, step in enumerate(one):
        step()
        upto = (number + 1) * len(two) // len(one)
        for other in two[done:upto]:
            other()
        done = upto
    for other in two[done:]:
        other()


def group_steps(
    skip_ref, pt_ref, pta_ref, qt_ref, qta_ref, ct_ref, inner_ref, w_ref, coef, pgr_ref, skip_acc, filt_acc, pg, qg
):
    groups, width, block = ct_ref.shape
    members = LANES // groups
    blocks = width // members
    row, col = lag_masks(block)
    near_side = col <= row
    skip = skip_columns(skip_ref, block)

    def step(group):
        members_at = slice(group * members, (group + 1) * members)
        every = jnp.concatenate([pta_ref[group], pt_ref[group]], axis=0)
        now = every[members:]
        q = jnp.concatenate([qta_ref[group], qt_ref[group]], axis=0).astype(F32)
        inner = inner_ref[group]
        output = q * inner
        out_grad = coef[0] * ct_ref[group].astype(F32) - coef[1] * output
        conv_grad = out_grad * q
        cot = conv_grad.astype(BF16)
        query_grad = out_grad * inner
        weighted = conv_grad * now.astype(F32)
        part_sum = weighted[:members]
        for number in range(1, blocks):
            part_sum = part_sum + weighted[number * members : (number + 1) * members]
        skip_acc[members_at, :] = part_sum
        gap = jnp.zeros((members, block), BF16)
        here = jnp.concatenate([gap, cot], axis=0)
        later = jnp.concatenate([cot, gap], axis=0)
        grad = matmul(here, w_ref[group, :block, :], ((1,), (1,))) + matmul(
            later, w_ref[group, block:, :], ((1,), (1,))
        )
        own = skip[members_at]
        pgr_ref[members_at, :] = grad[:members]
        for number in range(blocks):
            span = slice(number * members, (number + 1) * members)
            pg[number, members_at, :] = (
                grad[(number + 1) * members : (number + 2) * members] + own * conv_grad[span]
            )
            qg[number, members_at, :] = query_grad[span]
        both = matmul(cot, jnp.concatenate([now, every[:width]], axis=1), ((0,), (0,)))
        lagged = jnp.where(near_side, both[:, :block], both[:, block:])
        skewed = lagged[:8]
        for start in range(8, block, 8):
            skewed = skewed + pltpu.roll(lagged[start : start + 8], block - start, 1)
        filt_acc[group * 8 : group * 8 + 8, :] = skewed

    return [functools.partial(step, group) for group in range(groups)]


def tap_steps(taps, groups, xf_ref, kvf_ref, out_ref, skip_acc, filt_acc, pg, qg, gn):
    parts, lanes = xf_ref.shape[0], xf_ref.shape[2]
    block = pg.shape[2]
    blocks = qg.shape[0]
    piece = 32
    sums = {}

    def step(number, part):
        if part != 2:
            gn[...] = pg[number].T if part else qg[number].T
        for at in range(0, block, piece):
            begin = number * block + at
            grads = gn[at : at + piece, :]
            if part:
                grads = grads * kvf_ref[2 - part, begin : begin + piece, :]
            for tap in range(taps):
                start = HALO + begin - tap
                term = grads * xf_ref[part, start : start + piece, :]
                term = term.reshape(piece // 8, 8, lanes).sum(axis=0)
                sums[part, tap] = term if (part, tap) not in sums else sums[part, tap] + term
        if number == blocks - 1:
            for tap in range(taps):
                at = part * 8 + tap
                out_ref[at : at + 1, :] = jnp.sum(sums[part, tap], axis=0, keepdims=True)

    def last():
        row, col = lag_masks(block)
        flip = jnp.where(((row + col) % block) == 0, 1.0, 0.0).astype(F32)
        lags = filt_acc[pl.ds(0, groups, stride=8), :]
        for at in range(1, 8):
            lags = lags + pltpu.roll(filt_acc[pl.ds(at, groups, stride=8), :], block - at, 1)
        out_ref[3 * 8 :, :] = lax.dot_general(
            lags, flip, (((1,), (0,)), ((), ())),
            preferred_element_type=F32, precision=lax.Precision.HIGHEST,
        )
        skip_row = jnp.sum(skip_acc[...].T, axis=0, keepdims=True)
        for part in range(parts):
            out_ref[part * 8 + taps : part * 8 + 8, :] = skip_row

    steps = [functools.partial(step, number, 0) for number in range(blocks)]
    steps += [functools.partial(step, number, part) for number in range(blocks) for part in (1, 2)]
    return [last] + steps


def finish_kernel(n_in, *refs):
    ins = refs[:n_in]
    feat_ref, filt_ref, skip_ref = refs[n_in:]
    total = merged([ref[...].astype(F32) for ref in ins])
    taps = feat_ref.shape[1]
    for part in range(feat_ref.shape[0]):
        feat_ref[part] = total[part * 8 : part * 8 + taps]
    skip_ref[...] = total[taps : taps + 1]
    groups = total.shape[0] - 24
    for chunk in range(total.shape[1] // LANES):
        filt_ref[chunk * groups : (chunk + 1) * groups, :] = total[24:, chunk * LANES : (chunk + 1) * LANES]


def shifted(array, axis, by):
    length = lax.axis_size(axis)
    pairs = [(i, i + by) for i in range(length) if 0 <= i + by < length]
    return lax.ppermute(array, axis, pairs)


def crossed(array, axis, bit):
    length = lax.axis_size(axis)
    return lax.ppermute(array, axis, [(i, i ^ bit) for i in range(length)])


def quartet(array, axis, bit):
    return [array] + [crossed(array, axis, bit * k) for k in (1, 2, 3)]


def merged(parts):
    if len(parts) == 1:
        return parts[0]
    return (parts[0] + parts[1]) + (parts[2] + parts[3])


def on_chip(kernel, out_shape, scratch, args, outside=(), final=False):
    place = pl.BlockSpec(memory_space=pltpu.VMEM)
    apart = pl.BlockSpec(memory_space=pl.ANY)
    if not final:
        out_shape = [pltpu.VMEM(out.shape, out.dtype) for out in out_shape]
    args = [
        pltpu.with_memory_space_constraint(arg, pltpu.HBM if number in outside else pltpu.VMEM)
        for number, arg in enumerate(args)
    ]
    return pl.pallas_call(
        kernel,
        in_specs=[apart if number in outside else place for number in range(len(args))],
        out_specs=[place] * len(out_shape),
        out_shape=out_shape,
        scratch_shapes=scratch,
        compiler_params=pltpu.CompilerParams(vmem_limit_bytes=16 * 1024 * 1024),
    )(*args)


def body(projected, featurizer, long_filter, skip_gain, out_cotangent):
    parts, rows, channels = projected.shape
    groups, block = long_filter.shape
    taps = featurizer.shape[0]
    members = channels // groups
    chunk_groups = LANES // members
    blocks = rows // block
    width = blocks * members
    tail = block + HALO
    taps_major = jnp.transpose(featurizer, (1, 0, 2))
    skip_row = skip_gain.reshape(1, channels)

    sds = jax.ShapeDtypeStruct
    chunks = channels // LANES

    near, taps_major = on_chip(
        edge_kernel,
        [sds((block + parts * HALO, channels), BF16), sds((parts, taps, channels), BF16)],
        [
            pltpu.VMEM((2, tail, channels), BF16),
            pltpu.VMEM((parts, tail, LANES), F32),
            pltpu.SemaphoreType.DMA((4,)),
        ],
        (projected, taps_major),
        outside=(0, 1),
    )
    near = shifted(near, "seq", 1)

    far, x_all, kv, q0, pt, qt, ct, w = on_chip(
        front_kernel,
        [
            sds((2 * tail, channels), BF16),
            sds((chunks, parts, rows, LANES), BF16),
            sds((chunks, 2, rows, LANES), BF16),
            sds((block, channels), BF16),
            sds((groups, width - members, block), BF16),
            sds((groups, width - members, block), BF16),
            sds((groups, width, block), BF16),
            sds((groups, 2 * block, block), BF16),
        ],
        [
            pltpu.VMEM((parts, HALO + rows, LANES), F32),
            pltpu.VMEM((block, block), BF16),
            pltpu.VMEM((chunks, rows, LANES), BF16),
            pltpu.SemaphoreType.DMA((chunks,)),
            pltpu.SemaphoreType.DMA((chunks,)),
        ],
        (projected, taps_major, long_filter, out_cotangent),
        outside=(0, 3),
    )
    far = shifted(far, "seq", 1)
    kve, pta, qta, inner, stats = on_chip(
        middle_kernel,
        [
            sds((chunks, 2, EDGE, LANES), BF16),
            sds((groups, 2 * members, block), BF16),
            sds((groups, members, block), BF16),
            sds((groups, width, block), F32),
            sds((2 * blocks, block), F32),
        ],
        [
            pltpu.VMEM((parts, HALO + EDGE, LANES), F32),
            pltpu.VMEM((2, 8 * blocks, block), F32),
        ],
        (near, x_all, taps_major, skip_row, kv, q0, pt, qt, ct, w),
    )

    dp_size = lax.axis_size("dp")
    stat_parts = [stats]
    bit = 1
    while bit < dp_size:
        current = merged(stat_parts)
        if bit * 4 <= dp_size:
            stat_parts = quartet(current, "dp", bit)
            bit *= 4
        else:
            stat_parts = [current + crossed(current, "dp", bit)]
            bit *= 2
    xf, kvf = on_chip(
        prep_kernel,
        [sds((chunks, parts, HALO + rows, LANES), F32), sds((chunks, 2, rows, LANES), F32)],
        [],
        (near, x_all, kv, kve),
    )
    token_scale = 1.0 / math.sqrt(rows * lax.axis_size("seq"))
    out, pgr = on_chip(
        functools.partial(back_kernel, channels * dp_size, token_scale, taps, len(stat_parts)),
        [sds((24 + chunk_groups, channels), F32), sds((chunks, LANES, block), F32)],
        [pltpu.VMEM((2, width, block), F32)]
        + [
            pltpu.VMEM((LANES, block), F32),
            pltpu.VMEM((chunk_groups * 8, block), F32),
            pltpu.VMEM((blocks, LANES, block), F32),
            pltpu.VMEM((blocks, LANES, block), F32),
            pltpu.VMEM((block, LANES), F32),
        ]
        * 2,
        (*stat_parts, skip_row, xf, kvf, pt, pta, qt, qta, ct, inner, w),
    )
    (out,) = on_chip(
        rim_kernel,
        [sds((24 + chunk_groups, channels), F32)],
        [pltpu.VMEM((parts, tail, LANES), F32)],
        (far, taps_major, pgr, out),
    )

    seq_size = lax.axis_size("seq")
    out_parts = [out + crossed(out, "seq", 1)]
    bit = 2
    while bit < seq_size:
        current = merged([part.astype(F32) for part in out_parts]).astype(BF16)
        if bit * 4 <= seq_size:
            out_parts = quartet(current, "seq", bit)
            bit *= 4
        else:
            out_parts = [current.astype(F32) + crossed(current, "seq", bit).astype(F32)]
            bit *= 2

    feat, filt, skip = on_chip(
        functools.partial(finish_kernel, len(out_parts)),
        [
            sds((parts, taps, channels), F32),
            sds((groups, block), F32),
            sds((1, channels), F32),
        ],
        [],
        out_parts,
        final=True,
    )
    return (jnp.transpose(feat, (1, 0, 2)), filt, skip.reshape(channels))


def solution(mesh):
    return jax.shard_map(
        body,
        mesh=mesh,
        in_specs=(
            P(None, "seq", "dp"),
            P(None, None, "dp"),
            P("dp", None),
            P("dp"),
            P("seq", "dp"),
        ),
        out_specs=(P(None, None, "dp"), P("dp", None), P("dp")),
        check_vma=False,
    )
```

```python
import functools
import math

import jax
import jax.numpy as jnp
from jax import lax
from jax.experimental import pallas as pl
from jax.experimental.pallas import tpu as pltpu
from jax.sharding import PartitionSpec as P


F32 = jnp.float32
BF16 = jnp.bfloat16
LANES = 128
HALO = 8
EDGE = 16


def matmul(a, b, contract):
    return lax.dot_general(
        a, b, ((contract[0], contract[1]), ((), ())), preferred_element_type=F32
    )


def featurize(buf, part, start, rows, taps_ref):
    taps = taps_ref.shape[1]
    total = None
    for tap in range(taps):
        weight = taps_ref[part, tap : tap + 1, :].astype(F32)
        term = weight * buf[part, start - tap : start - tap + rows, :]
        total = term if total is None else total + term
    return total.astype(BF16)


def lag_masks(block):
    row = lax.broadcasted_iota(jnp.int32, (block, block), 0)
    col = lax.broadcasted_iota(jnp.int32, (block, block), 1)
    return row, col


def edge_kernel(x_ref, taps_hbm, near_ref, taps_ref, far_ref, bufs, sems):
    _, rows, channels = x_ref.shape
    tail = far_ref.shape[1]
    block = tail - HALO
    copies = [
        pltpu.make_async_copy(
            x_ref.at[1 + part, pl.ds(rows - tail, tail), :], far_ref.at[part], sems.at[part]
        )
        for part in range(2)
    ]
    copies.append(
        pltpu.make_async_copy(
            x_ref.at[0, pl.ds(rows - HALO, HALO), :], near_ref.at[pl.ds(block, HALO), :], sems.at[2]
        )
    )
    copies.append(pltpu.make_async_copy(taps_hbm, taps_ref, sems.at[3]))
    for copy in copies:
        copy.start()
    for copy in copies:
        copy.wait()

    def product(chunk, buf):
        lane = pl.ds(pl.multiple_of(chunk * LANES, LANES), LANES)
        for part in range(2):
            buf[1 + part] = far_ref[part, :, lane].astype(F32)
            at = block + (1 + part) * HALO
            near_ref[at : at + HALO, lane] = far_ref[part, tail - HALO :, lane]
        k = featurize(buf, 1, HALO, block, taps_ref.at[:, :, lane])
        v = featurize(buf, 2, HALO, block, taps_ref.at[:, :, lane])
        near_ref[:block, lane] = (k.astype(F32) * v.astype(F32)).astype(BF16)

    at_once = math.gcd(channels // LANES, bufs.shape[0])

    @pl.loop(0, channels // LANES // at_once)
    def _(turn):
        for number in range(at_once):
            product(turn * at_once + number, bufs.at[number])


def front_kernel(
    x_ref, taps_ref, filt_ref, skip_ref, cot_ref,
    far_ref, skt_ref, x_all, kv_ref, q0_ref, pt_ref, qt_ref, ct_ref, w_ref,
    buf, mask, cot_all, x_sems, cot_sems,
):
    parts, rows, channels = x_ref.shape
    block = filt_ref.shape[1]
    members = channels // filt_ref.shape[0]
    groups = LANES // members

    def copies(chunk):
        lane = pl.ds(pl.multiple_of(chunk * LANES, LANES), LANES)
        return (
            pltpu.make_async_copy(x_ref.at[:, :, lane], x_all.at[chunk], x_sems.at[chunk]),
            pltpu.make_async_copy(cot_ref.at[:, lane], cot_all.at[chunk], cot_sems.at[chunk]),
        )

    @pl.loop(0, channels // LANES)
    def _(chunk):
        for copy in copies(chunk):
            copy.start()

    buf[:, :HALO, :] = jnp.zeros((parts, HALO, LANES), F32)
    row, col = lag_masks(block)
    mask[...] = jnp.where(col >= row, 1.0, 0.0).astype(BF16)

    @pl.loop(0, channels // LANES)
    def _(chunk):
        lane = pl.ds(pl.multiple_of(chunk * LANES, LANES), LANES)
        group_at = pl.ds(pl.multiple_of(chunk * groups, groups), groups)
        skt_ref[group_at] = skip_columns(skip_ref.at[:, lane], block).reshape(groups, members, block)
        rows_here = filt_ref[pl.ds(pl.multiple_of(chunk * groups, groups), groups), :].astype(F32)
        for number in range(groups):
            group = chunk * groups + number
            taps = jnp.broadcast_to(rows_here[number : number + 1], (block, block))
            circ = pltpu.roll(taps, 0, 1, stride=1, stride_axis=0).astype(BF16)
            near = circ * mask[...]
            w_ref[group, :block, :] = near
            w_ref[group, block:, :] = circ - near

    @pl.loop(0, channels // LANES)
    def _(chunk):
        lane = pl.ds(pl.multiple_of(chunk * LANES, LANES), LANES)
        group_at = pl.ds(pl.multiple_of(chunk * groups, groups), groups)
        for copy in copies(chunk):
            copy.wait()
        front_chunk(
            x_all.at[chunk], taps_ref.at[:, :, lane], cot_all.at[chunk],
            kv_ref.at[chunk], q0_ref.at[:, lane], pt_ref.at[group_at], qt_ref.at[group_at],
            ct_ref.at[group_at], buf,
        )
        tail = far_ref.shape[0] // 2
        for part in range(2):
            far_ref[part * tail : (part + 1) * tail, lane] = x_all[chunk, 1 + part, rows - tail :, :]


def front_chunk(x_ref, taps_ref, cot_ref, kv_ref, q0_ref, pt_ref, qt_ref, ct_ref, buf):
    parts, rows, lanes = x_ref.shape
    groups, _, block = ct_ref.shape
    members = lanes // groups
    blocks = rows // block
    for part in range(parts):
        buf[part, HALO:, :] = x_ref[part].astype(F32)
    for number in range(blocks):
        span = slice(number * block, (number + 1) * block)
        start = HALO + number * block
        q, k, v = (featurize(buf, part, start, block, taps_ref) for part in range(3))
        kv_ref[0, span, :] = k
        kv_ref[1, span, :] = v
        if number == 0:
            q0_ref[...] = q
        else:
            place = slice((number - 1) * members, number * members)
            product = (k.astype(F32) * v.astype(F32)).astype(BF16)
            pt_ref[:, place, :] = product.T.reshape(groups, members, block)
            qt_ref[:, place, :] = q.T.reshape(groups, members, block)
        place = slice(number * members, (number + 1) * members)
        ct_ref[:, place, :] = cot_ref[span, :].T.reshape(groups, members, block)


def skip_columns(skip_ref, block):
    lanes = skip_ref.shape[1]
    return jnp.broadcast_to(skip_ref[...].astype(F32), (block, lanes)).T


def middle_kernel(
    near_ref, x_ref, taps_ref, skt_ref, kv_ref, q0_ref, pt_ref, qt_ref, ct_ref, w_ref,
    kve_ref, pta_ref, qta_ref, inner_ref, stats_ref,
    buf, acc,
):
    channels = near_ref.shape[1]
    block = q0_ref.shape[0]
    members = channels // w_ref.shape[0]
    groups = LANES // members
    width = ct_ref.shape[1]
    blocks = width // members
    chunks = channels // LANES
    acc[...] = jnp.zeros_like(acc)

    def heads(chunk):
        lane = pl.ds(pl.multiple_of(chunk * LANES, LANES), LANES)
        group_at = pl.ds(pl.multiple_of(chunk * groups, groups), groups)
        for part in range(3):
            at = block + part * HALO
            buf[part, :HALO, :] = near_ref[at : at + HALO, lane].astype(F32)
            buf[part, HALO:, :] = x_ref[chunk, part, :EDGE, :].astype(F32)
        q_edge, k_edge, v_edge = (
            featurize(buf, part, HALO, EDGE, taps_ref.at[:, :, lane]) for part in range(3)
        )
        kve_ref[chunk, 0] = k_edge
        kve_ref[chunk, 1] = v_edge
        k0 = jnp.concatenate([k_edge, kv_ref[chunk, 0, EDGE:block, :]], axis=0)
        v0 = jnp.concatenate([v_edge, kv_ref[chunk, 1, EDGE:block, :]], axis=0)
        q0 = jnp.concatenate([q_edge, q0_ref[EDGE:, lane]], axis=0)
        p0 = (k0.astype(F32) * v0.astype(F32)).astype(BF16)
        pta_ref[group_at, :members, :] = near_ref[:block, lane].T.reshape(groups, members, block)
        pta_ref[group_at, members:, :] = p0.T.reshape(groups, members, block)
        qta_ref[group_at] = q0.T.reshape(groups, members, block)

    def filters(chunk):
        sums = [[None] * blocks, [None] * blocks]
        for within in range(groups):
            group = chunk * groups + within
            every = jnp.concatenate([pta_ref[group], pt_ref[group]], axis=0)
            now = every[members:]
            filtered = matmul(
                jnp.concatenate([now, every[:width]], axis=1), w_ref[group], ((1,), (0,))
            )
            own = jnp.concatenate([skt_ref[group]] * blocks, axis=0)
            inner = filtered + own * now.astype(F32)
            inner_ref[group] = inner
            q = jnp.concatenate([qta_ref[group], qt_ref[group]], axis=0).astype(F32)
            output = q * inner
            for which, value in enumerate((output * output, ct_ref[group].astype(F32) * output)):
                for number in range(blocks):
                    span = value[number * members : (number + 1) * members]
                    span = span.reshape(members // 8, 8, block).sum(axis=0)
                    sums[which][number] = span if within == 0 else sums[which][number] + span
        for which in range(2):
            for number in range(blocks):
                place = slice(number * 8, number * 8 + 8)
                acc[which, place, :] += sums[which][number]

    heads(0)

    @pl.loop(1, chunks)
    def _(chunk):
        filters(chunk - 1)
        heads(chunk)

    filters(chunks - 1)
    for which in range(2):
        for number in range(blocks):
            at = which * blocks + number
            stats_ref[at : at + 1, :] = jnp.sum(
                acc[which, number * 8 : number * 8 + 8, :], axis=0, keepdims=True
            )


def prep_kernel(near_ref, x_ref, kv_ref, kve_ref, xf_ref, kvf_ref):
    parts, rows, _ = x_ref.shape[1:]
    block = near_ref.shape[0] - parts * HALO
    blocks = rows // block

    @pl.loop(0, x_ref.shape[0])
    def _(chunk):
        lane = pl.ds(pl.multiple_of(chunk * LANES, LANES), LANES)
        for part in range(parts):
            at = block + part * HALO
            xf_ref[chunk, 0, part, :HALO, :] = near_ref[at : at + HALO, lane].astype(F32)
            for number in range(blocks):
                at = number * block
                if number:
                    xf_ref[chunk, number, part, :HALO, :] = x_ref[chunk, part, at - HALO : at, :].astype(F32)
                xf_ref[chunk, number, part, HALO:, :] = x_ref[chunk, part, at : at + block, :].astype(F32)
        for part in range(2):
            kvf_ref[chunk, 0, part, :EDGE, :] = kve_ref[chunk, part].astype(F32)
            kvf_ref[chunk, 0, part, EDGE:, :] = kv_ref[chunk, part, EDGE:block, :].astype(F32)
            for number in range(1, blocks):
                at = number * block
                kvf_ref[chunk, number, part] = kv_ref[chunk, part, at : at + block, :].astype(F32)


def braid(one, two):
    done = 0
    for number, step in enumerate(one):
        step()
        upto = (number + 1) * len(two) // len(one)
        for other in two[done:upto]:
            other()
        done = upto
    for other in two[done:]:
        other()


def rim_kernel(far_ref, taps_ref, pgr_ref, out_ref, sum_ref, buf):
    members, block = pgr_ref.shape[1:]
    groups = LANES // members
    chunks = pgr_ref.shape[0] // groups
    taps = taps_ref.shape[1]
    tail = block + HALO
    sum_ref[:8, :] = out_ref[:8, :]
    sum_ref[24:, :] = out_ref[24:, :]

    @pl.loop(0, chunks)
    def _(chunk):
        lane = pl.ds(pl.multiple_of(chunk * LANES, LANES), LANES)
        for part in range(2):
            buf[1 + part] = far_ref[part * tail : (part + 1) * tail, lane].astype(F32)
        group_at = pl.ds(pl.multiple_of(chunk * groups, groups), groups)
        back = pgr_ref[group_at].reshape(LANES, block).T
        for part in (1, 2):
            other = featurize(buf, 3 - part, HALO, block, taps_ref.at[:, :, lane]).astype(F32)
            grads = back * other
            for tap in range(taps):
                at = part * 8 + tap
                term = grads * buf[part, HALO - tap : HALO - tap + block, :]
                sum_ref[at : at + 1, lane] = out_ref[at : at + 1, lane] + jnp.sum(term, axis=0, keepdims=True)
            sum_ref[part * 8 + taps : part * 8 + 8, lane] = out_ref[part * 8 + taps : part * 8 + 8, lane]


def back_kernel(channels_all, token_scale, taps, n_stats, *refs):
    stats_refs = refs[:n_stats]
    (skt_ref, xf_ref, kvf_ref, pt_ref, pta_ref, qt_ref, qta_ref, ct_ref, inner_ref, w_ref,
     out_ref, pgr_ref, coef, skip_acc, filt_acc, sums, pg, qg, gn) = refs[n_stats:]
    chunks, blocks = xf_ref.shape[:2]
    parts = xf_ref.shape[2]
    width, block = ct_ref.shape[1:]
    members = width // blocks
    groups = LANES // members
    total = merged([ref[...] for ref in stats_refs])
    square = total[:blocks]
    cross = total[blocks : 2 * blocks] / channels_all
    rms = jnp.sqrt(square / channels_all + 1e-05)
    inv = token_scale / rms
    fall = token_scale * cross / (rms * rms * rms)
    for number in range(blocks):
        place = slice(number * members, (number + 1) * members)
        coef[0, place, :] = jnp.broadcast_to(inv[number : number + 1], (members, block))
        coef[1, place, :] = jnp.broadcast_to(fall[number : number + 1], (members, block))
    row, col = lag_masks(block)

    def group_part(chunk, within):
        group = chunk * groups + within
        slot = lax.rem(chunk, 2)
        every = jnp.concatenate([pta_ref[group], pt_ref[group]], axis=0)
        now = every[members:]
        q = jnp.concatenate([qta_ref[group], qt_ref[group]], axis=0).astype(F32)
        inner = inner_ref[group]
        output = q * inner
        out_grad = coef[0] * ct_ref[group].astype(F32) - coef[1] * output
        conv_grad = out_grad * q
        cot = conv_grad.astype(BF16)
        query_grad = out_grad * inner
        weighted = conv_grad * now.astype(F32)
        part_sum = weighted[:members]
        for number in range(1, blocks):
            part_sum = part_sum + weighted[number * members : (number + 1) * members]
        skip_acc[group] = part_sum
        gap = jnp.zeros((members, block), BF16)
        here = jnp.concatenate([gap, cot], axis=0)
        later = jnp.concatenate([cot, gap], axis=0)
        grad = matmul(
            jnp.concatenate([here, later], axis=1),
            jnp.concatenate([w_ref[group, :block, :], w_ref[group, block:, :]], axis=1),
            ((1,), (1,)),
        )
        own = skt_ref[group]
        pgr_ref[group] = grad[:members]
        for number in range(blocks):
            span = slice(number * members, (number + 1) * members)
            pg[slot, number, within] = (
                grad[(number + 1) * members : (number + 2) * members] + own * conv_grad[span]
            )
            qg[slot, number, within] = query_grad[span]
        both = matmul(cot, jnp.concatenate([now, every[:width]], axis=1), ((0,), (0,)))
        lagged = jnp.where(col <= row, both[:, :block], both[:, block:])
        skewed = lagged[:8]
        for start in range(8, block, 8):
            skewed = skewed + pltpu.roll(lagged[start : start + 8], block - start, 1)
        filt_acc[group] = skewed

    def turn(chunk):
        slot = lax.rem(chunk, 2)
        for number in range(blocks):
            gn[0, number] = qg[slot, number].reshape(LANES, block).T
            gn[1, number] = pg[slot, number].reshape(LANES, block).T

    def tap_steps(chunk):
        piece = 32
        totals = {}

        def step(part, number):
            for at in range(0, block, piece):
                if part:
                    grads = gn[1, number, at : at + piece, :]
                    grads = grads * kvf_ref[chunk, number, 2 - part, at : at + piece, :]
                else:
                    grads = gn[0, number, at : at + piece, :]
                for tap in range(taps):
                    start = HALO + at - tap
                    term = grads * xf_ref[chunk, number, part, start : start + piece, :]
                    term = term.reshape(piece // 8, 8, LANES).sum(axis=0)
                    totals[part, tap] = totals[part, tap] + term if (part, tap) in totals else term
            if number == blocks - 1:
                for tap in range(taps):
                    sums[chunk, part * taps + tap] = totals[part, tap]

        return [functools.partial(step, part, number) for part in range(parts) for number in range(blocks)]

    def group_steps(chunk):
        return [functools.partial(group_part, chunk, within) for within in range(groups)]

    braid(group_steps(0), [])

    @pl.loop(1, chunks)
    def _(chunk):
        turn(chunk - 1)
        braid(group_steps(chunk), tap_steps(chunk - 1))

    turn(chunks - 1)
    braid([], tap_steps(chunks - 1))

    flip = jnp.where(((row + col) % block) == 0, 1.0, 0.0).astype(F32)
    lags = filt_acc[:, 0, :]
    for at in range(1, 8):
        lags = lags + pltpu.roll(filt_acc[:, at, :], block - at, 1)
    lags = lax.dot_general(
        lags, flip, (((1,), (0,)), ((), ())), preferred_element_type=F32, precision=lax.Precision.HIGHEST
    )
    for chunk in range(chunks):
        lane = slice(chunk * LANES, (chunk + 1) * LANES)
        group_at = slice(chunk * groups, (chunk + 1) * groups)
        out_ref[3 * 8 :, lane] = lags[group_at]
        skip_row = jnp.sum(skip_acc[group_at].reshape(LANES, block).T, axis=0, keepdims=True)
        for part in range(parts):
            for tap in range(taps):
                out_ref[part * 8 + tap : part * 8 + tap + 1, lane] = jnp.sum(
                    sums[chunk, part * taps + tap], axis=0, keepdims=True
                )
            out_ref[part * 8 + taps : part * 8 + 8, lane] = skip_row


def finish_kernel(n_in, *refs):
    ins = refs[:n_in]
    feat_ref, filt_ref, skip_ref = refs[n_in:]
    total = merged([ref[...].astype(F32) for ref in ins])
    taps = feat_ref.shape[1]
    for part in range(feat_ref.shape[0]):
        feat_ref[part] = total[part * 8 : part * 8 + taps]
    skip_ref[...] = total[taps : taps + 1]
    groups = total.shape[0] - 24
    for chunk in range(total.shape[1] // LANES):
        filt_ref[chunk * groups : (chunk + 1) * groups, :] = total[24:, chunk * LANES : (chunk + 1) * LANES]


def shifted(array, axis, by):
    length = lax.axis_size(axis)
    pairs = [(i, i + by) for i in range(length) if 0 <= i + by < length]
    return lax.ppermute(array, axis, pairs)


def crossed(array, axis, bit):
    length = lax.axis_size(axis)
    return lax.ppermute(array, axis, [(i, i ^ bit) for i in range(length)])


def quartet(array, axis, bit):
    return [array] + [crossed(array, axis, bit * k) for k in (1, 2, 3)]


def merged(parts):
    if len(parts) == 1:
        return parts[0]
    return (parts[0] + parts[1]) + (parts[2] + parts[3])


def on_chip(kernel, out_shape, scratch, args, outside=(), final=False):
    place = pl.BlockSpec(memory_space=pltpu.VMEM)
    apart = pl.BlockSpec(memory_space=pl.ANY)
    if not final:
        out_shape = [pltpu.VMEM(out.shape, out.dtype) for out in out_shape]
    args = [
        pltpu.with_memory_space_constraint(arg, pltpu.HBM if number in outside else pltpu.VMEM)
        for number, arg in enumerate(args)
    ]
    return pl.pallas_call(
        kernel,
        in_specs=[apart if number in outside else place for number in range(len(args))],
        out_specs=[place] * len(out_shape),
        out_shape=out_shape,
        scratch_shapes=scratch,
        compiler_params=pltpu.CompilerParams(vmem_limit_bytes=16 * 1024 * 1024),
    )(*args)


def body(projected, featurizer, long_filter, skip_gain, out_cotangent):
    parts, rows, channels = projected.shape
    groups, block = long_filter.shape
    taps = featurizer.shape[0]
    members = channels // groups
    chunk_groups = LANES // members
    blocks = rows // block
    width = blocks * members
    tail = block + HALO
    taps_major = jnp.transpose(featurizer, (1, 0, 2))
    skip_row = skip_gain.reshape(1, channels)

    sds = jax.ShapeDtypeStruct
    chunks = channels // LANES

    near, taps_major = on_chip(
        edge_kernel,
        [sds((block + parts * HALO, channels), BF16), sds((parts, taps, channels), BF16)],
        [
            pltpu.VMEM((2, tail, channels), BF16),
            pltpu.VMEM((2, parts, tail, LANES), F32),
            pltpu.SemaphoreType.DMA((4,)),
        ],
        (projected, taps_major),
        outside=(0, 1),
    )
    near = shifted(near, "seq", 1)

    far, skt, x_all, kv, q0, pt, qt, ct, w = on_chip(
        front_kernel,
        [
            sds((2 * tail, channels), BF16),
            sds((groups, members, block), F32),
            sds((chunks, parts, rows, LANES), BF16),
            sds((chunks, 2, rows, LANES), BF16),
            sds((block, channels), BF16),
            sds((groups, width - members, block), BF16),
            sds((groups, width - members, block), BF16),
            sds((groups, width, block), BF16),
            sds((groups, 2 * block, block), BF16),
        ],
        [
            pltpu.VMEM((parts, HALO + rows, LANES), F32),
            pltpu.VMEM((block, block), BF16),
            pltpu.VMEM((chunks, rows, LANES), BF16),
            pltpu.SemaphoreType.DMA((chunks,)),
            pltpu.SemaphoreType.DMA((chunks,)),
        ],
        (projected, taps_major, long_filter, skip_row, out_cotangent),
        outside=(0, 4),
    )
    far = shifted(far, "seq", 1)
    kve, pta, qta, inner, stats = on_chip(
        middle_kernel,
        [
            sds((chunks, 2, EDGE, LANES), BF16),
            sds((groups, 2 * members, block), BF16),
            sds((groups, members, block), BF16),
            sds((groups, width, block), F32),
            sds((2 * blocks, block), F32),
        ],
        [
            pltpu.VMEM((parts, HALO + EDGE, LANES), F32),
            pltpu.VMEM((2, 8 * blocks, block), F32),
        ],
        (near, x_all, taps_major, skt, kv, q0, pt, qt, ct, w),
    )

    dp_size = lax.axis_size("dp")
    stat_parts = [stats]
    bit = 1
    while bit < dp_size:
        current = merged(stat_parts)
        if bit * 4 <= dp_size:
            stat_parts = quartet(current, "dp", bit)
            bit *= 4
        else:
            stat_parts = [current + crossed(current, "dp", bit)]
            bit *= 2
    xf, kvf = on_chip(
        prep_kernel,
        [
            sds((chunks, blocks, parts, HALO + block, LANES), F32),
            sds((chunks, blocks, 2, block, LANES), F32),
        ],
        [],
        (near, x_all, kv, kve),
    )
    token_scale = 1.0 / math.sqrt(rows * lax.axis_size("seq"))
    out, pgr = on_chip(
        functools.partial(back_kernel, channels * dp_size, token_scale, taps, len(stat_parts)),
        [sds((24 + chunk_groups, channels), F32), sds((groups, members, block), F32)],
        [
            pltpu.VMEM((2, width, block), F32),
            pltpu.VMEM((groups, members, block), F32),
            pltpu.VMEM((groups, 8, block), F32),
            pltpu.VMEM((chunks, parts * taps, 8, LANES), F32),
            pltpu.VMEM((2, blocks, chunk_groups, members, block), F32),
            pltpu.VMEM((2, blocks, chunk_groups, members, block), F32),
            pltpu.VMEM((2, blocks, block, LANES), F32),
        ],
        (*stat_parts, skt, xf, kvf, pt, pta, qt, qta, ct, inner, w),
    )
    (out,) = on_chip(
        rim_kernel,
        [sds((24 + chunk_groups, channels), F32)],
        [pltpu.VMEM((parts, tail, LANES), F32)],
        (far, taps_major, pgr, out),
    )

    seq_size = lax.axis_size("seq")
    out_parts = [out + crossed(out, "seq", 1)]
    bit = 2
    while bit < seq_size:
        current = merged([part.astype(F32) for part in out_parts]).astype(BF16)
        if bit * 4 <= seq_size:
            out_parts = quartet(current, "seq", bit)
            bit *= 4
        else:
            out_parts = [current.astype(F32) + crossed(current, "seq", bit).astype(F32)]
            bit *= 2

    feat, filt, skip = on_chip(
        functools.partial(finish_kernel, len(out_parts)),
        [
            sds((parts, taps, channels), F32),
            sds((groups, block), F32),
            sds((1, channels), F32),
        ],
        [],
        out_parts,
        final=True,
    )
    return (jnp.transpose(feat, (1, 0, 2)), filt, skip.reshape(channels))


def solution(mesh):
    return jax.shard_map(
        body,
        mesh=mesh,
        in_specs=(
            P(None, "seq", "dp"),
            P(None, None, "dp"),
            P("dp", None),
            P("dp"),
            P("seq", "dp"),
        ),
        out_specs=(P(None, None, "dp"), P("dp", None), P("dp")),
        check_vma=False,
    )
```

```python
import functools
import math

import jax
import jax.numpy as jnp
from jax import lax
from jax.experimental import pallas as pl
from jax.experimental.pallas import tpu as pltpu
from jax.sharding import PartitionSpec as P


F32 = jnp.float32
BF16 = jnp.bfloat16
LANES = 128
HALO = 8
EDGE = 16


def matmul(a, b, contract):
    return lax.dot_general(
        a, b, ((contract[0], contract[1]), ((), ())), preferred_element_type=F32
    )


def featurize(buf, part, start, rows, taps_ref):
    taps = taps_ref.shape[1]
    total = None
    for tap in range(taps):
        weight = taps_ref[part, tap : tap + 1, :].astype(F32)
        term = weight * buf[part, start - tap : start - tap + rows, :]
        total = term if total is None else total + term
    return total.astype(BF16)


def lag_masks(block):
    row = lax.broadcasted_iota(jnp.int32, (block, block), 0)
    col = lax.broadcasted_iota(jnp.int32, (block, block), 1)
    return row, col


def edge_kernel(
    x_ref, taps_hbm, filt_hbm, cot_hbm, near_ref, taps_ref, filt_ref, cot_ref, far_ref, bufs, sems
):
    _, rows, channels = x_ref.shape
    tail = far_ref.shape[1]
    block = tail - HALO
    copies = [
        pltpu.make_async_copy(
            x_ref.at[1 + part, pl.ds(rows - tail, tail), :], far_ref.at[part], sems.at[part]
        )
        for part in range(2)
    ]
    copies.append(
        pltpu.make_async_copy(
            x_ref.at[0, pl.ds(rows - HALO, HALO), :], near_ref.at[pl.ds(block, HALO), :], sems.at[2]
        )
    )
    copies.append(pltpu.make_async_copy(taps_hbm, taps_ref, sems.at[3]))
    others = [
        pltpu.make_async_copy(filt_hbm, filt_ref, sems.at[4]),
        pltpu.make_async_copy(cot_hbm, cot_ref, sems.at[5]),
    ]
    for copy in copies + others:
        copy.start()
    for copy in copies:
        copy.wait()
    inside = lax.axis_index("seq") < lax.axis_size("seq") - 1
    near_ref[block : block + HALO, :] = jnp.where(inside, near_ref[block : block + HALO, :], 0)

    def product(chunk, buf):
        lane = pl.ds(pl.multiple_of(chunk * LANES, LANES), LANES)
        for part in range(2):
            buf[1 + part] = far_ref[part, :, lane].astype(F32)
            at = block + (1 + part) * HALO
            near_ref[at : at + HALO, lane] = jnp.where(inside, far_ref[part, tail - HALO :, lane], 0)
        k = featurize(buf, 1, HALO, block, taps_ref.at[:, :, lane])
        v = featurize(buf, 2, HALO, block, taps_ref.at[:, :, lane])
        both = (k.astype(F32) * v.astype(F32)).astype(BF16)
        near_ref[:block, lane] = jnp.where(inside, both, 0)

    at_once = math.gcd(channels // LANES, bufs.shape[0])

    @pl.loop(0, channels // LANES // at_once)
    def _(turn):
        for number in range(at_once):
            product(turn * at_once + number, bufs.at[number])

    for copy in others:
        copy.wait()


def front_kernel(
    x_ref, taps_ref, filt_ref, skip_ref, cot_ref,
    far_ref, skt_ref, kv_ref, q0_ref, pt_ref, qt_ref, ct_ref, w_ref,
    buf, mask,
):
    parts, rows, channels = x_ref.shape
    block = filt_ref.shape[1]
    members = channels // filt_ref.shape[0]
    groups = LANES // members
    blocks = rows // block
    tail = far_ref.shape[0] // 2
    buf[:, :HALO, :] = jnp.zeros((parts, HALO, LANES), F32)
    row, col = lag_masks(block)
    mask[...] = jnp.where(col >= row, 1.0, 0.0).astype(BF16)
    inside = lax.axis_index("seq") < lax.axis_size("seq") - 1

    def filters(chunk, within, filt):
        group = chunk * groups + within
        taps = jnp.broadcast_to(filt[within : within + 1], (block, block))
        circ = pltpu.roll(taps, 0, 1, stride=1, stride_axis=0).astype(BF16)
        near = circ * mask[...]
        w_ref[group, :block, :] = near
        w_ref[group, block:, :] = circ - near

    def features(chunk, number):
        lane = pl.ds(pl.multiple_of(chunk * LANES, LANES), LANES)
        group_at = pl.ds(pl.multiple_of(chunk * groups, groups), groups)
        span = slice(number * block, (number + 1) * block)
        start = HALO + number * block
        for part in range(parts):
            buf[part, start : start + block, :] = x_ref[part, span, lane].astype(F32)
        q, k, v = (featurize(buf, part, start, block, taps_ref.at[:, :, lane]) for part in range(3))
        kv_ref[chunk, 0, span, :] = k
        kv_ref[chunk, 1, span, :] = v
        if number == 0:
            q0_ref[:, lane] = q
        else:
            place = slice((number - 1) * members, number * members)
            product = (k.astype(F32) * v.astype(F32)).astype(BF16)
            pt_ref[group_at, place, :] = product.T.reshape(groups, members, block)
            qt_ref[group_at, place, :] = q.T.reshape(groups, members, block)
        place = slice(number * members, (number + 1) * members)
        ct_ref[group_at, place, :] = cot_ref[span, lane].T.reshape(groups, members, block)

    @pl.loop(0, channels // LANES)
    def _(chunk):
        lane = pl.ds(pl.multiple_of(chunk * LANES, LANES), LANES)
        group_at = pl.ds(pl.multiple_of(chunk * groups, groups), groups)
        filt = filt_ref[group_at, :].astype(F32)
        skt_ref[group_at] = skip_columns(skip_ref.at[:, lane], block).reshape(groups, members, block)
        braid(
            [functools.partial(features, chunk, number) for number in range(blocks)],
            [functools.partial(filters, chunk, within, filt) for within in range(groups)],
        )
        for part in range(2):
            ends = jnp.where(inside, x_ref[1 + part, rows - tail :, lane], 0)
            far_ref[part * tail : (part + 1) * tail, lane] = ends


def skip_columns(skip_ref, block):
    lanes = skip_ref.shape[1]
    return jnp.broadcast_to(skip_ref[...].astype(F32), (block, lanes)).T


def middle_kernel(
    near_ref, x_ref, taps_ref, skt_ref, kv_ref, q0_ref, pt_ref, qt_ref, ct_ref, w_ref,
    kve_ref, pta_ref, qta_ref, inner_ref, stats_ref,
    buf, acc,
):
    channels = near_ref.shape[1]
    block = q0_ref.shape[0]
    members = channels // w_ref.shape[0]
    groups = LANES // members
    width = ct_ref.shape[1]
    blocks = width // members
    chunks = channels // LANES
    acc[...] = jnp.zeros_like(acc)

    def heads(chunk):
        lane = pl.ds(pl.multiple_of(chunk * LANES, LANES), LANES)
        group_at = pl.ds(pl.multiple_of(chunk * groups, groups), groups)
        for part in range(3):
            at = block + part * HALO
            buf[part, :HALO, :] = near_ref[at : at + HALO, lane].astype(F32)
            buf[part, HALO:, :] = x_ref[part, :EDGE, lane].astype(F32)
        q_edge, k_edge, v_edge = (
            featurize(buf, part, HALO, EDGE, taps_ref.at[:, :, lane]) for part in range(3)
        )
        kve_ref[chunk, 0] = k_edge
        kve_ref[chunk, 1] = v_edge
        k0 = jnp.concatenate([k_edge, kv_ref[chunk, 0, EDGE:block, :]], axis=0)
        v0 = jnp.concatenate([v_edge, kv_ref[chunk, 1, EDGE:block, :]], axis=0)
        q0 = jnp.concatenate([q_edge, q0_ref[EDGE:, lane]], axis=0)
        p0 = (k0.astype(F32) * v0.astype(F32)).astype(BF16)
        pta_ref[group_at, :members, :] = near_ref[:block, lane].T.reshape(groups, members, block)
        pta_ref[group_at, members:, :] = p0.T.reshape(groups, members, block)
        qta_ref[group_at] = q0.T.reshape(groups, members, block)

    def filters(chunk):
        sums = [[None] * blocks, [None] * blocks]
        for within in range(groups):
            group = chunk * groups + within
            every = jnp.concatenate([pta_ref[group], pt_ref[group]], axis=0)
            now = every[members:]
            filtered = matmul(
                jnp.concatenate([now, every[:width]], axis=1), w_ref[group], ((1,), (0,))
            )
            own = jnp.concatenate([skt_ref[group]] * blocks, axis=0)
            inner = filtered + own * now.astype(F32)
            inner_ref[group] = inner
            q = jnp.concatenate([qta_ref[group], qt_ref[group]], axis=0).astype(F32)
            output = q * inner
            for which, value in enumerate((output * output, ct_ref[group].astype(F32) * output)):
                for number in range(blocks):
                    span = value[number * members : (number + 1) * members]
                    span = span.reshape(members // 8, 8, block).sum(axis=0)
                    sums[which][number] = span if within == 0 else sums[which][number] + span
        for which in range(2):
            for number in range(blocks):
                place = slice(number * 8, number * 8 + 8)
                acc[which, place, :] += sums[which][number]

    heads(0)

    @pl.loop(1, chunks)
    def _(chunk):
        filters(chunk - 1)
        heads(chunk)

    filters(chunks - 1)
    for which in range(2):
        for number in range(blocks):
            at = which * blocks + number
            stats_ref[at : at + 1, :] = jnp.sum(
                acc[which, number * 8 : number * 8 + 8, :], axis=0, keepdims=True
            )


def prep_kernel(near_ref, x_ref, kv_ref, kve_ref, xf_ref, kvf_ref):
    parts, rows, channels = x_ref.shape
    block = near_ref.shape[0] - parts * HALO
    blocks = rows // block

    @pl.loop(0, channels // LANES)
    def _(chunk):
        lane = pl.ds(pl.multiple_of(chunk * LANES, LANES), LANES)
        for part in range(parts):
            at = block + part * HALO
            xf_ref[chunk, 0, part, :HALO, :] = near_ref[at : at + HALO, lane].astype(F32)
            for number in range(blocks):
                at = number * block
                if number:
                    xf_ref[chunk, number, part, :HALO, :] = x_ref[part, at - HALO : at, lane].astype(F32)
                xf_ref[chunk, number, part, HALO:, :] = x_ref[part, at : at + block, lane].astype(F32)
        for part in range(2):
            kvf_ref[chunk, 0, part, :EDGE, :] = kve_ref[chunk, part].astype(F32)
            kvf_ref[chunk, 0, part, EDGE:, :] = kv_ref[chunk, part, EDGE:block, :].astype(F32)
            for number in range(1, blocks):
                at = number * block
                kvf_ref[chunk, number, part] = kv_ref[chunk, part, at : at + block, :].astype(F32)


def braid(one, two):
    done = 0
    for number, step in enumerate(one):
        step()
        upto = (number + 1) * len(two) // len(one)
        for other in two[done:upto]:
            other()
        done = upto
    for other in two[done:]:
        other()


def rim_kernel(far_ref, taps_ref, pgr_ref, out_ref, sum_ref, buf):
    members, block = pgr_ref.shape[1:]
    groups = LANES // members
    chunks = pgr_ref.shape[0] // groups
    taps = taps_ref.shape[1]
    tail = block + HALO
    sum_ref[:8, :] = out_ref[:8, :]
    sum_ref[24:, :] = out_ref[24:, :]

    @pl.loop(0, chunks)
    def _(chunk):
        lane = pl.ds(pl.multiple_of(chunk * LANES, LANES), LANES)
        for part in range(2):
            buf[1 + part] = far_ref[part * tail : (part + 1) * tail, lane].astype(F32)
        group_at = pl.ds(pl.multiple_of(chunk * groups, groups), groups)
        back = pgr_ref[group_at].reshape(LANES, block).T
        for part in (1, 2):
            other = featurize(buf, 3 - part, HALO, block, taps_ref.at[:, :, lane]).astype(F32)
            grads = back * other
            for tap in range(taps):
                at = part * 8 + tap
                term = grads * buf[part, HALO - tap : HALO - tap + block, :]
                sum_ref[at : at + 1, lane] = out_ref[at : at + 1, lane] + jnp.sum(term, axis=0, keepdims=True)
            sum_ref[part * 8 + taps : part * 8 + 8, lane] = out_ref[part * 8 + taps : part * 8 + 8, lane]


def back_kernel(channels_all, token_scale, taps, n_stats, *refs):
    stats_refs = refs[:n_stats]
    (skt_ref, xf_ref, kvf_ref, pt_ref, pta_ref, qt_ref, qta_ref, ct_ref, inner_ref, w_ref,
     out_ref, pgr_ref, coef, skip_acc, filt_acc, sums, *slots) = refs[n_stats:]
    chunks, blocks = xf_ref.shape[:2]
    parts = xf_ref.shape[2]
    width, block = ct_ref.shape[1:]
    members = width // blocks
    groups = LANES // members
    total = merged([ref[...] for ref in stats_refs])
    square = total[:blocks]
    cross = total[blocks : 2 * blocks] / channels_all
    rms = jnp.sqrt(square / channels_all + 1e-05)
    inv = token_scale / rms
    fall = token_scale * cross / (rms * rms * rms)
    for number in range(blocks):
        place = slice(number * members, (number + 1) * members)
        coef[0, place, :] = jnp.broadcast_to(inv[number : number + 1], (members, block))
        coef[1, place, :] = jnp.broadcast_to(fall[number : number + 1], (members, block))
    row, col = lag_masks(block)
    slots = (slots[:3], slots[3:])

    def group_part(chunk, slot, within):
        pg, qg, _ = slots[slot]
        group = chunk * groups + within
        every = jnp.concatenate([pta_ref[group], pt_ref[group]], axis=0)
        now = every[members:]
        q = jnp.concatenate([qta_ref[group], qt_ref[group]], axis=0).astype(F32)
        inner = inner_ref[group]
        output = q * inner
        out_grad = coef[0] * ct_ref[group].astype(F32) - coef[1] * output
        conv_grad = out_grad * q
        cot = conv_grad.astype(BF16)
        query_grad = out_grad * inner
        weighted = conv_grad * now.astype(F32)
        part_sum = weighted[:members]
        for number in range(1, blocks):
            part_sum = part_sum + weighted[number * members : (number + 1) * members]
        skip_acc[group] = part_sum
        gap = jnp.zeros((members, block), BF16)
        here = jnp.concatenate([gap, cot], axis=0)
        later = jnp.concatenate([cot, gap], axis=0)
        grad = matmul(
            jnp.concatenate([here, later], axis=1),
            jnp.concatenate([w_ref[group, :block, :], w_ref[group, block:, :]], axis=1),
            ((1,), (1,)),
        )
        own = skt_ref[group]
        pgr_ref[group] = grad[:members]
        for number in range(blocks):
            span = slice(number * members, (number + 1) * members)
            pg[number, within] = (
                grad[(number + 1) * members : (number + 2) * members] + own * conv_grad[span]
            )
            qg[number, within] = query_grad[span]
        both = matmul(cot, jnp.concatenate([now, every[:width]], axis=1), ((0,), (0,)))
        lagged = jnp.where(col <= row, both[:, :block], both[:, block:])
        skewed = lagged[:8]
        for start in range(8, block, 8):
            skewed = skewed + pltpu.roll(lagged[start : start + 8], block - start, 1)
        filt_acc[group] = skewed

    def turn(slot):
        pg, qg, gn = slots[slot]
        for number in range(blocks):
            gn[0, number] = qg[number].reshape(LANES, block).T
            gn[1, number] = pg[number].reshape(LANES, block).T

    def tap_steps(chunk, slot):
        gn = slots[slot][2]
        piece = 32
        totals = {}

        def step(part, number):
            for at in range(0, block, piece):
                if part:
                    grads = gn[1, number, at : at + piece, :]
                    grads = grads * kvf_ref[chunk, number, 2 - part, at : at + piece, :]
                else:
                    grads = gn[0, number, at : at + piece, :]
                for tap in range(taps):
                    start = HALO + at - tap
                    term = grads * xf_ref[chunk, number, part, start : start + piece, :]
                    term = term.reshape(piece // 8, 8, LANES).sum(axis=0)
                    totals[part, tap] = totals[part, tap] + term if (part, tap) in totals else term
            if number == blocks - 1:
                for tap in range(taps):
                    sums[chunk, part * taps + tap] = totals[part, tap]

        return [functools.partial(step, part, number) for part in range(parts) for number in range(blocks)]

    def group_steps(chunk, slot):
        return [functools.partial(group_part, chunk, slot, within) for within in range(groups)]

    def whole_step(chunk, slot):
        turn(1 - slot)
        braid(group_steps(chunk, slot), tap_steps(chunk - 2, slot))

    braid(group_steps(0, 0), [])
    if chunks > 1:
        braid(group_steps(1, 1), [])
        turn(0)

        @pl.loop(1, chunks // 2)
        def _(pair):
            whole_step(2 * pair, 0)
            whole_step(2 * pair + 1, 1)

        if chunks % 2:
            whole_step(chunks - 1, 0)
        turn((chunks - 1) % 2)
        braid([], tap_steps(chunks - 2, chunks % 2))
    else:
        turn(0)
    braid([], tap_steps(chunks - 1, (chunks - 1) % 2))

    flip = jnp.where(((row + col) % block) == 0, 1.0, 0.0).astype(F32)
    lags = filt_acc[:, 0, :]
    for at in range(1, 8):
        lags = lags + pltpu.roll(filt_acc[:, at, :], block - at, 1)
    lags = lax.dot_general(
        lags, flip, (((1,), (0,)), ((), ())), preferred_element_type=F32, precision=lax.Precision.HIGHEST
    )
    for chunk in range(chunks):
        lane = slice(chunk * LANES, (chunk + 1) * LANES)
        group_at = slice(chunk * groups, (chunk + 1) * groups)
        out_ref[3 * 8 :, lane] = lags[group_at]
        skip_row = jnp.sum(skip_acc[group_at].reshape(LANES, block).T, axis=0, keepdims=True)
        for part in range(parts):
            for tap in range(taps):
                out_ref[part * 8 + tap : part * 8 + tap + 1, lane] = jnp.sum(
                    sums[chunk, part * taps + tap], axis=0, keepdims=True
                )
            out_ref[part * 8 + taps : part * 8 + 8, lane] = skip_row


def finish_kernel(n_in, *refs):
    ins = refs[:n_in]
    feat_ref, filt_ref, skip_ref = refs[n_in:]
    total = merged([ref[...].astype(F32) for ref in ins])
    taps = feat_ref.shape[1]
    for part in range(feat_ref.shape[0]):
        feat_ref[part] = total[part * 8 : part * 8 + taps]
    skip_ref[...] = total[taps : taps + 1]
    groups = total.shape[0] - 24
    for chunk in range(total.shape[1] // LANES):
        filt_ref[chunk * groups : (chunk + 1) * groups, :] = total[24:, chunk * LANES : (chunk + 1) * LANES]


def ring(array, axis):
    length = lax.axis_size(axis)
    return lax.ppermute(array, axis, [(i, (i + 1) % length) for i in range(length)])


def crossed(array, axis, bit):
    length = lax.axis_size(axis)
    return lax.ppermute(array, axis, [(i, i ^ bit) for i in range(length)])


def quartet(array, axis, bit):
    return [array] + [crossed(array, axis, bit * k) for k in (1, 2, 3)]


def merged(parts):
    if len(parts) == 1:
        return parts[0]
    return (parts[0] + parts[1]) + (parts[2] + parts[3])


def on_chip(kernel, out_shape, scratch, args, outside=(), final=False):
    place = pl.BlockSpec(memory_space=pltpu.VMEM)
    apart = pl.BlockSpec(memory_space=pl.ANY)
    if not final:
        out_shape = [pltpu.VMEM(out.shape, out.dtype) for out in out_shape]
    args = [
        pltpu.with_memory_space_constraint(arg, pltpu.HBM if number in outside else pltpu.VMEM)
        for number, arg in enumerate(args)
    ]
    return pl.pallas_call(
        kernel,
        in_specs=[apart if number in outside else place for number in range(len(args))],
        out_specs=[place] * len(out_shape),
        out_shape=out_shape,
        scratch_shapes=scratch,
        compiler_params=pltpu.CompilerParams(vmem_limit_bytes=16 * 1024 * 1024),
    )(*args)


def body(projected, featurizer, long_filter, skip_gain, out_cotangent):
    parts, rows, channels = projected.shape
    groups, block = long_filter.shape
    taps = featurizer.shape[0]
    members = channels // groups
    chunk_groups = LANES // members
    blocks = rows // block
    width = blocks * members
    tail = block + HALO
    taps_major = jnp.transpose(featurizer, (1, 0, 2))
    skip_row = skip_gain.reshape(1, channels)

    sds = jax.ShapeDtypeStruct
    chunks = channels // LANES

    near, taps_major, filters, cots = on_chip(
        edge_kernel,
        [
            sds((block + parts * HALO, channels), BF16),
            sds((parts, taps, channels), BF16),
            sds((groups, block), BF16),
            sds((rows, channels), BF16),
        ],
        [
            pltpu.VMEM((2, tail, channels), BF16),
            pltpu.VMEM((2, parts, tail, LANES), F32),
            pltpu.SemaphoreType.DMA((6,)),
        ],
        (projected, taps_major, long_filter, out_cotangent),
        outside=(0, 1, 2, 3),
    )
    near = ring(near, "seq")

    far, skt, kv, q0, pt, qt, ct, w = on_chip(
        front_kernel,
        [
            sds((2 * tail, channels), BF16),
            sds((groups, members, block), F32),
            sds((chunks, 2, rows, LANES), BF16),
            sds((block, channels), BF16),
            sds((groups, width - members, block), BF16),
            sds((groups, width - members, block), BF16),
            sds((groups, width, block), BF16),
            sds((groups, 2 * block, block), BF16),
        ],
        [
            pltpu.VMEM((parts, HALO + rows, LANES), F32),
            pltpu.VMEM((block, block), BF16),
        ],
        (projected, taps_major, filters, skip_row, cots),
    )
    far = ring(far, "seq")
    kve, pta, qta, inner, stats = on_chip(
        middle_kernel,
        [
            sds((chunks, 2, EDGE, LANES), BF16),
            sds((groups, 2 * members, block), BF16),
            sds((groups, members, block), BF16),
            sds((groups, width, block), F32),
            sds((2 * blocks, block), F32),
        ],
        [
            pltpu.VMEM((parts, HALO + EDGE, LANES), F32),
            pltpu.VMEM((2, 8 * blocks, block), F32),
        ],
        (near, projected, taps_major, skt, kv, q0, pt, qt, ct, w),
    )

    dp_size = lax.axis_size("dp")
    stat_parts = [stats]
    bit = 1
    while bit < dp_size:
        current = merged(stat_parts)
        if bit * 4 <= dp_size:
            stat_parts = quartet(current, "dp", bit)
            bit *= 4
        else:
            stat_parts = [current + crossed(current, "dp", bit)]
            bit *= 2
    xf, kvf = on_chip(
        prep_kernel,
        [
            sds((chunks, blocks, parts, HALO + block, LANES), F32),
            sds((chunks, blocks, 2, block, LANES), F32),
        ],
        [],
        (near, projected, kv, kve),
    )
    token_scale = 1.0 / math.sqrt(rows * lax.axis_size("seq"))
    out, pgr = on_chip(
        functools.partial(back_kernel, channels * dp_size, token_scale, taps, len(stat_parts)),
        [sds((24 + chunk_groups, channels), F32), sds((groups, members, block), F32)],
        [
            pltpu.VMEM((2, width, block), F32),
            pltpu.VMEM((groups, members, block), F32),
            pltpu.VMEM((groups, 8, block), F32),
            pltpu.VMEM((chunks, parts * taps, 8, LANES), F32),
        ]
        + [
            pltpu.VMEM((blocks, chunk_groups, members, block), F32),
            pltpu.VMEM((blocks, chunk_groups, members, block), F32),
            pltpu.VMEM((2, blocks, block, LANES), F32),
        ]
        * 2,
        (*stat_parts, skt, xf, kvf, pt, pta, qt, qta, ct, inner, w),
    )
    (out,) = on_chip(
        rim_kernel,
        [sds((24 + chunk_groups, channels), F32)],
        [pltpu.VMEM((parts, tail, LANES), F32)],
        (far, taps_major, pgr, out),
    )

    seq_size = lax.axis_size("seq")
    out_parts = [out + crossed(out, "seq", 1)]
    bit = 2
    while bit < seq_size:
        current = merged([part.astype(F32) for part in out_parts]).astype(BF16)
        if bit * 4 <= seq_size:
            out_parts = quartet(current, "seq", bit)
            bit *= 4
        else:
            out_parts = [current.astype(F32) + crossed(current, "seq", bit).astype(F32)]
            bit *= 2

    feat, filt, skip = on_chip(
        functools.partial(finish_kernel, len(out_parts)),
        [
            sds((parts, taps, channels), F32),
            sds((groups, block), F32),
            sds((1, channels), F32),
        ],
        [],
        out_parts,
        final=True,
    )
    return (jnp.transpose(feat, (1, 0, 2)), filt, skip.reshape(channels))


def solution(mesh):
    return jax.shard_map(
        body,
        mesh=mesh,
        in_specs=(
            P(None, "seq", "dp"),
            P(None, None, "dp"),
            P("dp", None),
            P("dp"),
            P("seq", "dp"),
        ),
        out_specs=(P(None, None, "dp"), P("dp", None), P("dp")),
        check_vma=False,
    )
```

```python
import functools
import math

import jax
import jax.numpy as jnp
from jax import lax
from jax.experimental import pallas as pl
from jax.experimental.pallas import tpu as pltpu
from jax.sharding import PartitionSpec as P


F32 = jnp.float32
BF16 = jnp.bfloat16
LANES = 128
HALO = 8
EDGE = 16


def matmul(a, b, contract):
    return lax.dot_general(
        a, b, ((contract[0], contract[1]), ((), ())), preferred_element_type=F32
    )


def featurize(buf, part, start, rows, taps_ref):
    taps = taps_ref.shape[1]
    total = None
    for tap in range(taps):
        weight = taps_ref[part, tap : tap + 1, :].astype(F32)
        term = weight * buf[part, start - tap : start - tap + rows, :]
        total = term if total is None else total + term
    return total.astype(BF16)


def lag_masks(block):
    row = lax.broadcasted_iota(jnp.int32, (block, block), 0)
    col = lax.broadcasted_iota(jnp.int32, (block, block), 1)
    return row, col


def edge_kernel(
    x_ref, taps_hbm, filt_hbm, cot_hbm, near_ref, taps_ref, filt_ref, cot_ref, far_ref, bufs, sems
):
    _, rows, channels = x_ref.shape
    tail = far_ref.shape[1]
    block = tail - HALO
    copies = [
        pltpu.make_async_copy(
            x_ref.at[1 + part, pl.ds(rows - tail, tail), :], far_ref.at[part], sems.at[part]
        )
        for part in range(2)
    ]
    copies.append(
        pltpu.make_async_copy(
            x_ref.at[0, pl.ds(rows - HALO, HALO), :], near_ref.at[pl.ds(block, HALO), :], sems.at[2]
        )
    )
    copies.append(pltpu.make_async_copy(taps_hbm, taps_ref, sems.at[3]))
    others = [
        pltpu.make_async_copy(filt_hbm, filt_ref, sems.at[4]),
        pltpu.make_async_copy(cot_hbm, cot_ref, sems.at[5]),
    ]
    for copy in copies + others:
        copy.start()
    for copy in copies:
        copy.wait()
    inside = lax.axis_index("seq") < lax.axis_size("seq") - 1
    near_ref[block : block + HALO, :] = jnp.where(inside, near_ref[block : block + HALO, :], 0)

    def product(chunk, buf):
        lane = pl.ds(pl.multiple_of(chunk * LANES, LANES), LANES)
        for part in range(2):
            buf[1 + part] = far_ref[part, :, lane].astype(F32)
            at = block + (1 + part) * HALO
            near_ref[at : at + HALO, lane] = jnp.where(inside, far_ref[part, tail - HALO :, lane], 0)
        k = featurize(buf, 1, HALO, block, taps_ref.at[:, :, lane])
        v = featurize(buf, 2, HALO, block, taps_ref.at[:, :, lane])
        near_ref[:block, lane] = jnp.where(inside, k * v, 0)

    at_once = math.gcd(channels // LANES, bufs.shape[0])

    @pl.loop(0, channels // LANES // at_once)
    def _(turn):
        for number in range(at_once):
            product(turn * at_once + number, bufs.at[number])

    for copy in others:
        copy.wait()


def front_kernel(
    x_ref, taps_ref, filt_ref, skip_ref, cot_ref,
    far_ref, skt_ref, kv_ref, q0_ref, pt_ref, qt_ref, ct_ref, w_ref,
    buf, mask,
):
    parts, rows, channels = x_ref.shape
    block = filt_ref.shape[1]
    members = channels // filt_ref.shape[0]
    groups = LANES // members
    blocks = rows // block
    tail = far_ref.shape[0] // 2
    buf[:, :HALO, :] = jnp.zeros((parts, HALO, LANES), F32)
    row, col = lag_masks(block)
    mask[...] = jnp.where(col >= row, 1.0, 0.0).astype(BF16)
    inside = lax.axis_index("seq") < lax.axis_size("seq") - 1

    def filters(chunk, within, filt):
        group = chunk * groups + within
        taps = jnp.broadcast_to(filt[within : within + 1], (block, block))
        circ = pltpu.roll(taps, 0, 1, stride=1, stride_axis=0).astype(BF16)
        near = circ * mask[...]
        w_ref[group, :block, :] = near
        w_ref[group, block:, :] = circ - near

    def features(chunk, number):
        lane = pl.ds(pl.multiple_of(chunk * LANES, LANES), LANES)
        group_at = pl.ds(pl.multiple_of(chunk * groups, groups), groups)
        span = slice(number * block, (number + 1) * block)
        start = HALO + number * block
        for part in range(parts):
            buf[part, start : start + block, :] = x_ref[part, span, lane].astype(F32)
        q, k, v = (featurize(buf, part, start, block, taps_ref.at[:, :, lane]) for part in range(3))
        kv_ref[chunk, 0, span, :] = k
        kv_ref[chunk, 1, span, :] = v
        if number == 0:
            q0_ref[:, lane] = q
        else:
            place = slice((number - 1) * members, number * members)
            product = k * v
            pt_ref[group_at, place, :] = product.T.reshape(groups, members, block)
            qt_ref[group_at, place, :] = q.T.reshape(groups, members, block)
        place = slice(number * members, (number + 1) * members)
        ct_ref[group_at, place, :] = cot_ref[span, lane].T.reshape(groups, members, block)

    @pl.loop(0, channels // LANES)
    def _(chunk):
        lane = pl.ds(pl.multiple_of(chunk * LANES, LANES), LANES)
        group_at = pl.ds(pl.multiple_of(chunk * groups, groups), groups)
        filt = filt_ref[group_at, :].astype(F32)
        skt_ref[group_at] = skip_columns(skip_ref.at[:, lane], block).reshape(groups, members, block)
        braid(
            [functools.partial(features, chunk, number) for number in range(blocks)],
            [functools.partial(filters, chunk, within, filt) for within in range(groups)],
        )
        for part in range(2):
            ends = jnp.where(inside, x_ref[1 + part, rows - tail :, lane], 0)
            far_ref[part * tail : (part + 1) * tail, lane] = ends


def skip_columns(skip_ref, block):
    lanes = skip_ref.shape[1]
    return jnp.broadcast_to(skip_ref[...].astype(F32), (block, lanes)).T


def middle_kernel(
    near_ref, x_ref, taps_ref, skt_ref, kv_ref, q0_ref, pt_ref, qt_ref, ct_ref, w_ref,
    kve_ref, pta_ref, qta_ref, inner_ref, stats_ref,
    buf, acc,
):
    channels = near_ref.shape[1]
    block = q0_ref.shape[0]
    members = channels // w_ref.shape[0]
    groups = LANES // members
    width = ct_ref.shape[1]
    blocks = width // members
    chunks = channels // LANES
    acc[...] = jnp.zeros_like(acc)

    def heads(chunk):
        lane = pl.ds(pl.multiple_of(chunk * LANES, LANES), LANES)
        group_at = pl.ds(pl.multiple_of(chunk * groups, groups), groups)
        for part in range(3):
            at = block + part * HALO
            buf[part, :HALO, :] = near_ref[at : at + HALO, lane].astype(F32)
            buf[part, HALO:, :] = x_ref[part, :EDGE, lane].astype(F32)
        q_edge, k_edge, v_edge = (
            featurize(buf, part, HALO, EDGE, taps_ref.at[:, :, lane]) for part in range(3)
        )
        kve_ref[chunk, 0] = k_edge
        kve_ref[chunk, 1] = v_edge
        k0 = jnp.concatenate([k_edge, kv_ref[chunk, 0, EDGE:block, :]], axis=0)
        v0 = jnp.concatenate([v_edge, kv_ref[chunk, 1, EDGE:block, :]], axis=0)
        q0 = jnp.concatenate([q_edge, q0_ref[EDGE:, lane]], axis=0)
        p0 = k0 * v0
        pta_ref[group_at, :members, :] = near_ref[:block, lane].T.reshape(groups, members, block)
        pta_ref[group_at, members:, :] = p0.T.reshape(groups, members, block)
        qta_ref[group_at] = q0.T.reshape(groups, members, block)

    def filters(chunk):
        sums = [[None] * blocks, [None] * blocks]
        for within in range(groups):
            group = chunk * groups + within
            every = jnp.concatenate([pta_ref[group], pt_ref[group]], axis=0)
            now = every[members:]
            filtered = matmul(
                jnp.concatenate([now, every[:width]], axis=1), w_ref[group], ((1,), (0,))
            )
            own = jnp.concatenate([skt_ref[group]] * blocks, axis=0)
            inner = filtered + own * now.astype(F32)
            inner_ref[group] = inner
            q = jnp.concatenate([qta_ref[group], qt_ref[group]], axis=0).astype(F32)
            output = q * inner
            for which, value in enumerate((output * output, ct_ref[group].astype(F32) * output)):
                for number in range(blocks):
                    span = value[number * members : (number + 1) * members]
                    span = span.reshape(members // 8, 8, block).sum(axis=0)
                    sums[which][number] = span if within == 0 else sums[which][number] + span
        for which in range(2):
            for number in range(blocks):
                place = slice(number * 8, number * 8 + 8)
                acc[which, place, :] += sums[which][number]

    heads(0)

    @pl.loop(1, chunks)
    def _(chunk):
        filters(chunk - 1)
        heads(chunk)

    filters(chunks - 1)
    for which in range(2):
        for number in range(blocks):
            at = which * blocks + number
            stats_ref[at : at + 1, :] = jnp.sum(
                acc[which, number * 8 : number * 8 + 8, :], axis=0, keepdims=True
            )


def prep_kernel(near_ref, x_ref, kv_ref, kve_ref, xf_ref, kvf_ref, xq_ref, buf):
    parts, rows, channels = x_ref.shape
    block = near_ref.shape[0] - parts * HALO
    blocks = rows // block

    @pl.loop(0, channels // LANES)
    def _(chunk):
        lane = pl.ds(pl.multiple_of(chunk * LANES, LANES), LANES)
        buf[:HALO, :] = near_ref[block : block + HALO, lane].astype(F32)
        buf[HALO:, :] = x_ref[0, :, lane].astype(F32)
        for tap in range(xq_ref.shape[1]):
            xq_ref[chunk, tap] = buf[HALO - tap : HALO - tap + rows, :].astype(BF16)
        for part in range(1, parts):
            at = block + part * HALO
            xf_ref[chunk, 0, part - 1, :HALO, :] = near_ref[at : at + HALO, lane].astype(F32)
            for number in range(blocks):
                at = number * block
                if number:
                    xf_ref[chunk, number, part - 1, :HALO, :] = x_ref[part, at - HALO : at, lane].astype(F32)
                xf_ref[chunk, number, part - 1, HALO:, :] = x_ref[part, at : at + block, lane].astype(F32)
        for part in range(2):
            kvf_ref[chunk, 0, part, :EDGE, :] = kve_ref[chunk, part].astype(F32)
            kvf_ref[chunk, 0, part, EDGE:, :] = kv_ref[chunk, part, EDGE:block, :].astype(F32)
            for number in range(1, blocks):
                at = number * block
                kvf_ref[chunk, number, part] = kv_ref[chunk, part, at : at + block, :].astype(F32)


def braid(one, two):
    done = 0
    for number, step in enumerate(one):
        step()
        upto = (number + 1) * len(two) // len(one)
        for other in two[done:upto]:
            other()
        done = upto
    for other in two[done:]:
        other()


def rim_kernel(far_ref, taps_ref, pgr_ref, out_ref, sum_ref, buf):
    members, block = pgr_ref.shape[1:]
    groups = LANES // members
    chunks = pgr_ref.shape[0] // groups
    taps = taps_ref.shape[1]
    tail = block + HALO
    sum_ref[:8, :] = out_ref[:8, :]
    sum_ref[24:, :] = out_ref[24:, :]

    @pl.loop(0, chunks)
    def _(chunk):
        lane = pl.ds(pl.multiple_of(chunk * LANES, LANES), LANES)
        for part in range(2):
            buf[1 + part] = far_ref[part * tail : (part + 1) * tail, lane].astype(F32)
        group_at = pl.ds(pl.multiple_of(chunk * groups, groups), groups)
        back = pgr_ref[group_at].reshape(LANES, block).T
        for part in (1, 2):
            other = featurize(buf, 3 - part, HALO, block, taps_ref.at[:, :, lane]).astype(F32)
            grads = back * other
            for tap in range(taps):
                at = part * 8 + tap
                term = grads * buf[part, HALO - tap : HALO - tap + block, :]
                sum_ref[at : at + 1, lane] = out_ref[at : at + 1, lane] + jnp.sum(term, axis=0, keepdims=True)
            sum_ref[part * 8 + taps : part * 8 + 8, lane] = out_ref[part * 8 + taps : part * 8 + 8, lane]


def back_kernel(channels_all, token_scale, taps, n_stats, *refs):
    stats_refs = refs[:n_stats]
    (skt_ref, xf_ref, kvf_ref, xq_ref, pt_ref, pta_ref, qt_ref, qta_ref, ct_ref, inner_ref, w_ref,
     out_ref, pgr_ref, coef, skip_acc, filt_acc, sums, eye, *slots) = refs[n_stats:]
    chunks, blocks = xf_ref.shape[:2]
    parts = 1 + xf_ref.shape[2]
    width, block = ct_ref.shape[1:]
    members = width // blocks
    groups = LANES // members
    total = merged([ref[...] for ref in stats_refs])
    square = total[:blocks]
    cross = total[blocks : 2 * blocks] / channels_all
    rms = jnp.sqrt(square / channels_all + 1e-05)
    inv = token_scale / rms
    fall = token_scale * cross / (rms * rms * rms)
    for number in range(blocks):
        place = slice(number * members, (number + 1) * members)
        coef[0, place, :] = jnp.broadcast_to(inv[number : number + 1], (members, block))
        coef[1, place, :] = jnp.broadcast_to(fall[number : number + 1], (members, block))
    row, col = lag_masks(block)
    slots = (slots[:3], slots[3:])
    eye[...] = jnp.where(row == col, 1.0, 0.0)

    def group_part(chunk, slot, within):
        pg, qg, _ = slots[slot]
        group = chunk * groups + within
        every = jnp.concatenate([pta_ref[group], pt_ref[group]], axis=0)
        now = every[members:]
        q = jnp.concatenate([qta_ref[group], qt_ref[group]], axis=0).astype(F32)
        inner = inner_ref[group]
        output = q * inner
        out_grad = coef[0] * ct_ref[group].astype(F32) - coef[1] * output
        conv_grad = out_grad * q
        cot = conv_grad.astype(BF16)
        query_grad = out_grad * inner
        weighted = conv_grad * now.astype(F32)
        part_sum = weighted[:members]
        for number in range(1, blocks):
            part_sum = part_sum + weighted[number * members : (number + 1) * members]
        skip_acc[group] = part_sum
        gap = jnp.zeros((members, block), BF16)
        here = jnp.concatenate([gap, cot], axis=0)
        later = jnp.concatenate([cot, gap], axis=0)
        grad = matmul(
            jnp.concatenate([here, later], axis=1),
            jnp.concatenate([w_ref[group, :block, :], w_ref[group, block:, :]], axis=1),
            ((1,), (1,)),
        )
        own = skt_ref[group]
        pgr_ref[group] = grad[:members]
        for number in range(blocks):
            span = slice(number * members, (number + 1) * members)
            pg[number, within] = (
                grad[(number + 1) * members : (number + 2) * members] + own * conv_grad[span]
            )
            qg[number, within] = query_grad[span].astype(BF16)
        both = matmul(cot, jnp.concatenate([now, every[:width]], axis=1), ((0,), (0,)))
        lagged = jnp.where(col <= row, both[:, :block], both[:, block:])
        skewed = lagged[:8]
        for start in range(8, block, 8):
            skewed = skewed + pltpu.roll(lagged[start : start + 8], block - start, 1)
        filt_acc[group] = skewed

    def turn(slot):
        pg, _, gn = slots[slot]
        for number in range(blocks):
            gn[number] = pg[number].reshape(LANES, block).T

    def query_steps(chunk, slot):
        qg = slots[slot][1]

        def step(first):
            grads = jnp.concatenate([qg[number].reshape(LANES, block) for number in range(blocks)], axis=1)
            some = range(first, min(first + 2, taps))
            every = matmul(
                grads, jnp.concatenate([xq_ref[chunk, tap] for tap in some], axis=1), ((1,), (0,))
            )
            for place, tap in enumerate(some):
                own = every[:, place * LANES : (place + 1) * LANES] * eye[...]
                sums[chunk, tap] = own.reshape(LANES // 8, 8, LANES).sum(axis=0)

        return [functools.partial(step, first) for first in range(0, taps, 2)]

    def tap_steps(chunk, slot):
        gn = slots[slot][2]
        piece = 32
        totals = {}

        def step(part, number):
            for at in range(0, block, piece):
                grads = gn[number, at : at + piece, :]
                grads = grads * kvf_ref[chunk, number, 2 - part, at : at + piece, :]
                for tap in range(taps):
                    start = HALO + at - tap
                    term = grads * xf_ref[chunk, number, part - 1, start : start + piece, :]
                    term = term.reshape(piece // 8, 8, LANES).sum(axis=0)
                    totals[part, tap] = totals[part, tap] + term if (part, tap) in totals else term
            if number == blocks - 1:
                for tap in range(taps):
                    sums[chunk, part * taps + tap] = totals[part, tap]

        return [functools.partial(step, part, number) for part in range(1, parts) for number in range(blocks)]

    def group_steps(chunk, slot):
        return [functools.partial(group_part, chunk, slot, within) for within in range(groups)]

    def whole_step(chunk, slot):
        turn(1 - slot)
        braid(group_steps(chunk, slot), tap_steps(chunk - 2, slot) + query_steps(chunk - 1, 1 - slot))

    braid(group_steps(0, 0), [])
    if chunks > 1:
        braid(group_steps(1, 1), query_steps(0, 0))
        turn(0)

        @pl.loop(1, chunks // 2)
        def _(pair):
            whole_step(2 * pair, 0)
            whole_step(2 * pair + 1, 1)

        if chunks % 2:
            whole_step(chunks - 1, 0)
        turn((chunks - 1) % 2)
        braid([], tap_steps(chunks - 2, chunks % 2))
    else:
        turn(0)
    last = (chunks - 1) % 2
    braid(query_steps(chunks - 1, last), tap_steps(chunks - 1, last))

    flip = jnp.where(((row + col) % block) == 0, 1.0, 0.0).astype(F32)
    lags = filt_acc[:, 0, :]
    for at in range(1, 8):
        lags = lags + pltpu.roll(filt_acc[:, at, :], block - at, 1)
    lags = lax.dot_general(
        lags, flip, (((1,), (0,)), ((), ())), preferred_element_type=F32, precision=lax.Precision.HIGHEST
    )
    for chunk in range(chunks):
        lane = slice(chunk * LANES, (chunk + 1) * LANES)
        group_at = slice(chunk * groups, (chunk + 1) * groups)
        out_ref[3 * 8 :, lane] = lags[group_at]
        skip_row = jnp.sum(skip_acc[group_at].reshape(LANES, block).T, axis=0, keepdims=True)
        for part in range(parts):
            for tap in range(taps):
                out_ref[part * 8 + tap : part * 8 + tap + 1, lane] = jnp.sum(
                    sums[chunk, part * taps + tap], axis=0, keepdims=True
                )
            out_ref[part * 8 + taps : part * 8 + 8, lane] = skip_row


def finish_kernel(n_in, *refs):
    ins = refs[:n_in]
    feat_ref, filt_ref, skip_ref = refs[n_in:]
    total = merged([ref[...].astype(F32) for ref in ins])
    taps = feat_ref.shape[1]
    for part in range(feat_ref.shape[0]):
        feat_ref[part] = total[part * 8 : part * 8 + taps]
    skip_ref[...] = total[taps : taps + 1]
    groups = total.shape[0] - 24
    for chunk in range(total.shape[1] // LANES):
        filt_ref[chunk * groups : (chunk + 1) * groups, :] = total[24:, chunk * LANES : (chunk + 1) * LANES]


def ring(array, axis):
    length = lax.axis_size(axis)
    return lax.ppermute(array, axis, [(i, (i + 1) % length) for i in range(length)])


def crossed(array, axis, bit):
    length = lax.axis_size(axis)
    return lax.ppermute(array, axis, [(i, i ^ bit) for i in range(length)])


def quartet(array, axis, bit):
    return [array] + [crossed(array, axis, bit * k) for k in (1, 2, 3)]


def merged(parts):
    if len(parts) == 1:
        return parts[0]
    return (parts[0] + parts[1]) + (parts[2] + parts[3])


def on_chip(kernel, out_shape, scratch, args, outside=(), final=False):
    place = pl.BlockSpec(memory_space=pltpu.VMEM)
    apart = pl.BlockSpec(memory_space=pl.ANY)
    if not final:
        out_shape = [pltpu.VMEM(out.shape, out.dtype) for out in out_shape]
    args = [
        pltpu.with_memory_space_constraint(arg, pltpu.HBM if number in outside else pltpu.VMEM)
        for number, arg in enumerate(args)
    ]
    return pl.pallas_call(
        kernel,
        in_specs=[apart if number in outside else place for number in range(len(args))],
        out_specs=[place] * len(out_shape),
        out_shape=out_shape,
        scratch_shapes=scratch,
        compiler_params=pltpu.CompilerParams(vmem_limit_bytes=16 * 1024 * 1024),
    )(*args)


def body(projected, featurizer, long_filter, skip_gain, out_cotangent):
    parts, rows, channels = projected.shape
    groups, block = long_filter.shape
    taps = featurizer.shape[0]
    members = channels // groups
    chunk_groups = LANES // members
    blocks = rows // block
    width = blocks * members
    tail = block + HALO
    taps_major = jnp.transpose(featurizer, (1, 0, 2))
    skip_row = skip_gain.reshape(1, channels)

    sds = jax.ShapeDtypeStruct
    chunks = channels // LANES

    near, taps_major, filters, cots = on_chip(
        edge_kernel,
        [
            sds((block + parts * HALO, channels), BF16),
            sds((parts, taps, channels), BF16),
            sds((groups, block), BF16),
            sds((rows, channels), BF16),
        ],
        [
            pltpu.VMEM((2, tail, channels), BF16),
            pltpu.VMEM((4, parts, tail, LANES), F32),
            pltpu.SemaphoreType.DMA((6,)),
        ],
        (projected, taps_major, long_filter, out_cotangent),
        outside=(0, 1, 2, 3),
    )
    near = ring(near, "seq")

    far, skt, kv, q0, pt, qt, ct, w = on_chip(
        front_kernel,
        [
            sds((2 * tail, channels), BF16),
            sds((groups, members, block), F32),
            sds((chunks, 2, rows, LANES), BF16),
            sds((block, channels), BF16),
            sds((groups, width - members, block), BF16),
            sds((groups, width - members, block), BF16),
            sds((groups, width, block), BF16),
            sds((groups, 2 * block, block), BF16),
        ],
        [
            pltpu.VMEM((parts, HALO + rows, LANES), F32),
            pltpu.VMEM((block, block), BF16),
        ],
        (projected, taps_major, filters, skip_row, cots),
    )
    far = ring(far, "seq")
    kve, pta, qta, inner, stats = on_chip(
        middle_kernel,
        [
            sds((chunks, 2, EDGE, LANES), BF16),
            sds((groups, 2 * members, block), BF16),
            sds((groups, members, block), BF16),
            sds((groups, width, block), F32),
            sds((2 * blocks, block), F32),
        ],
        [
            pltpu.VMEM((parts, HALO + EDGE, LANES), F32),
            pltpu.VMEM((2, 8 * blocks, block), F32),
        ],
        (near, projected, taps_major, skt, kv, q0, pt, qt, ct, w),
    )

    dp_size = lax.axis_size("dp")
    stat_parts = [stats]
    bit = 1
    while bit < dp_size:
        current = merged(stat_parts)
        if bit * 4 <= dp_size:
            stat_parts = quartet(current, "dp", bit)
            bit *= 4
        else:
            stat_parts = [current + crossed(current, "dp", bit)]
            bit *= 2
    xf, kvf, xq = on_chip(
        prep_kernel,
        [
            sds((chunks, blocks, 2, HALO + block, LANES), F32),
            sds((chunks, blocks, 2, block, LANES), F32),
            sds((chunks, taps, rows, LANES), BF16),
        ],
        [pltpu.VMEM((HALO + rows, LANES), F32)],
        (near, projected, kv, kve),
    )
    token_scale = 1.0 / math.sqrt(rows * lax.axis_size("seq"))
    out, pgr = on_chip(
        functools.partial(back_kernel, channels * dp_size, token_scale, taps, len(stat_parts)),
        [sds((24 + chunk_groups, channels), F32), sds((groups, members, block), F32)],
        [
            pltpu.VMEM((2, width, block), F32),
            pltpu.VMEM((groups, members, block), F32),
            pltpu.VMEM((groups, 8, block), F32),
            pltpu.VMEM((chunks, parts * taps, 8, LANES), F32),
            pltpu.VMEM((LANES, LANES), F32),
        ]
        + [
            pltpu.VMEM((blocks, chunk_groups, members, block), F32),
            pltpu.VMEM((blocks, chunk_groups, members, block), BF16),
            pltpu.VMEM((blocks, block, LANES), F32),
        ]
        * 2,
        (*stat_parts, skt, xf, kvf, xq, pt, pta, qt, qta, ct, inner, w),
    )
    (out,) = on_chip(
        rim_kernel,
        [sds((24 + chunk_groups, channels), F32)],
        [pltpu.VMEM((parts, tail, LANES), F32)],
        (far, taps_major, pgr, out),
    )

    seq_size = lax.axis_size("seq")
    out_parts = [out + crossed(out, "seq", 1)]
    bit = 2
    while bit < seq_size:
        current = merged([part.astype(F32) for part in out_parts]).astype(BF16)
        if bit * 4 <= seq_size:
            out_parts = quartet(current, "seq", bit)
            bit *= 4
        else:
            out_parts = [current.astype(F32) + crossed(current, "seq", bit).astype(F32)]
            bit *= 2

    feat, filt, skip = on_chip(
        functools.partial(finish_kernel, len(out_parts)),
        [
            sds((parts, taps, channels), F32),
            sds((groups, block), F32),
            sds((1, channels), F32),
        ],
        [],
        out_parts,
        final=True,
    )
    return (jnp.transpose(feat, (1, 0, 2)), filt, skip.reshape(channels))


def solution(mesh):
    return jax.shard_map(
        body,
        mesh=mesh,
        in_specs=(
            P(None, "seq", "dp"),
            P(None, None, "dp"),
            P("dp", None),
            P("dp"),
            P("seq", "dp"),
        ),
        out_specs=(P(None, None, "dp"), P("dp", None), P("dp")),
        check_vma=False,
    )
```

```python
import functools
import math

import jax
import jax.numpy as jnp
from jax import lax
from jax.experimental import pallas as pl
from jax.experimental.pallas import tpu as pltpu
from jax.sharding import PartitionSpec as P


F32 = jnp.float32
BF16 = jnp.bfloat16
LANES = 128
HALO = 8
EDGE = 16


def matmul(a, b, contract):
    return lax.dot_general(
        a, b, ((contract[0], contract[1]), ((), ())), preferred_element_type=F32
    )


def featurize(buf, part, start, rows, taps_ref):
    taps = taps_ref.shape[1]
    total = None
    for tap in range(taps):
        weight = taps_ref[part, tap : tap + 1, :].astype(F32)
        term = weight * buf[part, start - tap : start - tap + rows, :]
        total = term if total is None else total + term
    return total.astype(BF16)


def lag_masks(block):
    row = lax.broadcasted_iota(jnp.int32, (block, block), 0)
    col = lax.broadcasted_iota(jnp.int32, (block, block), 1)
    return row, col


def edge_kernel(
    x_ref, taps_hbm, filt_hbm, cot_hbm, near_ref, taps_ref, filt_ref, cot_ref, far_ref, bufs, sems
):
    _, rows, channels = x_ref.shape
    tail = far_ref.shape[1]
    block = tail - HALO
    copies = [
        pltpu.make_async_copy(
            x_ref.at[1 + part, pl.ds(rows - tail, tail), :], far_ref.at[part], sems.at[part]
        )
        for part in range(2)
    ]
    copies.append(
        pltpu.make_async_copy(
            x_ref.at[0, pl.ds(rows - HALO, HALO), :], near_ref.at[pl.ds(block, HALO), :], sems.at[2]
        )
    )
    copies.append(pltpu.make_async_copy(taps_hbm, taps_ref, sems.at[3]))
    others = [
        pltpu.make_async_copy(filt_hbm, filt_ref, sems.at[4]),
        pltpu.make_async_copy(cot_hbm, cot_ref, sems.at[5]),
    ]
    for copy in copies + others:
        copy.start()
    for copy in copies:
        copy.wait()
    inside = lax.axis_index("seq") < lax.axis_size("seq") - 1
    near_ref[block : block + HALO, :] = jnp.where(inside, near_ref[block : block + HALO, :], 0)

    def product(chunk, buf):
        lane = pl.ds(pl.multiple_of(chunk * LANES, LANES), LANES)
        for part in range(2):
            buf[1 + part] = far_ref[part, :, lane].astype(F32)
            at = block + (1 + part) * HALO
            near_ref[at : at + HALO, lane] = jnp.where(inside, far_ref[part, tail - HALO :, lane], 0)
        k = featurize(buf, 1, HALO, block, taps_ref.at[:, :, lane])
        v = featurize(buf, 2, HALO, block, taps_ref.at[:, :, lane])
        near_ref[:block, lane] = jnp.where(inside, k * v, 0)

    at_once = math.gcd(channels // LANES, bufs.shape[0])

    @pl.loop(0, channels // LANES // at_once)
    def _(turn):
        for number in range(at_once):
            product(turn * at_once + number, bufs.at[number])

    for copy in others:
        copy.wait()


def front_kernel(
    x_ref, taps_ref, filt_ref, skip_ref, cot_ref,
    far_ref, skt_ref, kv_ref, q0_ref, pt_ref, qt_ref, ct_ref, w_ref,
    buf, mask,
):
    parts, rows, channels = x_ref.shape
    block = filt_ref.shape[1]
    members = channels // filt_ref.shape[0]
    groups = LANES // members
    blocks = rows // block
    tail = far_ref.shape[0] // 2
    buf[:, :HALO, :] = jnp.zeros((parts, HALO, LANES), F32)
    row, col = lag_masks(block)
    mask[...] = jnp.where(col >= row, 1.0, 0.0).astype(BF16)
    inside = lax.axis_index("seq") < lax.axis_size("seq") - 1

    def filters(chunk, within, filt):
        group = chunk * groups + within
        taps = jnp.broadcast_to(filt[within : within + 1], (block, block))
        circ = pltpu.roll(taps, 0, 1, stride=1, stride_axis=0).astype(BF16)
        near = circ * mask[...]
        w_ref[group, :block, :] = near
        w_ref[group, block:, :] = circ - near

    def features(chunk, number):
        lane = pl.ds(pl.multiple_of(chunk * LANES, LANES), LANES)
        group_at = pl.ds(pl.multiple_of(chunk * groups, groups), groups)
        span = slice(number * block, (number + 1) * block)
        start = HALO + number * block
        for part in range(parts):
            buf[part, start : start + block, :] = x_ref[part, span, lane].astype(F32)
        q, k, v = (featurize(buf, part, start, block, taps_ref.at[:, :, lane]) for part in range(3))
        kv_ref[chunk, 0, span, :] = k
        kv_ref[chunk, 1, span, :] = v
        if number == 0:
            q0_ref[:, lane] = q
        else:
            place = slice((number - 1) * members, number * members)
            product = k * v
            pt_ref[group_at, place, :] = product.T.reshape(groups, members, block)
            qt_ref[group_at, place, :] = q.T.reshape(groups, members, block)
        place = slice(number * members, (number + 1) * members)
        ct_ref[group_at, place, :] = cot_ref[span, lane].T.reshape(groups, members, block)

    @pl.loop(0, channels // LANES)
    def _(chunk):
        lane = pl.ds(pl.multiple_of(chunk * LANES, LANES), LANES)
        group_at = pl.ds(pl.multiple_of(chunk * groups, groups), groups)
        filt = filt_ref[group_at, :].astype(F32)
        skt_ref[group_at] = skip_columns(skip_ref.at[:, lane], block).reshape(groups, members, block)
        braid(
            [functools.partial(features, chunk, number) for number in range(blocks)],
            [functools.partial(filters, chunk, within, filt) for within in range(groups)],
        )
        for part in range(2):
            ends = jnp.where(inside, x_ref[1 + part, rows - tail :, lane], 0)
            far_ref[part * tail : (part + 1) * tail, lane] = ends


def skip_columns(skip_ref, block):
    lanes = skip_ref.shape[1]
    return jnp.broadcast_to(skip_ref[...].astype(F32), (block, lanes)).T


def middle_kernel(
    near_ref, x_ref, taps_ref, skt_ref, kv_ref, q0_ref, pt_ref, qt_ref, ct_ref, w_ref,
    kve_ref, pta_ref, qta_ref, inner_ref, stats_ref,
    bufs, acc,
):
    channels = near_ref.shape[1]
    block = q0_ref.shape[0]
    members = channels // w_ref.shape[0]
    groups = LANES // members
    width = ct_ref.shape[1]
    blocks = width // members
    chunks = channels // LANES
    acc[...] = jnp.zeros_like(acc)

    def heads(chunk, buf):
        lane = pl.ds(pl.multiple_of(chunk * LANES, LANES), LANES)
        group_at = pl.ds(pl.multiple_of(chunk * groups, groups), groups)
        for part in range(3):
            at = block + part * HALO
            buf[part, :HALO, :] = near_ref[at : at + HALO, lane].astype(F32)
            buf[part, HALO:, :] = x_ref[part, :EDGE, lane].astype(F32)
        q_edge, k_edge, v_edge = (
            featurize(buf, part, HALO, EDGE, taps_ref.at[:, :, lane]) for part in range(3)
        )
        kve_ref[chunk, 0] = k_edge
        kve_ref[chunk, 1] = v_edge
        k0 = jnp.concatenate([k_edge, kv_ref[chunk, 0, EDGE:block, :]], axis=0)
        v0 = jnp.concatenate([v_edge, kv_ref[chunk, 1, EDGE:block, :]], axis=0)
        q0 = jnp.concatenate([q_edge, q0_ref[EDGE:, lane]], axis=0)
        p0 = k0 * v0
        pta_ref[group_at, :members, :] = near_ref[:block, lane].T.reshape(groups, members, block)
        pta_ref[group_at, members:, :] = p0.T.reshape(groups, members, block)
        qta_ref[group_at] = q0.T.reshape(groups, members, block)

    def filters(chunk):
        sums = [[None] * blocks, [None] * blocks]
        for within in range(groups):
            group = chunk * groups + within
            every = jnp.concatenate([pta_ref[group], pt_ref[group]], axis=0)
            now = every[members:]
            filtered = matmul(
                jnp.concatenate([now, every[:width]], axis=1), w_ref[group], ((1,), (0,))
            )
            own = jnp.concatenate([skt_ref[group]] * blocks, axis=0)
            inner = filtered + own * now.astype(F32)
            inner_ref[group] = inner
            q = jnp.concatenate([qta_ref[group], qt_ref[group]], axis=0).astype(F32)
            output = q * inner
            for which, value in enumerate((output * output, ct_ref[group].astype(F32) * output)):
                for number in range(blocks):
                    span = value[number * members : (number + 1) * members]
                    span = span.reshape(members // 8, 8, block).sum(axis=0)
                    sums[which][number] = span if within == 0 else sums[which][number] + span
        for which in range(2):
            for number in range(blocks):
                place = slice(number * 8, number * 8 + 8)
                acc[which, place, :] += sums[which][number]

    at_once = math.gcd(chunks, bufs.shape[0])
    for number in range(at_once):
        heads(number, bufs.at[number])

    @pl.loop(1, chunks // at_once)
    def _(turn):
        for number in range(at_once):
            filters((turn - 1) * at_once + number)
        for number in range(at_once):
            heads(turn * at_once + number, bufs.at[number])

    for number in range(at_once):
        filters(chunks - at_once + number)
    for which in range(2):
        for number in range(blocks):
            at = which * blocks + number
            stats_ref[at : at + 1, :] = jnp.sum(
                acc[which, number * 8 : number * 8 + 8, :], axis=0, keepdims=True
            )


def prep_kernel(near_ref, x_ref, kv_ref, kve_ref, xf_ref, kvf_ref, xq_ref, buf):
    parts, rows, channels = x_ref.shape
    block = near_ref.shape[0] - parts * HALO
    blocks = rows // block

    @pl.loop(0, channels // LANES)
    def _(chunk):
        lane = pl.ds(pl.multiple_of(chunk * LANES, LANES), LANES)
        buf[:HALO, :] = near_ref[block : block + HALO, lane].astype(F32)
        buf[HALO:, :] = x_ref[0, :, lane].astype(F32)
        for tap in range(xq_ref.shape[1]):
            xq_ref[chunk, tap] = buf[HALO - tap : HALO - tap + rows, :].astype(BF16)
        for part in range(1, parts):
            at = block + part * HALO
            xf_ref[chunk, 0, part - 1, :HALO, :] = near_ref[at : at + HALO, lane].astype(F32)
            for number in range(blocks):
                at = number * block
                if number:
                    xf_ref[chunk, number, part - 1, :HALO, :] = x_ref[part, at - HALO : at, lane].astype(F32)
                xf_ref[chunk, number, part - 1, HALO:, :] = x_ref[part, at : at + block, lane].astype(F32)
        for part in range(2):
            kvf_ref[chunk, 0, part, :EDGE, :] = kve_ref[chunk, part].astype(F32)
            kvf_ref[chunk, 0, part, EDGE:, :] = kv_ref[chunk, part, EDGE:block, :].astype(F32)
            for number in range(1, blocks):
                at = number * block
                kvf_ref[chunk, number, part] = kv_ref[chunk, part, at : at + block, :].astype(F32)


def braid(one, two):
    done = 0
    for number, step in enumerate(one):
        step()
        upto = (number + 1) * len(two) // len(one)
        for other in two[done:upto]:
            other()
        done = upto
    for other in two[done:]:
        other()


def rim_kernel(far_ref, taps_ref, pgr_ref, out_ref, sum_ref, buf):
    members, block = pgr_ref.shape[1:]
    groups = LANES // members
    chunks = pgr_ref.shape[0] // groups
    taps = taps_ref.shape[1]
    tail = block + HALO
    sum_ref[:8, :] = out_ref[:8, :]
    sum_ref[24:, :] = out_ref[24:, :]

    @pl.loop(0, chunks)
    def _(chunk):
        lane = pl.ds(pl.multiple_of(chunk * LANES, LANES), LANES)
        for part in range(2):
            buf[1 + part] = far_ref[part * tail : (part + 1) * tail, lane].astype(F32)
        group_at = pl.ds(pl.multiple_of(chunk * groups, groups), groups)
        back = pgr_ref[group_at].reshape(LANES, block).T
        for part in (1, 2):
            other = featurize(buf, 3 - part, HALO, block, taps_ref.at[:, :, lane]).astype(F32)
            grads = back * other
            for tap in range(taps):
                at = part * 8 + tap
                term = grads * buf[part, HALO - tap : HALO - tap + block, :]
                sum_ref[at : at + 1, lane] = out_ref[at : at + 1, lane] + jnp.sum(term, axis=0, keepdims=True)
            sum_ref[part * 8 + taps : part * 8 + 8, lane] = out_ref[part * 8 + taps : part * 8 + 8, lane]


def back_kernel(channels_all, token_scale, taps, n_stats, *refs):
    stats_refs = refs[:n_stats]
    (skt_ref, xf_ref, kvf_ref, xq_ref, pt_ref, pta_ref, qt_ref, qta_ref, ct_ref, inner_ref, w_ref,
     out_ref, pgr_ref, coef, skip_acc, filt_acc, sums, eye, *slots) = refs[n_stats:]
    chunks, blocks = xf_ref.shape[:2]
    parts = 1 + xf_ref.shape[2]
    width, block = ct_ref.shape[1:]
    members = width // blocks
    groups = LANES // members
    total = merged([ref[...] for ref in stats_refs])
    square = total[:blocks]
    cross = total[blocks : 2 * blocks] / channels_all
    rms = jnp.sqrt(square / channels_all + 1e-05)
    inv = token_scale / rms
    fall = token_scale * cross / (rms * rms * rms)
    for number in range(blocks):
        place = slice(number * members, (number + 1) * members)
        coef[0, place, :] = jnp.broadcast_to(inv[number : number + 1], (members, block))
        coef[1, place, :] = jnp.broadcast_to(fall[number : number + 1], (members, block))
    row, col = lag_masks(block)
    slots = (slots[:3], slots[3:])
    eye[...] = jnp.where(row == col, 1.0, 0.0)

    def group_part(chunk, slot, within):
        pg, qg, _ = slots[slot]
        group = chunk * groups + within
        every = jnp.concatenate([pta_ref[group], pt_ref[group]], axis=0)
        now = every[members:]
        q = jnp.concatenate([qta_ref[group], qt_ref[group]], axis=0).astype(F32)
        inner = inner_ref[group]
        output = q * inner
        out_grad = coef[0] * ct_ref[group].astype(F32) - coef[1] * output
        conv_grad = out_grad * q
        cot = conv_grad.astype(BF16)
        query_grad = out_grad * inner
        weighted = conv_grad * now.astype(F32)
        part_sum = weighted[:members]
        for number in range(1, blocks):
            part_sum = part_sum + weighted[number * members : (number + 1) * members]
        skip_acc[group] = part_sum
        gap = jnp.zeros((members, block), BF16)
        here = jnp.concatenate([gap, cot], axis=0)
        later = jnp.concatenate([cot, gap], axis=0)
        grad = matmul(
            jnp.concatenate([here, later], axis=1),
            jnp.concatenate([w_ref[group, :block, :], w_ref[group, block:, :]], axis=1),
            ((1,), (1,)),
        )
        own = skt_ref[group]
        pgr_ref[group] = grad[:members]
        for number in range(blocks):
            span = slice(number * members, (number + 1) * members)
            pg[number, within] = (
                grad[(number + 1) * members : (number + 2) * members] + own * conv_grad[span]
            )
            qg[number, within] = query_grad[span].astype(BF16)
        both = matmul(cot, jnp.concatenate([now, every[:width]], axis=1), ((0,), (0,)))
        lagged = jnp.where(col <= row, both[:, :block], both[:, block:])
        skewed = lagged[:8]
        for start in range(8, block, 8):
            skewed = skewed + pltpu.roll(lagged[start : start + 8], block - start, 1)
        filt_acc[group] = skewed

    def turn(slot):
        pg, _, gn = slots[slot]
        for number in range(blocks):
            gn[number] = pg[number].reshape(LANES, block).T

    def query_steps(chunk, slot):
        qg = slots[slot][1]

        def step(first):
            grads = jnp.concatenate([qg[number].reshape(LANES, block) for number in range(blocks)], axis=1)
            some = range(first, min(first + 2, taps))
            every = matmul(
                grads, jnp.concatenate([xq_ref[chunk, tap] for tap in some], axis=1), ((1,), (0,))
            )
            for place, tap in enumerate(some):
                own = every[:, place * LANES : (place + 1) * LANES] * eye[...]
                sums[chunk, tap] = own.reshape(LANES // 8, 8, LANES).sum(axis=0)

        return [functools.partial(step, first) for first in range(0, taps, 2)]

    def tap_steps(chunk, slot):
        gn = slots[slot][2]
        piece = 32
        totals = {}

        def step(part, number):
            for at in range(0, block, piece):
                grads = gn[number, at : at + piece, :]
                grads = grads * kvf_ref[chunk, number, 2 - part, at : at + piece, :]
                for tap in range(taps):
                    start = HALO + at - tap
                    term = grads * xf_ref[chunk, number, part - 1, start : start + piece, :]
                    term = term.reshape(piece // 8, 8, LANES).sum(axis=0)
                    totals[part, tap] = totals[part, tap] + term if (part, tap) in totals else term
            if number == blocks - 1:
                for tap in range(taps):
                    sums[chunk, part * taps + tap] = totals[part, tap]

        return [functools.partial(step, part, number) for part in range(1, parts) for number in range(blocks)]

    def group_steps(chunk, slot):
        return [functools.partial(group_part, chunk, slot, within) for within in range(groups)]

    def whole_step(chunk, slot):
        turn(1 - slot)
        braid(group_steps(chunk, slot), tap_steps(chunk - 2, slot) + query_steps(chunk - 1, 1 - slot))

    braid(group_steps(0, 0), [])
    if chunks > 1:
        braid(group_steps(1, 1), query_steps(0, 0))
        turn(0)

        @pl.loop(1, chunks // 2)
        def _(pair):
            whole_step(2 * pair, 0)
            whole_step(2 * pair + 1, 1)

        if chunks % 2:
            whole_step(chunks - 1, 0)
        turn((chunks - 1) % 2)
        braid([], tap_steps(chunks - 2, chunks % 2))
    else:
        turn(0)
    last = (chunks - 1) % 2
    braid(query_steps(chunks - 1, last), tap_steps(chunks - 1, last))

    flip = jnp.where(((row + col) % block) == 0, 1.0, 0.0).astype(F32)
    lags = filt_acc[:, 0, :]
    for at in range(1, 8):
        lags = lags + pltpu.roll(filt_acc[:, at, :], block - at, 1)
    lags = lax.dot_general(
        lags, flip, (((1,), (0,)), ((), ())), preferred_element_type=F32, precision=lax.Precision.HIGHEST
    )
    for chunk in range(chunks):
        lane = slice(chunk * LANES, (chunk + 1) * LANES)
        group_at = slice(chunk * groups, (chunk + 1) * groups)
        out_ref[3 * 8 :, lane] = lags[group_at]
        skip_row = jnp.sum(skip_acc[group_at].reshape(LANES, block).T, axis=0, keepdims=True)
        for part in range(parts):
            for tap in range(taps):
                out_ref[part * 8 + tap : part * 8 + tap + 1, lane] = jnp.sum(
                    sums[chunk, part * taps + tap], axis=0, keepdims=True
                )
            out_ref[part * 8 + taps : part * 8 + 8, lane] = skip_row


def finish_kernel(n_in, *refs):
    ins = refs[:n_in]
    feat_ref, filt_ref, skip_ref = refs[n_in:]
    total = merged([ref[...].astype(F32) for ref in ins])
    taps = feat_ref.shape[1]
    for part in range(feat_ref.shape[0]):
        feat_ref[part] = total[part * 8 : part * 8 + taps]
    skip_ref[...] = total[taps : taps + 1]
    groups = total.shape[0] - 24
    for chunk in range(total.shape[1] // LANES):
        filt_ref[chunk * groups : (chunk + 1) * groups, :] = total[24:, chunk * LANES : (chunk + 1) * LANES]


def ring(array, axis):
    length = lax.axis_size(axis)
    return lax.ppermute(array, axis, [(i, (i + 1) % length) for i in range(length)])


def crossed(array, axis, bit):
    length = lax.axis_size(axis)
    return lax.ppermute(array, axis, [(i, i ^ bit) for i in range(length)])


def quartet(array, axis, bit):
    return [array] + [crossed(array, axis, bit * k) for k in (1, 2, 3)]


def merged(parts):
    if len(parts) == 1:
        return parts[0]
    return (parts[0] + parts[1]) + (parts[2] + parts[3])


def on_chip(kernel, out_shape, scratch, args, outside=(), final=False):
    place = pl.BlockSpec(memory_space=pltpu.VMEM)
    apart = pl.BlockSpec(memory_space=pl.ANY)
    if not final:
        out_shape = [pltpu.VMEM(out.shape, out.dtype) for out in out_shape]
    args = [
        pltpu.with_memory_space_constraint(arg, pltpu.HBM if number in outside else pltpu.VMEM)
        for number, arg in enumerate(args)
    ]
    return pl.pallas_call(
        kernel,
        in_specs=[apart if number in outside else place for number in range(len(args))],
        out_specs=[place] * len(out_shape),
        out_shape=out_shape,
        scratch_shapes=scratch,
        compiler_params=pltpu.CompilerParams(vmem_limit_bytes=16 * 1024 * 1024),
    )(*args)


def body(projected, featurizer, long_filter, skip_gain, out_cotangent):
    parts, rows, channels = projected.shape
    groups, block = long_filter.shape
    taps = featurizer.shape[0]
    members = channels // groups
    chunk_groups = LANES // members
    blocks = rows // block
    width = blocks * members
    tail = block + HALO
    taps_major = jnp.transpose(featurizer, (1, 0, 2))
    skip_row = skip_gain.reshape(1, channels)

    sds = jax.ShapeDtypeStruct
    chunks = channels // LANES

    near, taps_major, filters, cots = on_chip(
        edge_kernel,
        [
            sds((block + parts * HALO, channels), BF16),
            sds((parts, taps, channels), BF16),
            sds((groups, block), BF16),
            sds((rows, channels), BF16),
        ],
        [
            pltpu.VMEM((2, tail, channels), BF16),
            pltpu.VMEM((4, parts, tail, LANES), F32),
            pltpu.SemaphoreType.DMA((6,)),
        ],
        (projected, taps_major, long_filter, out_cotangent),
        outside=(0, 1, 2, 3),
    )
    near = ring(near, "seq")

    far, skt, kv, q0, pt, qt, ct, w = on_chip(
        front_kernel,
        [
            sds((2 * tail, channels), BF16),
            sds((groups, members, block), F32),
            sds((chunks, 2, rows, LANES), BF16),
            sds((block, channels), BF16),
            sds((groups, width - members, block), BF16),
            sds((groups, width - members, block), BF16),
            sds((groups, width, block), BF16),
            sds((groups, 2 * block, block), BF16),
        ],
        [
            pltpu.VMEM((parts, HALO + rows, LANES), F32),
            pltpu.VMEM((block, block), BF16),
        ],
        (projected, taps_major, filters, skip_row, cots),
    )
    far = ring(far, "seq")
    kve, pta, qta, inner, stats = on_chip(
        middle_kernel,
        [
            sds((chunks, 2, EDGE, LANES), BF16),
            sds((groups, 2 * members, block), BF16),
            sds((groups, members, block), BF16),
            sds((groups, width, block), F32),
            sds((2 * blocks, block), F32),
        ],
        [
            pltpu.VMEM((2, parts, HALO + EDGE, LANES), F32),
            pltpu.VMEM((2, 8 * blocks, block), F32),
        ],
        (near, projected, taps_major, skt, kv, q0, pt, qt, ct, w),
    )

    dp_size = lax.axis_size("dp")
    stat_parts = [stats]
    bit = 1
    while bit < dp_size:
        current = merged(stat_parts)
        if bit * 4 <= dp_size:
            stat_parts = quartet(current, "dp", bit)
            bit *= 4
        else:
            stat_parts = [current + crossed(current, "dp", bit)]
            bit *= 2
    xf, kvf, xq = on_chip(
        prep_kernel,
        [
            sds((chunks, blocks, 2, HALO + block, LANES), F32),
            sds((chunks, blocks, 2, block, LANES), F32),
            sds((chunks, taps, rows, LANES), BF16),
        ],
        [pltpu.VMEM((HALO + rows, LANES), F32)],
        (near, projected, kv, kve),
    )
    token_scale = 1.0 / math.sqrt(rows * lax.axis_size("seq"))
    out, pgr = on_chip(
        functools.partial(back_kernel, channels * dp_size, token_scale, taps, len(stat_parts)),
        [sds((24 + chunk_groups, channels), F32), sds((groups, members, block), F32)],
        [
            pltpu.VMEM((2, width, block), F32),
            pltpu.VMEM((groups, members, block), F32),
            pltpu.VMEM((groups, 8, block), F32),
            pltpu.VMEM((chunks, parts * taps, 8, LANES), F32),
            pltpu.VMEM((LANES, LANES), F32),
        ]
        + [
            pltpu.VMEM((blocks, chunk_groups, members, block), F32),
            pltpu.VMEM((blocks, chunk_groups, members, block), BF16),
            pltpu.VMEM((blocks, block, LANES), F32),
        ]
        * 2,
        (*stat_parts, skt, xf, kvf, xq, pt, pta, qt, qta, ct, inner, w),
    )
    (out,) = on_chip(
        rim_kernel,
        [sds((24 + chunk_groups, channels), F32)],
        [pltpu.VMEM((parts, tail, LANES), F32)],
        (far, taps_major, pgr, out),
    )

    seq_size = lax.axis_size("seq")
    out_parts = [out + crossed(out, "seq", 1)]
    bit = 2
    while bit < seq_size:
        current = merged([part.astype(F32) for part in out_parts]).astype(BF16)
        if bit * 4 <= seq_size:
            out_parts = quartet(current, "seq", bit)
            bit *= 4
        else:
            out_parts = [current.astype(F32) + crossed(current, "seq", bit).astype(F32)]
            bit *= 2

    feat, filt, skip = on_chip(
        functools.partial(finish_kernel, len(out_parts)),
        [
            sds((parts, taps, channels), F32),
            sds((groups, block), F32),
            sds((1, channels), F32),
        ],
        [],
        out_parts,
        final=True,
    )
    return (jnp.transpose(feat, (1, 0, 2)), filt, skip.reshape(channels))


def solution(mesh):
    return jax.shard_map(
        body,
        mesh=mesh,
        in_specs=(
            P(None, "seq", "dp"),
            P(None, None, "dp"),
            P("dp", None),
            P("dp"),
            P("seq", "dp"),
        ),
        out_specs=(P(None, None, "dp"), P("dp", None), P("dp")),
        check_vma=False,
    )
```

```python
import functools
import math

import jax
import jax.numpy as jnp
from jax import lax
from jax.experimental import pallas as pl
from jax.experimental.pallas import tpu as pltpu
from jax.sharding import PartitionSpec as P


F32 = jnp.float32
BF16 = jnp.bfloat16
LANES = 128
HALO = 8
EDGE = 16


def matmul(a, b, contract):
    return lax.dot_general(
        a, b, ((contract[0], contract[1]), ((), ())), preferred_element_type=F32
    )


def featurize(buf, part, start, rows, taps_ref):
    taps = taps_ref.shape[1]
    total = None
    for tap in range(taps):
        weight = taps_ref[part, tap : tap + 1, :].astype(F32)
        term = weight * buf[part, start - tap : start - tap + rows, :]
        total = term if total is None else total + term
    return total.astype(BF16)


def lag_masks(block):
    row = lax.broadcasted_iota(jnp.int32, (block, block), 0)
    col = lax.broadcasted_iota(jnp.int32, (block, block), 1)
    return row, col


def edge_kernel(
    x_ref, taps_hbm, filt_hbm, cot_hbm, near_ref, taps_ref, filt_ref, cot_ref, far_ref, bufs, sems
):
    _, rows, channels = x_ref.shape
    tail = far_ref.shape[1]
    block = tail - HALO
    copies = [
        pltpu.make_async_copy(
            x_ref.at[1 + part, pl.ds(rows - tail, tail), :], far_ref.at[part], sems.at[part]
        )
        for part in range(2)
    ]
    copies.append(
        pltpu.make_async_copy(
            x_ref.at[0, pl.ds(rows - HALO, HALO), :], near_ref.at[pl.ds(block, HALO), :], sems.at[2]
        )
    )
    copies.append(pltpu.make_async_copy(taps_hbm, taps_ref, sems.at[3]))
    others = [
        pltpu.make_async_copy(filt_hbm, filt_ref, sems.at[4]),
        pltpu.make_async_copy(cot_hbm, cot_ref, sems.at[5]),
    ]
    for copy in copies + others:
        copy.start()
    for copy in copies:
        copy.wait()
    inside = lax.axis_index("seq") < lax.axis_size("seq") - 1
    near_ref[block : block + HALO, :] = jnp.where(inside, near_ref[block : block + HALO, :], 0)

    def product(chunk, buf):
        lane = pl.ds(pl.multiple_of(chunk * LANES, LANES), LANES)
        for part in range(2):
            buf[1 + part] = far_ref[part, :, lane].astype(F32)
            at = block + (1 + part) * HALO
            near_ref[at : at + HALO, lane] = jnp.where(inside, far_ref[part, tail - HALO :, lane], 0)
        k = featurize(buf, 1, HALO, block, taps_ref.at[:, :, lane])
        v = featurize(buf, 2, HALO, block, taps_ref.at[:, :, lane])
        near_ref[:block, lane] = jnp.where(inside, k * v, 0)

    at_once = math.gcd(channels // LANES, bufs.shape[0])

    @pl.loop(0, channels // LANES // at_once)
    def _(turn):
        for number in range(at_once):
            product(turn * at_once + number, bufs.at[number])

    for copy in others:
        copy.wait()


def front_kernel(
    x_ref, taps_ref, filt_ref, skip_ref, cot_ref,
    far_ref, skt_ref, kv_ref, q0_ref, pt_ref, qt_ref, ct_ref, w_ref,
    buf, mask,
):
    parts, rows, channels = x_ref.shape
    block = filt_ref.shape[1]
    members = channels // filt_ref.shape[0]
    groups = LANES // members
    blocks = rows // block
    tail = far_ref.shape[0] // 2
    buf[:, :HALO, :] = jnp.zeros((parts, HALO, LANES), F32)
    row, col = lag_masks(block)
    mask[...] = jnp.where(col >= row, 1.0, 0.0).astype(BF16)
    inside = lax.axis_index("seq") < lax.axis_size("seq") - 1

    def filters(chunk, within, filt):
        group = chunk * groups + within
        taps = jnp.broadcast_to(filt[within : within + 1], (block, block))
        circ = pltpu.roll(taps, 0, 1, stride=1, stride_axis=0).astype(BF16)
        near = circ * mask[...]
        w_ref[group, :block, :] = near
        w_ref[group, block:, :] = circ - near

    def features(chunk, number):
        lane = pl.ds(pl.multiple_of(chunk * LANES, LANES), LANES)
        group_at = pl.ds(pl.multiple_of(chunk * groups, groups), groups)
        span = slice(number * block, (number + 1) * block)
        start = HALO + number * block
        for part in range(parts):
            buf[part, start : start + block, :] = x_ref[part, span, lane].astype(F32)
        q, k, v = (featurize(buf, part, start, block, taps_ref.at[:, :, lane]) for part in range(3))
        kv_ref[chunk, 0, span, :] = k
        kv_ref[chunk, 1, span, :] = v
        if number == 0:
            q0_ref[:, lane] = q
        else:
            place = slice((number - 1) * members, number * members)
            product = k * v
            pt_ref[group_at, place, :] = product.T.reshape(groups, members, block)
            qt_ref[group_at, place, :] = q.T.reshape(groups, members, block)
        place = slice(number * members, (number + 1) * members)
        ct_ref[group_at, place, :] = cot_ref[span, lane].T.reshape(groups, members, block)

    @pl.loop(0, channels // LANES)
    def _(chunk):
        lane = pl.ds(pl.multiple_of(chunk * LANES, LANES), LANES)
        group_at = pl.ds(pl.multiple_of(chunk * groups, groups), groups)
        filt = filt_ref[group_at, :].astype(F32)
        skt_ref[group_at] = skip_columns(skip_ref.at[:, lane], block).reshape(groups, members, block)
        braid(
            [functools.partial(features, chunk, number) for number in range(blocks)],
            [functools.partial(filters, chunk, within, filt) for within in range(groups)],
        )
        for part in range(2):
            ends = jnp.where(inside, x_ref[1 + part, rows - tail :, lane], 0)
            far_ref[part * tail : (part + 1) * tail, lane] = ends


def skip_columns(skip_ref, block):
    lanes = skip_ref.shape[1]
    return jnp.broadcast_to(skip_ref[...].astype(F32), (block, lanes)).T


def middle_kernel(
    near_ref, x_ref, taps_ref, skt_ref, kv_ref, q0_ref, pt_ref, qt_ref, ct_ref, w_ref,
    kve_ref, pta_ref, qta_ref, inner_ref, stats_ref,
    bufs, acc,
):
    channels = near_ref.shape[1]
    block = q0_ref.shape[0]
    members = channels // w_ref.shape[0]
    groups = LANES // members
    width = ct_ref.shape[1]
    blocks = width // members
    chunks = channels // LANES
    acc[...] = jnp.zeros_like(acc)

    def heads(chunk, buf):
        lane = pl.ds(pl.multiple_of(chunk * LANES, LANES), LANES)
        group_at = pl.ds(pl.multiple_of(chunk * groups, groups), groups)
        for part in range(3):
            at = block + part * HALO
            buf[part, :HALO, :] = near_ref[at : at + HALO, lane].astype(F32)
            buf[part, HALO:, :] = x_ref[part, :EDGE, lane].astype(F32)
        q_edge, k_edge, v_edge = (
            featurize(buf, part, HALO, EDGE, taps_ref.at[:, :, lane]) for part in range(3)
        )
        kve_ref[chunk, 0] = k_edge
        kve_ref[chunk, 1] = v_edge
        k0 = jnp.concatenate([k_edge, kv_ref[chunk, 0, EDGE:block, :]], axis=0)
        v0 = jnp.concatenate([v_edge, kv_ref[chunk, 1, EDGE:block, :]], axis=0)
        q0 = jnp.concatenate([q_edge, q0_ref[EDGE:, lane]], axis=0)
        p0 = k0 * v0
        pta_ref[group_at, :members, :] = near_ref[:block, lane].T.reshape(groups, members, block)
        pta_ref[group_at, members:, :] = p0.T.reshape(groups, members, block)
        qta_ref[group_at] = q0.T.reshape(groups, members, block)

    def filters(chunk):
        sums = [[None] * blocks, [None] * blocks]
        for within in range(groups):
            group = chunk * groups + within
            every = jnp.concatenate([pta_ref[group], pt_ref[group]], axis=0)
            now = every[members:]
            filtered = matmul(
                jnp.concatenate([now, every[:width]], axis=1), w_ref[group], ((1,), (0,))
            )
            own = jnp.concatenate([skt_ref[group]] * blocks, axis=0)
            inner = filtered + own * now.astype(F32)
            inner_ref[group] = inner
            q = jnp.concatenate([qta_ref[group], qt_ref[group]], axis=0).astype(F32)
            output = q * inner
            for which, value in enumerate((output * output, ct_ref[group].astype(F32) * output)):
                for number in range(blocks):
                    span = value[number * members : (number + 1) * members]
                    span = span.reshape(members // 8, 8, block).sum(axis=0)
                    sums[which][number] = span if within == 0 else sums[which][number] + span
        for which in range(2):
            for number in range(blocks):
                place = slice(number * 8, number * 8 + 8)
                acc[which, place, :] += sums[which][number]

    at_once = math.gcd(chunks, bufs.shape[0])
    for number in range(at_once):
        heads(number, bufs.at[number])

    @pl.loop(1, chunks // at_once)
    def _(turn):
        for number in range(at_once):
            filters((turn - 1) * at_once + number)
        for number in range(at_once):
            heads(turn * at_once + number, bufs.at[number])

    for number in range(at_once):
        filters(chunks - at_once + number)
    for which in range(2):
        for number in range(blocks):
            at = which * blocks + number
            stats_ref[at : at + 1, :] = jnp.sum(
                acc[which, number * 8 : number * 8 + 8, :], axis=0, keepdims=True
            )


def prep_kernel(near_ref, x_ref, kv_ref, kve_ref, xf_ref, kvf_ref, xq_ref, buf):
    parts, rows, channels = x_ref.shape
    block = near_ref.shape[0] - parts * HALO
    blocks = rows // block

    @pl.loop(0, channels // LANES)
    def _(chunk):
        lane = pl.ds(pl.multiple_of(chunk * LANES, LANES), LANES)
        buf[:HALO, :] = near_ref[block : block + HALO, lane].astype(F32)
        buf[HALO:, :] = x_ref[0, :, lane].astype(F32)
        for tap in range(xq_ref.shape[1]):
            xq_ref[chunk, tap] = buf[HALO - tap : HALO - tap + rows, :].astype(BF16)
        for part in range(1, parts):
            at = block + part * HALO
            xf_ref[chunk, 0, part - 1, :HALO, :] = near_ref[at : at + HALO, lane].astype(F32)
            for number in range(blocks):
                at = number * block
                if number:
                    xf_ref[chunk, number, part - 1, :HALO, :] = x_ref[part, at - HALO : at, lane].astype(F32)
                xf_ref[chunk, number, part - 1, HALO:, :] = x_ref[part, at : at + block, lane].astype(F32)
        for part in range(2):
            kvf_ref[chunk, 0, part, :EDGE, :] = kve_ref[chunk, part].astype(F32)
            kvf_ref[chunk, 0, part, EDGE:, :] = kv_ref[chunk, part, EDGE:block, :].astype(F32)
            for number in range(1, blocks):
                at = number * block
                kvf_ref[chunk, number, part] = kv_ref[chunk, part, at : at + block, :].astype(F32)


def braid(one, two):
    done = 0
    for number, step in enumerate(one):
        step()
        upto = (number + 1) * len(two) // len(one)
        for other in two[done:upto]:
            other()
        done = upto
    for other in two[done:]:
        other()


def rim_kernel(far_ref, taps_ref, pgr_ref, out_ref, sum_ref, buf):
    members, block = pgr_ref.shape[1:]
    groups = LANES // members
    chunks = pgr_ref.shape[0] // groups
    taps = taps_ref.shape[1]
    tail = block + HALO
    sum_ref[:8, :] = out_ref[:8, :]
    sum_ref[24:, :] = out_ref[24:, :]

    @pl.loop(0, chunks)
    def _(chunk):
        lane = pl.ds(pl.multiple_of(chunk * LANES, LANES), LANES)
        for part in range(2):
            buf[1 + part] = far_ref[part * tail : (part + 1) * tail, lane].astype(F32)
        group_at = pl.ds(pl.multiple_of(chunk * groups, groups), groups)
        back = pgr_ref[group_at].reshape(LANES, block).T
        for part in (1, 2):
            other = featurize(buf, 3 - part, HALO, block, taps_ref.at[:, :, lane]).astype(F32)
            grads = back * other
            for tap in range(taps):
                at = part * 8 + tap
                term = grads * buf[part, HALO - tap : HALO - tap + block, :]
                sum_ref[at : at + 1, lane] = out_ref[at : at + 1, lane] + jnp.sum(term, axis=0, keepdims=True)
            sum_ref[part * 8 + taps : part * 8 + 8, lane] = out_ref[part * 8 + taps : part * 8 + 8, lane]


def back_kernel(channels_all, token_scale, taps, n_stats, *refs):
    stats_refs = refs[:n_stats]
    (skt_ref, xf_ref, kvf_ref, xq_ref, pt_ref, pta_ref, qt_ref, qta_ref, ct_ref, inner_ref, w_ref,
     out_ref, pgr_ref, coef, skip_acc, filt_acc, sums, eye, *slots) = refs[n_stats:]
    chunks, blocks = xf_ref.shape[:2]
    parts = 1 + xf_ref.shape[2]
    width, block = ct_ref.shape[1:]
    members = width // blocks
    groups = LANES // members
    total = merged([ref[...] for ref in stats_refs])
    square = total[:blocks]
    cross = total[blocks : 2 * blocks] / channels_all
    rms = jnp.sqrt(square / channels_all + 1e-05)
    inv = token_scale / rms
    fall = token_scale * cross / (rms * rms * rms)
    for number in range(blocks):
        place = slice(number * members, (number + 1) * members)
        coef[0, place, :] = jnp.broadcast_to(inv[number : number + 1], (members, block))
        coef[1, place, :] = jnp.broadcast_to(fall[number : number + 1], (members, block))
    row, col = lag_masks(block)
    slots = (slots[:3], slots[3:])
    eye[...] = jnp.where(row == col, 1.0, 0.0)

    def group_part(chunk, slot, within):
        pg, qg, _ = slots[slot]
        group = chunk * groups + within
        every = jnp.concatenate([pta_ref[group], pt_ref[group]], axis=0)
        now = every[members:]
        q = jnp.concatenate([qta_ref[group], qt_ref[group]], axis=0).astype(F32)
        inner = inner_ref[group]
        output = q * inner
        out_grad = coef[0] * ct_ref[group].astype(F32) - coef[1] * output
        conv_grad = out_grad * q
        cot = conv_grad.astype(BF16)
        query_grad = out_grad * inner
        weighted = conv_grad * now.astype(F32)
        part_sum = weighted[:members]
        for number in range(1, blocks):
            part_sum = part_sum + weighted[number * members : (number + 1) * members]
        skip_acc[group] = part_sum
        gap = jnp.zeros((members, block), BF16)
        here = jnp.concatenate([gap, cot], axis=0)
        later = jnp.concatenate([cot, gap], axis=0)
        grad = matmul(
            jnp.concatenate([here, later], axis=1),
            jnp.concatenate([w_ref[group, :block, :], w_ref[group, block:, :]], axis=1),
            ((1,), (1,)),
        )
        own = skt_ref[group]
        pgr_ref[group] = grad[:members]
        for number in range(blocks):
            span = slice(number * members, (number + 1) * members)
            pg[number, within] = (
                grad[(number + 1) * members : (number + 2) * members] + own * conv_grad[span]
            )
            qg[number, within] = query_grad[span].astype(BF16)
        both = matmul(cot, jnp.concatenate([now, every[:width]], axis=1), ((0,), (0,)))
        lagged = jnp.where(col <= row, both[:, :block], both[:, block:])
        skewed = lagged[:8]
        for start in range(8, block, 8):
            skewed = skewed + pltpu.roll(lagged[start : start + 8], block - start, 1)
        filt_acc[group] = skewed

    def turn(slot):
        pg, _, gn = slots[slot]
        for number in range(blocks):
            gn[number] = pg[number].reshape(LANES, block).T

    def query_steps(chunk, slot):
        qg = slots[slot][1]

        def step(first):
            grads = jnp.concatenate([qg[number].reshape(LANES, block) for number in range(blocks)], axis=1)
            some = range(first, min(first + 2, taps))
            every = matmul(
                grads, jnp.concatenate([xq_ref[chunk, tap] for tap in some], axis=1), ((1,), (0,))
            )
            for place, tap in enumerate(some):
                own = every[:, place * LANES : (place + 1) * LANES] * eye[...]
                sums[chunk, tap] = own.reshape(LANES // 8, 8, LANES).sum(axis=0)

        return [functools.partial(step, first) for first in range(0, taps, 2)]

    def tap_steps(chunk, slot):
        gn = slots[slot][2]
        piece = 32
        totals = {}

        def step(part, number):
            for at in range(0, block, piece):
                grads = gn[number, at : at + piece, :]
                grads = grads * kvf_ref[chunk, number, 2 - part, at : at + piece, :]
                for tap in range(taps):
                    start = HALO + at - tap
                    term = grads * xf_ref[chunk, number, part - 1, start : start + piece, :]
                    term = term.reshape(piece // 8, 8, LANES).sum(axis=0)
                    totals[part, tap] = totals[part, tap] + term if (part, tap) in totals else term
            if number == blocks - 1:
                for tap in range(taps):
                    sums[chunk, part * taps + tap] = totals[part, tap]

        return [functools.partial(step, part, number) for part in range(1, parts) for number in range(blocks)]

    def group_steps(chunk, slot):
        return [functools.partial(group_part, chunk, slot, within) for within in range(groups)]

    def whole_step(chunk, slot):
        turn(1 - slot)
        braid(group_steps(chunk, slot), tap_steps(chunk - 2, slot) + query_steps(chunk - 1, 1 - slot))

    braid(group_steps(0, 0), [])
    if chunks > 1:
        braid(group_steps(1, 1), query_steps(0, 0))
        turn(0)

        pairs = chunks // 2 - 1
        at_once = 3 if pairs % 3 == 0 else 1

        @pl.loop(0, pairs // at_once)
        def _(turn):
            for number in range(at_once):
                pair = 1 + turn * at_once + number
                whole_step(2 * pair, 0)
                whole_step(2 * pair + 1, 1)

        if chunks % 2:
            whole_step(chunks - 1, 0)
        turn((chunks - 1) % 2)
        braid([], tap_steps(chunks - 2, chunks % 2))
    else:
        turn(0)
    last = (chunks - 1) % 2
    braid(query_steps(chunks - 1, last), tap_steps(chunks - 1, last))

    flip = jnp.where(((row + col) % block) == 0, 1.0, 0.0).astype(F32)
    lags = filt_acc[:, 0, :]
    for at in range(1, 8):
        lags = lags + pltpu.roll(filt_acc[:, at, :], block - at, 1)
    lags = lax.dot_general(
        lags, flip, (((1,), (0,)), ((), ())), preferred_element_type=F32, precision=lax.Precision.HIGHEST
    )
    for chunk in range(chunks):
        lane = slice(chunk * LANES, (chunk + 1) * LANES)
        group_at = slice(chunk * groups, (chunk + 1) * groups)
        out_ref[3 * 8 :, lane] = lags[group_at]
        skip_row = jnp.sum(skip_acc[group_at].reshape(LANES, block).T, axis=0, keepdims=True)
        for part in range(parts):
            for tap in range(taps):
                out_ref[part * 8 + tap : part * 8 + tap + 1, lane] = jnp.sum(
                    sums[chunk, part * taps + tap], axis=0, keepdims=True
                )
            out_ref[part * 8 + taps : part * 8 + 8, lane] = skip_row


def finish_kernel(n_in, *refs):
    ins = refs[:n_in]
    feat_ref, filt_ref, skip_ref = refs[n_in:]
    total = merged([ref[...].astype(F32) for ref in ins])
    taps = feat_ref.shape[1]
    for part in range(feat_ref.shape[0]):
        feat_ref[part] = total[part * 8 : part * 8 + taps]
    skip_ref[...] = total[taps : taps + 1]
    groups = total.shape[0] - 24
    for chunk in range(total.shape[1] // LANES):
        filt_ref[chunk * groups : (chunk + 1) * groups, :] = total[24:, chunk * LANES : (chunk + 1) * LANES]


def ring(array, axis):
    length = lax.axis_size(axis)
    return lax.ppermute(array, axis, [(i, (i + 1) % length) for i in range(length)])


def crossed(array, axis, bit):
    length = lax.axis_size(axis)
    return lax.ppermute(array, axis, [(i, i ^ bit) for i in range(length)])


def quartet(array, axis, bit):
    return [array] + [crossed(array, axis, bit * k) for k in (1, 2, 3)]


def merged(parts):
    if len(parts) == 1:
        return parts[0]
    return (parts[0] + parts[1]) + (parts[2] + parts[3])


def on_chip(kernel, out_shape, scratch, args, outside=(), final=False):
    place = pl.BlockSpec(memory_space=pltpu.VMEM)
    apart = pl.BlockSpec(memory_space=pl.ANY)
    if not final:
        out_shape = [pltpu.VMEM(out.shape, out.dtype) for out in out_shape]
    args = [
        pltpu.with_memory_space_constraint(arg, pltpu.HBM if number in outside else pltpu.VMEM)
        for number, arg in enumerate(args)
    ]
    return pl.pallas_call(
        kernel,
        in_specs=[apart if number in outside else place for number in range(len(args))],
        out_specs=[place] * len(out_shape),
        out_shape=out_shape,
        scratch_shapes=scratch,
        compiler_params=pltpu.CompilerParams(vmem_limit_bytes=16 * 1024 * 1024),
    )(*args)


def body(projected, featurizer, long_filter, skip_gain, out_cotangent):
    parts, rows, channels = projected.shape
    groups, block = long_filter.shape
    taps = featurizer.shape[0]
    members = channels // groups
    chunk_groups = LANES // members
    blocks = rows // block
    width = blocks * members
    tail = block + HALO
    taps_major = jnp.transpose(featurizer, (1, 0, 2))
    skip_row = skip_gain.reshape(1, channels)

    sds = jax.ShapeDtypeStruct
    chunks = channels // LANES

    near, taps_major, filters, cots = on_chip(
        edge_kernel,
        [
            sds((block + parts * HALO, channels), BF16),
            sds((parts, taps, channels), BF16),
            sds((groups, block), BF16),
            sds((rows, channels), BF16),
        ],
        [
            pltpu.VMEM((2, tail, channels), BF16),
            pltpu.VMEM((4, parts, tail, LANES), F32),
            pltpu.SemaphoreType.DMA((6,)),
        ],
        (projected, taps_major, long_filter, out_cotangent),
        outside=(0, 1, 2, 3),
    )
    near = ring(near, "seq")

    far, skt, kv, q0, pt, qt, ct, w = on_chip(
        front_kernel,
        [
            sds((2 * tail, channels), BF16),
            sds((groups, members, block), F32),
            sds((chunks, 2, rows, LANES), BF16),
            sds((block, channels), BF16),
            sds((groups, width - members, block), BF16),
            sds((groups, width - members, block), BF16),
            sds((groups, width, block), BF16),
            sds((groups, 2 * block, block), BF16),
        ],
        [
            pltpu.VMEM((parts, HALO + rows, LANES), F32),
            pltpu.VMEM((block, block), BF16),
        ],
        (projected, taps_major, filters, skip_row, cots),
    )
    far = ring(far, "seq")
    kve, pta, qta, inner, stats = on_chip(
        middle_kernel,
        [
            sds((chunks, 2, EDGE, LANES), BF16),
            sds((groups, 2 * members, block), BF16),
            sds((groups, members, block), BF16),
            sds((groups, width, block), F32),
            sds((2 * blocks, block), F32),
        ],
        [
            pltpu.VMEM((4, parts, HALO + EDGE, LANES), F32),
            pltpu.VMEM((2, 8 * blocks, block), F32),
        ],
        (near, projected, taps_major, skt, kv, q0, pt, qt, ct, w),
    )

    dp_size = lax.axis_size("dp")
    stat_parts = [stats]
    bit = 1
    while bit < dp_size:
        current = merged(stat_parts)
        if bit * 4 <= dp_size:
            stat_parts = quartet(current, "dp", bit)
            bit *= 4
        else:
            stat_parts = [current + crossed(current, "dp", bit)]
            bit *= 2
    xf, kvf, xq = on_chip(
        prep_kernel,
        [
            sds((chunks, blocks, 2, HALO + block, LANES), F32),
            sds((chunks, blocks, 2, block, LANES), F32),
            sds((chunks, taps, rows, LANES), BF16),
        ],
        [pltpu.VMEM((HALO + rows, LANES), F32)],
        (near, projected, kv, kve),
    )
    token_scale = 1.0 / math.sqrt(rows * lax.axis_size("seq"))
    out, pgr = on_chip(
        functools.partial(back_kernel, channels * dp_size, token_scale, taps, len(stat_parts)),
        [sds((24 + chunk_groups, channels), F32), sds((groups, members, block), F32)],
        [
            pltpu.VMEM((2, width, block), F32),
            pltpu.VMEM((groups, members, block), F32),
            pltpu.VMEM((groups, 8, block), F32),
            pltpu.VMEM((chunks, parts * taps, 8, LANES), F32),
            pltpu.VMEM((LANES, LANES), F32),
        ]
        + [
            pltpu.VMEM((blocks, chunk_groups, members, block), F32),
            pltpu.VMEM((blocks, chunk_groups, members, block), BF16),
            pltpu.VMEM((blocks, block, LANES), F32),
        ]
        * 2,
        (*stat_parts, skt, xf, kvf, xq, pt, pta, qt, qta, ct, inner, w),
    )
    (out,) = on_chip(
        rim_kernel,
        [sds((24 + chunk_groups, channels), F32)],
        [pltpu.VMEM((parts, tail, LANES), F32)],
        (far, taps_major, pgr, out),
    )

    seq_size = lax.axis_size("seq")
    out_parts = [out + crossed(out, "seq", 1)]
    bit = 2
    while bit < seq_size:
        current = merged([part.astype(F32) for part in out_parts]).astype(BF16)
        if bit * 4 <= seq_size:
            out_parts = quartet(current, "seq", bit)
            bit *= 4
        else:
            out_parts = [current.astype(F32) + crossed(current, "seq", bit).astype(F32)]
            bit *= 2

    feat, filt, skip = on_chip(
        functools.partial(finish_kernel, len(out_parts)),
        [
            sds((parts, taps, channels), F32),
            sds((groups, block), F32),
            sds((1, channels), F32),
        ],
        [],
        out_parts,
        final=True,
    )
    return (jnp.transpose(feat, (1, 0, 2)), filt, skip.reshape(channels))


def solution(mesh):
    return jax.shard_map(
        body,
        mesh=mesh,
        in_specs=(
            P(None, "seq", "dp"),
            P(None, None, "dp"),
            P("dp", None),
            P("dp"),
            P("seq", "dp"),
        ),
        out_specs=(P(None, None, "dp"), P("dp", None), P("dp")),
        check_vma=False,
    )
```

```python
import functools
import math

import jax
import jax.numpy as jnp
from jax import lax
from jax.experimental import pallas as pl
from jax.experimental.pallas import tpu as pltpu
from jax.sharding import PartitionSpec as P


F32 = jnp.float32
BF16 = jnp.bfloat16
LANES = 128
HALO = 8
EDGE = 16


def matmul(a, b, contract):
    return lax.dot_general(
        a, b, ((contract[0], contract[1]), ((), ())), preferred_element_type=F32
    )


def featurize(buf, part, start, rows, taps_ref):
    taps = taps_ref.shape[1]
    total = None
    for tap in range(taps):
        weight = taps_ref[part, tap : tap + 1, :].astype(F32)
        term = weight * buf[part, start - tap : start - tap + rows, :]
        total = term if total is None else total + term
    return total.astype(BF16)


def lag_masks(block):
    row = lax.broadcasted_iota(jnp.int32, (block, block), 0)
    col = lax.broadcasted_iota(jnp.int32, (block, block), 1)
    return row, col


def edge_kernel(
    x_ref, taps_hbm, filt_hbm, cot_hbm, near_ref, taps_ref, filt_ref, cot_ref, far_ref, bufs, sems
):
    _, rows, channels = x_ref.shape
    tail = far_ref.shape[1]
    block = tail - HALO
    copies = [
        pltpu.make_async_copy(
            x_ref.at[1 + part, pl.ds(rows - tail, tail), :], far_ref.at[part], sems.at[part]
        )
        for part in range(2)
    ]
    copies.append(
        pltpu.make_async_copy(
            x_ref.at[0, pl.ds(rows - HALO, HALO), :], near_ref.at[pl.ds(block, HALO), :], sems.at[2]
        )
    )
    copies.append(pltpu.make_async_copy(taps_hbm, taps_ref, sems.at[3]))
    others = [
        pltpu.make_async_copy(filt_hbm, filt_ref, sems.at[4]),
        pltpu.make_async_copy(cot_hbm, cot_ref, sems.at[5]),
    ]
    for copy in copies + others:
        copy.start()
    for copy in copies:
        copy.wait()
    inside = lax.axis_index("seq") < lax.axis_size("seq") - 1
    near_ref[block : block + HALO, :] = jnp.where(inside, near_ref[block : block + HALO, :], 0)

    def product(chunk, buf):
        lane = pl.ds(pl.multiple_of(chunk * LANES, LANES), LANES)
        for part in range(2):
            buf[1 + part] = far_ref[part, :, lane].astype(F32)
            at = block + (1 + part) * HALO
            near_ref[at : at + HALO, lane] = jnp.where(inside, far_ref[part, tail - HALO :, lane], 0)
        k = featurize(buf, 1, HALO, block, taps_ref.at[:, :, lane])
        v = featurize(buf, 2, HALO, block, taps_ref.at[:, :, lane])
        near_ref[:block, lane] = jnp.where(inside, k * v, 0)

    at_once = math.gcd(channels // LANES, bufs.shape[0])

    @pl.loop(0, channels // LANES // at_once)
    def _(turn):
        for number in range(at_once):
            product(turn * at_once + number, bufs.at[number])

    for copy in others:
        copy.wait()


def front_kernel(
    x_ref, taps_ref, filt_ref, skip_ref, cot_ref,
    far_ref, skt_ref, kv_ref, q0_ref, pt_ref, qt_ref, ct_ref, w_ref,
    bufs, mask,
):
    parts, rows, channels = x_ref.shape
    block = filt_ref.shape[1]
    members = channels // filt_ref.shape[0]
    groups = LANES // members
    blocks = rows // block
    tail = far_ref.shape[0] // 2
    bufs[:, :, :HALO, :] = jnp.zeros((bufs.shape[0], parts, HALO, LANES), F32)
    row, col = lag_masks(block)
    mask[...] = jnp.where(col >= row, 1.0, 0.0).astype(BF16)
    inside = lax.axis_index("seq") < lax.axis_size("seq") - 1

    def filters(chunk, within, filt):
        group = chunk * groups + within
        taps = jnp.broadcast_to(filt[within : within + 1], (block, block))
        circ = pltpu.roll(taps, 0, 1, stride=1, stride_axis=0).astype(BF16)
        near = circ * mask[...]
        w_ref[group, :block, :] = near
        w_ref[group, block:, :] = circ - near

    def features(chunk, buf, number):
        lane = pl.ds(pl.multiple_of(chunk * LANES, LANES), LANES)
        group_at = pl.ds(pl.multiple_of(chunk * groups, groups), groups)
        span = slice(number * block, (number + 1) * block)
        start = HALO + number * block
        for part in range(parts):
            buf[part, start : start + block, :] = x_ref[part, span, lane].astype(F32)
        q, k, v = (featurize(buf, part, start, block, taps_ref.at[:, :, lane]) for part in range(3))
        kv_ref[chunk, 0, span, :] = k
        kv_ref[chunk, 1, span, :] = v
        if number == 0:
            q0_ref[:, lane] = q
        else:
            place = slice((number - 1) * members, number * members)
            product = k * v
            pt_ref[group_at, place, :] = product.T.reshape(groups, members, block)
            qt_ref[group_at, place, :] = q.T.reshape(groups, members, block)
        place = slice(number * members, (number + 1) * members)
        ct_ref[group_at, place, :] = cot_ref[span, lane].T.reshape(groups, members, block)

    def everything(chunk, buf):
        lane = pl.ds(pl.multiple_of(chunk * LANES, LANES), LANES)
        group_at = pl.ds(pl.multiple_of(chunk * groups, groups), groups)
        filt = filt_ref[group_at, :].astype(F32)
        skt_ref[group_at] = skip_columns(skip_ref.at[:, lane], block).reshape(groups, members, block)
        braid(
            [functools.partial(features, chunk, buf, number) for number in range(blocks)],
            [functools.partial(filters, chunk, within, filt) for within in range(groups)],
        )
        for part in range(2):
            ends = jnp.where(inside, x_ref[1 + part, rows - tail :, lane], 0)
            far_ref[part * tail : (part + 1) * tail, lane] = ends

    at_once = math.gcd(channels // LANES, bufs.shape[0])

    @pl.loop(0, channels // LANES // at_once)
    def _(turn):
        for number in range(at_once):
            everything(turn * at_once + number, bufs.at[number])


def skip_columns(skip_ref, block):
    lanes = skip_ref.shape[1]
    return jnp.broadcast_to(skip_ref[...].astype(F32), (block, lanes)).T


def middle_kernel(
    near_ref, x_ref, taps_ref, skt_ref, kv_ref, q0_ref, pt_ref, qt_ref, ct_ref, w_ref,
    kve_ref, pta_ref, qta_ref, inner_ref, stats_ref,
    bufs, acc,
):
    channels = near_ref.shape[1]
    block = q0_ref.shape[0]
    members = channels // w_ref.shape[0]
    groups = LANES // members
    width = ct_ref.shape[1]
    blocks = width // members
    chunks = channels // LANES
    acc[...] = jnp.zeros_like(acc)

    def heads(chunk, buf):
        lane = pl.ds(pl.multiple_of(chunk * LANES, LANES), LANES)
        group_at = pl.ds(pl.multiple_of(chunk * groups, groups), groups)
        for part in range(3):
            at = block + part * HALO
            buf[part, :HALO, :] = near_ref[at : at + HALO, lane].astype(F32)
            buf[part, HALO:, :] = x_ref[part, :EDGE, lane].astype(F32)
        q_edge, k_edge, v_edge = (
            featurize(buf, part, HALO, EDGE, taps_ref.at[:, :, lane]) for part in range(3)
        )
        kve_ref[chunk, 0] = k_edge
        kve_ref[chunk, 1] = v_edge
        k0 = jnp.concatenate([k_edge, kv_ref[chunk, 0, EDGE:block, :]], axis=0)
        v0 = jnp.concatenate([v_edge, kv_ref[chunk, 1, EDGE:block, :]], axis=0)
        q0 = jnp.concatenate([q_edge, q0_ref[EDGE:, lane]], axis=0)
        p0 = k0 * v0
        pta_ref[group_at, :members, :] = near_ref[:block, lane].T.reshape(groups, members, block)
        pta_ref[group_at, members:, :] = p0.T.reshape(groups, members, block)
        qta_ref[group_at] = q0.T.reshape(groups, members, block)

    def filters(chunk):
        sums = [[None] * blocks, [None] * blocks]
        for within in range(groups):
            group = chunk * groups + within
            every = jnp.concatenate([pta_ref[group], pt_ref[group]], axis=0)
            now = every[members:]
            filtered = matmul(
                jnp.concatenate([now, every[:width]], axis=1), w_ref[group], ((1,), (0,))
            )
            own = jnp.concatenate([skt_ref[group]] * blocks, axis=0)
            inner = filtered + own * now.astype(F32)
            inner_ref[group] = inner
            q = jnp.concatenate([qta_ref[group], qt_ref[group]], axis=0).astype(F32)
            output = q * inner
            for which, value in enumerate((output * output, ct_ref[group].astype(F32) * output)):
                for number in range(blocks):
                    span = value[number * members : (number + 1) * members]
                    span = span.reshape(members // 8, 8, block).sum(axis=0)
                    sums[which][number] = span if within == 0 else sums[which][number] + span
        for which in range(2):
            for number in range(blocks):
                place = slice(number * 8, number * 8 + 8)
                acc[which, place, :] += sums[which][number]

    at_once = math.gcd(chunks, bufs.shape[0])
    for number in range(at_once):
        heads(number, bufs.at[number])

    @pl.loop(1, chunks // at_once)
    def _(turn):
        for number in range(at_once):
            filters((turn - 1) * at_once + number)
        for number in range(at_once):
            heads(turn * at_once + number, bufs.at[number])

    for number in range(at_once):
        filters(chunks - at_once + number)
    for which in range(2):
        for number in range(blocks):
            at = which * blocks + number
            stats_ref[at : at + 1, :] = jnp.sum(
                acc[which, number * 8 : number * 8 + 8, :], axis=0, keepdims=True
            )


def prep_kernel(near_ref, x_ref, kv_ref, kve_ref, xf_ref, kvf_ref, xq_ref, buf):
    parts, rows, channels = x_ref.shape
    block = near_ref.shape[0] - parts * HALO
    blocks = rows // block

    @pl.loop(0, channels // LANES)
    def _(chunk):
        lane = pl.ds(pl.multiple_of(chunk * LANES, LANES), LANES)
        buf[:HALO, :] = near_ref[block : block + HALO, lane].astype(F32)
        buf[HALO:, :] = x_ref[0, :, lane].astype(F32)
        for tap in range(xq_ref.shape[1]):
            xq_ref[chunk, tap] = buf[HALO - tap : HALO - tap + rows, :].astype(BF16)
        for part in range(1, parts):
            at = block + part * HALO
            xf_ref[chunk, 0, part - 1, :HALO, :] = near_ref[at : at + HALO, lane].astype(F32)
            for number in range(blocks):
                at = number * block
                if number:
                    xf_ref[chunk, number, part - 1, :HALO, :] = x_ref[part, at - HALO : at, lane].astype(F32)
                xf_ref[chunk, number, part - 1, HALO:, :] = x_ref[part, at : at + block, lane].astype(F32)
        for part in range(2):
            kvf_ref[chunk, 0, part, :EDGE, :] = kve_ref[chunk, part].astype(F32)
            kvf_ref[chunk, 0, part, EDGE:, :] = kv_ref[chunk, part, EDGE:block, :].astype(F32)
            for number in range(1, blocks):
                at = number * block
                kvf_ref[chunk, number, part] = kv_ref[chunk, part, at : at + block, :].astype(F32)


def braid(one, two):
    done = 0
    for number, step in enumerate(one):
        step()
        upto = (number + 1) * len(two) // len(one)
        for other in two[done:upto]:
            other()
        done = upto
    for other in two[done:]:
        other()


def rim_kernel(far_ref, taps_ref, pgr_ref, out_ref, sum_ref, buf):
    members, block = pgr_ref.shape[1:]
    groups = LANES // members
    chunks = pgr_ref.shape[0] // groups
    taps = taps_ref.shape[1]
    tail = block + HALO
    sum_ref[:8, :] = out_ref[:8, :]
    sum_ref[24:, :] = out_ref[24:, :]

    @pl.loop(0, chunks)
    def _(chunk):
        lane = pl.ds(pl.multiple_of(chunk * LANES, LANES), LANES)
        for part in range(2):
            buf[1 + part] = far_ref[part * tail : (part + 1) * tail, lane].astype(F32)
        group_at = pl.ds(pl.multiple_of(chunk * groups, groups), groups)
        back = pgr_ref[group_at].reshape(LANES, block).T
        for part in (1, 2):
            other = featurize(buf, 3 - part, HALO, block, taps_ref.at[:, :, lane]).astype(F32)
            grads = back * other
            for tap in range(taps):
                at = part * 8 + tap
                term = grads * buf[part, HALO - tap : HALO - tap + block, :]
                sum_ref[at : at + 1, lane] = out_ref[at : at + 1, lane] + jnp.sum(term, axis=0, keepdims=True)
            sum_ref[part * 8 + taps : part * 8 + 8, lane] = out_ref[part * 8 + taps : part * 8 + 8, lane]


def back_kernel(channels_all, token_scale, taps, n_stats, *refs):
    stats_refs = refs[:n_stats]
    (skt_ref, xf_ref, kvf_ref, xq_ref, pt_ref, pta_ref, qt_ref, qta_ref, ct_ref, inner_ref, w_ref,
     out_ref, pgr_ref, coef, skip_acc, filt_acc, sums, eye, *slots) = refs[n_stats:]
    chunks, blocks = xf_ref.shape[:2]
    parts = 1 + xf_ref.shape[2]
    width, block = ct_ref.shape[1:]
    members = width // blocks
    groups = LANES // members
    total = merged([ref[...] for ref in stats_refs])
    square = total[:blocks]
    cross = total[blocks : 2 * blocks] / channels_all
    rms = jnp.sqrt(square / channels_all + 1e-05)
    inv = token_scale / rms
    fall = token_scale * cross / (rms * rms * rms)
    for number in range(blocks):
        place = slice(number * members, (number + 1) * members)
        coef[0, place, :] = jnp.broadcast_to(inv[number : number + 1], (members, block))
        coef[1, place, :] = jnp.broadcast_to(fall[number : number + 1], (members, block))
    row, col = lag_masks(block)
    slots = (slots[:3], slots[3:])
    eye[...] = jnp.where(row == col, 1.0, 0.0)

    def group_part(chunk, slot, within):
        pg, qg, _ = slots[slot]
        group = chunk * groups + within
        every = jnp.concatenate([pta_ref[group], pt_ref[group]], axis=0)
        now = every[members:]
        q = jnp.concatenate([qta_ref[group], qt_ref[group]], axis=0).astype(F32)
        inner = inner_ref[group]
        output = q * inner
        out_grad = coef[0] * ct_ref[group].astype(F32) - coef[1] * output
        conv_grad = out_grad * q
        cot = conv_grad.astype(BF16)
        query_grad = out_grad * inner
        weighted = conv_grad * now.astype(F32)
        part_sum = weighted[:members]
        for number in range(1, blocks):
            part_sum = part_sum + weighted[number * members : (number + 1) * members]
        skip_acc[group] = part_sum
        gap = jnp.zeros((members, block), BF16)
        here = jnp.concatenate([gap, cot], axis=0)
        later = jnp.concatenate([cot, gap], axis=0)
        grad = matmul(
            jnp.concatenate([here, later], axis=1),
            jnp.concatenate([w_ref[group, :block, :], w_ref[group, block:, :]], axis=1),
            ((1,), (1,)),
        )
        own = skt_ref[group]
        pgr_ref[group] = grad[:members]
        for number in range(blocks):
            span = slice(number * members, (number + 1) * members)
            pg[number, within] = (
                grad[(number + 1) * members : (number + 2) * members] + own * conv_grad[span]
            )
            qg[number, within] = query_grad[span].astype(BF16)
        both = matmul(cot, jnp.concatenate([now, every[:width]], axis=1), ((0,), (0,)))
        lagged = jnp.where(col <= row, both[:, :block], both[:, block:])
        skewed = lagged[:8]
        for start in range(8, block, 8):
            skewed = skewed + pltpu.roll(lagged[start : start + 8], block - start, 1)
        filt_acc[group] = skewed

    def turn(slot):
        pg, _, gn = slots[slot]
        for number in range(blocks):
            gn[number] = pg[number].reshape(LANES, block).T

    def query_steps(chunk, slot):
        qg = slots[slot][1]

        def step(first):
            grads = jnp.concatenate([qg[number].reshape(LANES, block) for number in range(blocks)], axis=1)
            some = range(first, min(first + 2, taps))
            every = matmul(
                grads, jnp.concatenate([xq_ref[chunk, tap] for tap in some], axis=1), ((1,), (0,))
            )
            for place, tap in enumerate(some):
                own = every[:, place * LANES : (place + 1) * LANES] * eye[...]
                sums[chunk, tap] = own.reshape(LANES // 8, 8, LANES).sum(axis=0)

        return [functools.partial(step, first) for first in range(0, taps, 2)]

    def tap_steps(chunk, slot):
        gn = slots[slot][2]
        piece = 32
        totals = {}

        def step(part, number):
            for at in range(0, block, piece):
                grads = gn[number, at : at + piece, :]
                grads = grads * kvf_ref[chunk, number, 2 - part, at : at + piece, :]
                for tap in range(taps):
                    start = HALO + at - tap
                    term = grads * xf_ref[chunk, number, part - 1, start : start + piece, :]
                    term = term.reshape(piece // 8, 8, LANES).sum(axis=0)
                    totals[part, tap] = totals[part, tap] + term if (part, tap) in totals else term
            if number == blocks - 1:
                for tap in range(taps):
                    sums[chunk, part * taps + tap] = totals[part, tap]

        return [functools.partial(step, part, number) for part in range(1, parts) for number in range(blocks)]

    def group_steps(chunk, slot):
        return [functools.partial(group_part, chunk, slot, within) for within in range(groups)]

    def whole_step(chunk, slot):
        turn(1 - slot)
        braid(group_steps(chunk, slot), tap_steps(chunk - 2, slot) + query_steps(chunk - 1, 1 - slot))

    braid(group_steps(0, 0), [])
    if chunks > 1:
        braid(group_steps(1, 1), query_steps(0, 0))
        turn(0)

        pairs = chunks // 2 - 1
        at_once = 3 if pairs % 3 == 0 else 1

        @pl.loop(0, pairs // at_once)
        def _(turn):
            for number in range(at_once):
                pair = 1 + turn * at_once + number
                whole_step(2 * pair, 0)
                whole_step(2 * pair + 1, 1)

        if chunks % 2:
            whole_step(chunks - 1, 0)
        turn((chunks - 1) % 2)
        braid([], tap_steps(chunks - 2, chunks % 2))
    else:
        turn(0)
    last = (chunks - 1) % 2
    braid(query_steps(chunks - 1, last), tap_steps(chunks - 1, last))

    flip = jnp.where(((row + col) % block) == 0, 1.0, 0.0).astype(F32)
    lags = filt_acc[:, 0, :]
    for at in range(1, 8):
        lags = lags + pltpu.roll(filt_acc[:, at, :], block - at, 1)
    lags = lax.dot_general(
        lags, flip, (((1,), (0,)), ((), ())), preferred_element_type=F32, precision=lax.Precision.HIGHEST
    )
    for chunk in range(chunks):
        lane = slice(chunk * LANES, (chunk + 1) * LANES)
        group_at = slice(chunk * groups, (chunk + 1) * groups)
        out_ref[3 * 8 :, lane] = lags[group_at]
        skip_row = jnp.sum(skip_acc[group_at].reshape(LANES, block).T, axis=0, keepdims=True)
        for part in range(parts):
            for tap in range(taps):
                out_ref[part * 8 + tap : part * 8 + tap + 1, lane] = jnp.sum(
                    sums[chunk, part * taps + tap], axis=0, keepdims=True
                )
            out_ref[part * 8 + taps : part * 8 + 8, lane] = skip_row


def finish_kernel(n_in, *refs):
    ins = refs[:n_in]
    feat_ref, filt_ref, skip_ref = refs[n_in:]
    total = merged([ref[...].astype(F32) for ref in ins])
    taps = feat_ref.shape[1]
    for part in range(feat_ref.shape[0]):
        feat_ref[part] = total[part * 8 : part * 8 + taps]
    skip_ref[...] = total[taps : taps + 1]
    groups = total.shape[0] - 24
    for chunk in range(total.shape[1] // LANES):
        filt_ref[chunk * groups : (chunk + 1) * groups, :] = total[24:, chunk * LANES : (chunk + 1) * LANES]


def ring(array, axis):
    length = lax.axis_size(axis)
    return lax.ppermute(array, axis, [(i, (i + 1) % length) for i in range(length)])


def crossed(array, axis, bit):
    length = lax.axis_size(axis)
    return lax.ppermute(array, axis, [(i, i ^ bit) for i in range(length)])


def quartet(array, axis, bit):
    return [array] + [crossed(array, axis, bit * k) for k in (1, 2, 3)]


def merged(parts):
    if len(parts) == 1:
        return parts[0]
    return (parts[0] + parts[1]) + (parts[2] + parts[3])


def on_chip(kernel, out_shape, scratch, args, outside=(), final=False):
    place = pl.BlockSpec(memory_space=pltpu.VMEM)
    apart = pl.BlockSpec(memory_space=pl.ANY)
    if not final:
        out_shape = [pltpu.VMEM(out.shape, out.dtype) for out in out_shape]
    args = [
        pltpu.with_memory_space_constraint(arg, pltpu.HBM if number in outside else pltpu.VMEM)
        for number, arg in enumerate(args)
    ]
    return pl.pallas_call(
        kernel,
        in_specs=[apart if number in outside else place for number in range(len(args))],
        out_specs=[place] * len(out_shape),
        out_shape=out_shape,
        scratch_shapes=scratch,
        compiler_params=pltpu.CompilerParams(vmem_limit_bytes=16 * 1024 * 1024),
    )(*args)


def body(projected, featurizer, long_filter, skip_gain, out_cotangent):
    parts, rows, channels = projected.shape
    groups, block = long_filter.shape
    taps = featurizer.shape[0]
    members = channels // groups
    chunk_groups = LANES // members
    blocks = rows // block
    width = blocks * members
    tail = block + HALO
    taps_major = jnp.transpose(featurizer, (1, 0, 2))
    skip_row = skip_gain.reshape(1, channels)

    sds = jax.ShapeDtypeStruct
    chunks = channels // LANES

    near, taps_major, filters, cots = on_chip(
        edge_kernel,
        [
            sds((block + parts * HALO, channels), BF16),
            sds((parts, taps, channels), BF16),
            sds((groups, block), BF16),
            sds((rows, channels), BF16),
        ],
        [
            pltpu.VMEM((2, tail, channels), BF16),
            pltpu.VMEM((4, parts, tail, LANES), F32),
            pltpu.SemaphoreType.DMA((6,)),
        ],
        (projected, taps_major, long_filter, out_cotangent),
        outside=(0, 1, 2, 3),
    )
    near = ring(near, "seq")

    far, skt, kv, q0, pt, qt, ct, w = on_chip(
        front_kernel,
        [
            sds((2 * tail, channels), BF16),
            sds((groups, members, block), F32),
            sds((chunks, 2, rows, LANES), BF16),
            sds((block, channels), BF16),
            sds((groups, width - members, block), BF16),
            sds((groups, width - members, block), BF16),
            sds((groups, width, block), BF16),
            sds((groups, 2 * block, block), BF16),
        ],
        [
            pltpu.VMEM((2, parts, HALO + rows, LANES), F32),
            pltpu.VMEM((block, block), BF16),
        ],
        (projected, taps_major, filters, skip_row, cots),
    )
    far = ring(far, "seq")
    kve, pta, qta, inner, stats = on_chip(
        middle_kernel,
        [
            sds((chunks, 2, EDGE, LANES), BF16),
            sds((groups, 2 * members, block), BF16),
            sds((groups, members, block), BF16),
            sds((groups, width, block), F32),
            sds((2 * blocks, block), F32),
        ],
        [
            pltpu.VMEM((4, parts, HALO + EDGE, LANES), F32),
            pltpu.VMEM((2, 8 * blocks, block), F32),
        ],
        (near, projected, taps_major, skt, kv, q0, pt, qt, ct, w),
    )

    dp_size = lax.axis_size("dp")
    stat_parts = [stats]
    bit = 1
    while bit < dp_size:
        current = merged(stat_parts)
        if bit * 4 <= dp_size:
            stat_parts = quartet(current, "dp", bit)
            bit *= 4
        else:
            stat_parts = [current + crossed(current, "dp", bit)]
            bit *= 2
    xf, kvf, xq = on_chip(
        prep_kernel,
        [
            sds((chunks, blocks, 2, HALO + block, LANES), F32),
            sds((chunks, blocks, 2, block, LANES), F32),
            sds((chunks, taps, rows, LANES), BF16),
        ],
        [pltpu.VMEM((HALO + rows, LANES), F32)],
        (near, projected, kv, kve),
    )
    token_scale = 1.0 / math.sqrt(rows * lax.axis_size("seq"))
    out, pgr = on_chip(
        functools.partial(back_kernel, channels * dp_size, token_scale, taps, len(stat_parts)),
        [sds((24 + chunk_groups, channels), F32), sds((groups, members, block), F32)],
        [
            pltpu.VMEM((2, width, block), F32),
            pltpu.VMEM((groups, members, block), F32),
            pltpu.VMEM((groups, 8, block), F32),
            pltpu.VMEM((chunks, parts * taps, 8, LANES), F32),
            pltpu.VMEM((LANES, LANES), F32),
        ]
        + [
            pltpu.VMEM((blocks, chunk_groups, members, block), F32),
            pltpu.VMEM((blocks, chunk_groups, members, block), BF16),
            pltpu.VMEM((blocks, block, LANES), F32),
        ]
        * 2,
        (*stat_parts, skt, xf, kvf, xq, pt, pta, qt, qta, ct, inner, w),
    )
    (out,) = on_chip(
        rim_kernel,
        [sds((24 + chunk_groups, channels), F32)],
        [pltpu.VMEM((parts, tail, LANES), F32)],
        (far, taps_major, pgr, out),
    )

    seq_size = lax.axis_size("seq")
    out_parts = [out + crossed(out, "seq", 1)]
    bit = 2
    while bit < seq_size:
        current = merged([part.astype(F32) for part in out_parts]).astype(BF16)
        if bit * 4 <= seq_size:
            out_parts = quartet(current, "seq", bit)
            bit *= 4
        else:
            out_parts = [current.astype(F32) + crossed(current, "seq", bit).astype(F32)]
            bit *= 2

    feat, filt, skip = on_chip(
        functools.partial(finish_kernel, len(out_parts)),
        [
            sds((parts, taps, channels), F32),
            sds((groups, block), F32),
            sds((1, channels), F32),
        ],
        [],
        out_parts,
        final=True,
    )
    return (jnp.transpose(feat, (1, 0, 2)), filt, skip.reshape(channels))


def solution(mesh):
    return jax.shard_map(
        body,
        mesh=mesh,
        in_specs=(
            P(None, "seq", "dp"),
            P(None, None, "dp"),
            P("dp", None),
            P("dp"),
            P("seq", "dp"),
        ),
        out_specs=(P(None, None, "dp"), P("dp", None), P("dp")),
        check_vma=False,
    )
```
